512 devices in a mesh: gx: 32 (over z, core), gy: 16 (over x, y).
Axes of the slice: x: 4, y: 4, z: 16, core: 2. Of those that a mesh axis runs over, the one named last changes fastest.
Arguments:
- density: float32 [512, 128, 128], P('gx', 'gy'), may hold values from 0.05 to 0.95
- displacement: float32 [3, 512, 128, 128], P(None, 'gx', 'gy'), may hold values from -2 to 2
- passive: int32 [512, 128, 128], P('gx', 'gy'), may hold values from 0 to 2
Outputs:
- new_density: float32 [512, 128, 128], P('gx', 'gy')
- sensitivity: float32 [512, 128, 128], P('gx', 'gy')
The draws below stay inside these ranges and needn't reach their ends.
All inputs are finite; a program needn't handle non-finite values.
Results may differ from the reference program's by a relative error of at most 0.0003.
Values sent between devices are 32-bit elements; how exact they have to be, the bound alone decides.
No kernel may reach another device: no remote copies, remote signals or barrier semaphores. Data moves between devices by JAX's collectives and lax.ppermute only.
A program may use at most 64 MiB of HBM per device.

```python
import math
import jax
import jax.numpy as jnp
import numpy as np
from jax import lax

CZ = 128
BISECT = 8
NX = 512
NY = 128


def draw_density(key, part):
    across = jnp.arange(NX, dtype=jnp.float32) / max(NX - 1, 1)
    along = jnp.arange(NY, dtype=jnp.float32) / max(NY - 1, 1)
    profile = (0.3 + 0.7 * across)[:, None, None] * (0.3 + 0.7 * along)[None, :, None]
    jitter = jax.random.uniform(key, (NX, NY, CZ), jnp.float32, 0.6, 1.0)
    return 0.05 + 0.9 * profile * jitter


def draw_passive(key, part):
    rolled = jax.random.randint(key, (NX, NY, CZ), 0, 16)
    return jnp.where(rolled == 0, 1, jnp.where(rolled == 1, 2, 0)).astype(jnp.int32)


def steps_of(stream_key, dims, cuts, smallest, high):
    gain = 1.0
    for axis_at, blocks in cuts:
        steps = jax.random.uniform(jax.random.fold_in(jax.random.fold_in(stream_key, 6), axis_at), (blocks,), jnp.float32, smallest / len(cuts), high / len(cuts))
        gain = gain * jnp.repeat(jnp.exp(steps), dims[axis_at] // blocks).reshape((-1,) + (1,) * (len(dims) - 1 - axis_at))
    return gain


def normal_values(rng, dims, scale, reach, shards=(), kind=jnp.bfloat16):
    entries = scale * jax.random.normal(rng, dims, jnp.float32)
    if shards:
        entries = entries * steps_of(rng, dims, shards, -0.22, 0.18)
    return jnp.clip(entries, -reach, reach).astype(kind)


def setup_inputs(seed: int = 0) -> dict:
    streams_of = jax.random.split(jax.random.key(seed), 4)
    return {
        "density": draw_density(jax.random.fold_in(streams_of[3], 71), 0),
        "displacement": normal_values(streams_of[1], (3, NX, NY, CZ), 0.3, 2.0, ((1, 32), (2, 16)), jnp.float32),
        "passive": draw_passive(jax.random.fold_in(streams_of[3], 71), 0),
    }


BRACKET = 8.0
MOVE_LIMIT = 0.2
VOLUME_SHARE = 0.35
DERIVATIVE = 3.0 * (1.0 - 1e-09)
EDGE_WEIGHT = 1.5 - math.sqrt(2.0)

def element_stiffness():
    poisson = 0.3
    lame_first = poisson / ((1.0 + poisson) * (1.0 - 2.0 * poisson))
    shear_modulus = 0.5 / (1.0 + poisson)
    elastic = np.zeros((6, 6))
    elastic[:3, :3] = lame_first
    for entry in range(3):
        elastic[entry, entry] = lame_first + 2.0 * shear_modulus
        elastic[entry + 3, entry + 3] = shear_modulus
    points = [0.5 - 0.5 / math.sqrt(3.0), 0.5 + 0.5 / math.sqrt(3.0)]
    stiffness = np.zeros((24, 24))
    for point_x in points:
        for point_y in points:
            for point_z in points:
                strain = np.zeros((6, 24))
                for a in (0, 1):
                    for b in (0, 1):
                        for c in (0, 1):
                            corner = 4 * a + 2 * b + c
                            value_x = point_x if a else 1.0 - point_x
                            value_y = point_y if b else 1.0 - point_y
                            value_z = point_z if c else 1.0 - point_z
                            slope_x = (1.0 if a else -1.0) * value_y * value_z
                            slope_y = value_x * (1.0 if b else -1.0) * value_z
                            slope_z = value_x * value_y * (1.0 if c else -1.0)
                            strain[0, 3 * corner] = slope_x
                            strain[1, 3 * corner + 1] = slope_y
                            strain[2, 3 * corner + 2] = slope_z
                            strain[3, 3 * corner] = slope_y
                            strain[3, 3 * corner + 1] = slope_x
                            strain[4, 3 * corner + 1] = slope_z
                            strain[4, 3 * corner + 2] = slope_y
                            strain[5, 3 * corner] = slope_z
                            strain[5, 3 * corner + 2] = slope_x
                stiffness = stiffness + 0.125 * strain.T @ elastic @ strain
    return stiffness.astype(np.float32)

def weight_sums(index_x, index_y, index_z, count_x, count_y, count_z):
    along_x = (index_x > 0).astype(jnp.float32) + (index_x < count_x - 1).astype(jnp.float32)
    along_y = (index_y > 0).astype(jnp.float32) + (index_y < count_y - 1).astype(jnp.float32)
    along_z = (index_z > 0).astype(jnp.float32) + (index_z < count_z - 1).astype(jnp.float32)
    return 1.5 + 0.5 * (along_x + along_y + along_z) + EDGE_WEIGHT * (along_x * along_y + along_x * along_z + along_y * along_z)

def apply_filter(field):
    extent_x, extent_y, extent_z = field.shape
    padded = jnp.pad(field, 1)
    summed = jnp.zeros_like(field)
    for shift_x in (-1, 0, 1):
        for shift_y in (-1, 0, 1):
            for shift_z in (-1, 0, 1):
                squared = shift_x * shift_x + shift_y * shift_y + shift_z * shift_z
                if squared <= 2:
                    factor = 1.5 - math.sqrt(squared)
                    summed = summed + factor * padded[1 + shift_x:1 + shift_x + extent_x, 1 + shift_y:1 + shift_y + extent_y, 1 + shift_z:1 + shift_z + extent_z]
    return summed

def element_energy(displacement):
    stiffness = jnp.asarray(element_stiffness())
    extent_x, extent_y, extent_z = displacement.shape[1:]
    node_field = jnp.pad(displacement, ((0, 0), (0, 1), (0, 1), (0, 1)))

    def slab_energy(first):
        section = lax.dynamic_slice_in_dim(node_field, first, 9, 1)
        corners = [section[:, a:a + 8, b:b + extent_y, c:c + extent_z] for a in (0, 1) for b in (0, 1) for c in (0, 1)]
        stacked = jnp.stack(corners, 0).reshape(24, 8 * extent_y * extent_z)
        mapped = jnp.dot(stiffness, stacked, precision=lax.Precision.HIGHEST)
        return lax.optimization_barrier(jnp.sum(stacked * mapped, axis=0)).reshape(8, extent_y, extent_z)
    starts = jnp.arange(extent_x // 8, dtype=jnp.int32) * 8
    return lax.map(slab_energy, starts).reshape(extent_x, extent_y, extent_z)

def reference(density, displacement, passive):
    extent_x, extent_y, extent_z = density.shape
    index_x = jnp.arange(extent_x, dtype=jnp.int32)[:, None, None]
    index_y = jnp.arange(extent_y, dtype=jnp.int32)[None, :, None]
    index_z = jnp.arange(extent_z, dtype=jnp.int32)[None, None, :]
    sums = weight_sums(index_x, index_y, index_z, extent_x, extent_y, extent_z)
    physical = apply_filter(density) / sums
    physical = jnp.where(passive == 1, 1.0, jnp.where(passive == 2, 0.0, physical))
    energy = element_energy(displacement)
    raw_field = -DERIVATIVE * physical * physical * energy
    sensitivity = apply_filter(raw_field / sums)
    volume_weight = apply_filter(1.0 / sums)
    scaled = density * jnp.sqrt(-sensitivity / volume_weight)
    lower = jnp.where(passive == 0, jnp.maximum(density - MOVE_LIMIT, 0.0), jnp.where(passive == 1, 1.0, 0.0))
    upper = jnp.where(passive == 0, jnp.minimum(density + MOVE_LIMIT, 1.0), jnp.where(passive == 1, 1.0, 0.0))
    target = VOLUME_SHARE * extent_x * extent_y * extent_z
    lower_end = jnp.asarray(-BRACKET, jnp.float32)
    upper_end = jnp.asarray(BRACKET, jnp.float32)
    for bisection_step in range(BISECT):
        middle = 0.5 * (lower_end + upper_end)
        volume = jnp.sum(jnp.minimum(jnp.maximum(scaled * jnp.exp(-0.5 * middle), lower), upper))
        exceeds = volume > target
        lower_end = jnp.where(exceeds, middle, lower_end)
        upper_end = jnp.where(exceeds, upper_end, middle)
    middle = 0.5 * (lower_end + upper_end)
    new_density = jnp.minimum(jnp.maximum(scaled * jnp.exp(-0.5 * middle), lower), upper)
    return (new_density, sensitivity)
```

```python
import functools
import math

import jax
import jax.numpy as jnp
import numpy as np
from jax import lax
from jax.experimental import pallas as pl
from jax.experimental.pallas import tpu as pltpu
from jax.sharding import PartitionSpec as P

BISECT = 8
BRACKET = 8.0
MOVE_LIMIT = 0.2
VOLUME_SHARE = 0.35
DERIVATIVE = 3.0 * (1.0 - 1e-09)
EDGE_WEIGHT = 1.5 - math.sqrt(2.0)
POISSON = 0.3
LAME = POISSON / ((1.0 + POISSON) * (1.0 - 2.0 * POISSON))
SHEAR = 0.5 / (1.0 + POISSON)

NXL = 16
NYL = 8
NZ = 128
TRIALS = 2 ** BISECT - 1
SLOTS = TRIALS + 1
STEP = 2.0 * BRACKET / 2 ** BISECT

VMEM = pl.BlockSpec(memory_space=pltpu.VMEM)
SMEM = pl.BlockSpec(memory_space=pltpu.SMEM)


def trial_factors():
    middles = -BRACKET + STEP * np.arange(1, SLOTS + 1, dtype=np.float64)
    return np.exp(-0.5 * middles).astype(np.float32)


def pack_y(density, displacement, passive, to_low, to_high):
    for row in (0, 1):
        to_low[pl.ds(row * NXL, NXL), :] = density[:, row, :]
        to_high[pl.ds(row * NXL, NXL), :] = density[:, NYL - 2 + row, :]
    for c in range(3):
        for row in (0, 1):
            to_low[pl.ds((2 + 2 * c + row) * NXL, NXL), :] = displacement[c, :, row, :]
        to_high[pl.ds((2 + c) * NXL, NXL), :] = displacement[c, :, NYL - 1, :]
    to_low[pl.ds(8 * NXL, NXL), :] = passive[:, 0, :].astype(jnp.float32)
    to_high[pl.ds(5 * NXL, NXL), :] = passive[:, NYL - 1, :].astype(jnp.float32)


def pack_x(density, displacement, passive, y_high, y_low, to_low, to_high):
    for k in (0, 1):
        to_low[pl.ds(8 * k, 8), :] = density[k]
        to_high[pl.ds(8 * k, 8), :] = density[NXL - 2 + k]
    for c in range(3):
        for k in (0, 1):
            to_low[pl.ds(8 * (2 + 2 * c + k), 8), :] = displacement[c, k]
        to_high[pl.ds(8 * (2 + c), 8), :] = displacement[c, NXL - 1]
    to_low[pl.ds(64, 8), :] = passive[0].astype(jnp.float32)
    to_high[pl.ds(40, 8), :] = passive[NXL - 1].astype(jnp.float32)
    for base, first, out in ((72, 0, to_low), (48, NXL - 2, to_high)):
        for kind in range(9):
            out[pl.ds(base + 2 * kind, 2), :] = y_high[pl.ds(NXL * kind + first, 2), :]
        for kind in range(6):
            out[pl.ds(base + 18 + 2 * kind, 2), :] = y_low[pl.ds(NXL * kind + first, 2), :]
        out[pl.ds(base + 30, 2), :] = jnp.zeros((2, NZ), jnp.float32)


def z_sum(f, first, last):
    return jnp.where(first, 0.0, pltpu.roll(f, 1, 1)) + jnp.where(
        last, 0.0, pltpu.roll(f, NZ - 1, 1)
    )


def filter_terms(low, mid, high, first, last):
    across = z_sum(mid, first, last)
    along = low + high
    both = across + along
    side = 0.5 * mid + EDGE_WEIGHT * both
    rest = 1.5 * mid + 0.5 * both + EDGE_WEIGHT * z_sum(along, first, last)
    return side, rest


def corner_sums(here, above, last):
    total = here + above
    slope = above - here
    total_next = jnp.where(last, 0.0, pltpu.roll(total, NZ - 1, 1))
    slope_next = jnp.where(last, 0.0, pltpu.roll(slope, NZ - 1, 1))
    return (total + total_next, total_next - total, slope + slope_next, slope_next - slope)


def element_energy(before, after):
    modes = []
    for c in range(3):
        for k in range(4):
            low, high = before[4 * c + k], after[4 * c + k]
            modes.append((low + high, high - low))
    u, v, w = (
        {(a, k // 2, k % 2): modes[4 * c + k][a] for a in (0, 1) for k in range(4)}
        for c in range(3)
    )

    def sq(x):
        return x * x

    trace = sq(u[1, 0, 0] + v[0, 1, 0] + w[0, 0, 1]) + (1.0 / 3.0) * (
        sq(v[1, 1, 0] + w[1, 0, 1]) + sq(u[1, 1, 0] + w[0, 1, 1]) + sq(u[1, 0, 1] + v[0, 1, 1])
    )
    normal = sq(u[1, 0, 0]) + sq(v[0, 1, 0]) + sq(w[0, 0, 1])
    linear = (
        sq(v[1, 1, 0])
        + sq(w[1, 0, 1])
        + sq(u[1, 1, 0])
        + sq(w[0, 1, 1])
        + sq(u[1, 0, 1])
        + sq(v[0, 1, 1])
    )
    bilinear = sq(u[1, 1, 1]) + sq(v[1, 1, 1]) + sq(w[1, 1, 1])
    shear = (
        sq(u[0, 1, 0] + v[1, 0, 0]) + sq(u[0, 0, 1] + w[1, 0, 0]) + sq(v[0, 0, 1] + w[0, 1, 0])
    )
    twist = (
        sq(u[0, 1, 1] + v[1, 0, 1]) + sq(u[0, 1, 1] + w[1, 1, 0]) + sq(v[1, 0, 1] + w[1, 1, 0])
    )
    return (
        (LAME / 16.0) * trace
        + (SHEAR / 8.0) * normal
        + (SHEAR / 16.0) * (linear + shear)
        + ((LAME + 4.0 * SHEAR) / 144.0) * bilinear
        + (SHEAR / 48.0) * twist
    )


def update(
    factors,
    density,
    displacement,
    passive,
    y_high,
    y_low,
    x_high,
    x_low,
    sensitivity,
    scaled,
    sums_out,
    dens,
    disp,
    kind_of,
    spread,
    inverse,
    lower,
    upper,
    partial,
    *,
    copies,
):
    last_x = lax.axis_index("gx") == lax.axis_size("gx") - 1
    first_x = lax.axis_index("gx") == 0
    start_y = lax.axis_index("gy") * NYL
    total_y = lax.axis_size("gy") * NYL

    dens[pl.ds(2, NXL), pl.ds(2, NYL), :] = density[...]
    disp[:, pl.ds(1, NXL), pl.ds(1, NYL), :] = displacement[...]
    kind_of[pl.ds(1, NXL), pl.ds(1, NYL), :] = passive[...].astype(jnp.float32)
    for k in (0, 1):
        dens[pl.ds(2, NXL), NYL + 2 + k, :] = y_high[pl.ds(k * NXL, NXL), :]
        dens[pl.ds(2, NXL), k, :] = y_low[pl.ds(k * NXL, NXL), :]
        dens[NXL + 2 + k, pl.ds(2, NYL), :] = x_high[pl.ds(8 * k, 8), :]
        dens[k, pl.ds(2, NYL), :] = x_low[pl.ds(8 * k, 8), :]
        for row in (0, 1):
            dens[NXL + 2 + k, pl.ds(NYL + 2 + row, 1), :] = x_high[pl.ds(72 + 2 * row + k, 1), :]
            dens[NXL + 2 + k, pl.ds(row, 1), :] = x_high[pl.ds(90 + 2 * row + k, 1), :]
            dens[k, pl.ds(NYL + 2 + row, 1), :] = x_low[pl.ds(48 + 2 * row + k, 1), :]
            dens[k, pl.ds(row, 1), :] = x_low[pl.ds(66 + 2 * row + k, 1), :]
    for c in range(3):
        for k in (0, 1):
            at = 2 + 2 * c + k
            disp[c, pl.ds(1, NXL), NYL + 1 + k, :] = y_high[pl.ds(at * NXL, NXL), :]
            disp[c, NXL + 1 + k, pl.ds(1, NYL), :] = x_high[pl.ds(8 * at, 8), :]
            for row in (0, 1):
                disp[c, NXL + 1 + k, pl.ds(NYL + 1 + row, 1), :] = x_high[
                    pl.ds(72 + 2 * (2 + 2 * c + row) + k, 1), :
                ]
            disp[c, NXL + 1 + k, pl.ds(0, 1), :] = x_high[pl.ds(90 + 2 * (2 + c) + k, 1), :]
            disp[c, 0, pl.ds(NYL + 1 + k, 1), :] = x_low[pl.ds(48 + 2 * at + 1, 1), :]
        disp[c, pl.ds(1, NXL), 0, :] = y_low[pl.ds((2 + c) * NXL, NXL), :]
        disp[c, 0, pl.ds(1, NYL), :] = x_low[pl.ds(8 * (2 + c), 8), :]
        disp[c, 0, pl.ds(0, 1), :] = x_low[pl.ds(66 + 2 * (2 + c) + 1, 1), :]
    kind_of[pl.ds(1, NXL), NYL + 1, :] = y_high[pl.ds(8 * NXL, NXL), :]
    kind_of[pl.ds(1, NXL), 0, :] = y_low[pl.ds(5 * NXL, NXL), :]
    kind_of[NXL + 1, pl.ds(1, NYL), :] = x_high[pl.ds(64, 8), :]
    kind_of[0, pl.ds(1, NYL), :] = x_low[pl.ds(40, 8), :]
    kind_of[NXL + 1, pl.ds(NYL + 1, 1), :] = x_high[pl.ds(72 + 16, 1), :]
    kind_of[NXL + 1, pl.ds(0, 1), :] = x_high[pl.ds(90 + 10, 1), :]
    kind_of[0, pl.ds(NYL + 1, 1), :] = x_low[pl.ds(48 + 17, 1), :]
    kind_of[0, pl.ds(0, 1), :] = x_low[pl.ds(66 + 11, 1), :]

    lane = lax.broadcasted_iota(jnp.int32, (8, NZ), 1)
    first = lane == 0
    last = lane == NZ - 1
    along_z = jnp.where(first | last, 1.0, 2.0)

    for v in (0, 1):
        index_y = start_y - 1 + 8 * v + lax.broadcasted_iota(jnp.int32, (8, NZ), 0)
        inside = (index_y >= 0) & (index_y < total_y)
        along_y = jnp.where((index_y == 0) | (index_y == total_y - 1), 1.0, 2.0)
        base = 1.5 + 0.5 * (along_y + along_z) + EDGE_WEIGHT * along_y * along_z
        slope = 0.5 + EDGE_WEIGHT * (along_y + along_z)
        for slot, along_x in ((0, 2.0), (1, 1.0)):
            inverse[slot, pl.ds(8 * v, 8), :] = jnp.where(
                inside, 1.0 / (base + along_x * slope), 0.0
            )

    for v in (0, 1):
        rows = pl.ds(8 * v, 8)

        def density_terms(plane):
            return filter_terms(
                dens[plane, rows, :],
                dens[plane, pl.ds(8 * v + 1, 8), :],
                dens[plane, pl.ds(8 * v + 2, 8), :],
                first,
                last,
            )

        def node_plane(plane):
            return sum(
                (
                    corner_sums(
                        disp[c, plane, rows, :], disp[c, plane, pl.ds(8 * v + 1, 8), :], last
                    )
                    for c in range(3)
                ),
                (),
            )

        def rim_plane(j, carry):
            side_before, side_here, rest_here, nodes = carry
            side_after, rest_after = density_terms(j + 2)
            nodes_after = node_plane(j + 1)
            inner = inverse[0, rows, :]
            edge = inverse[1, rows, :]
            weight = jnp.where(
                ((j == 1) & first_x) | ((j == NXL) & last_x),
                edge,
                jnp.where(((j == 0) & first_x) | ((j == NXL + 1) & last_x), 0.0, inner),
            )
            physical = (rest_here + side_before + side_after) * weight
            kind = kind_of[j, rows, :]
            physical = jnp.where(kind == 1.0, 1.0, jnp.where(kind == 2.0, 0.0, physical))
            energy = element_energy(nodes, nodes_after)
            spread[j, rows, :] = -DERIVATIVE * physical * physical * energy * weight
            return side_here, side_after, rest_after, nodes_after

        side_0, _ = density_terms(0)
        side_1, rest_1 = density_terms(1)
        lax.fori_loop(0, NXL + 2, rim_plane, (side_0, side_1, rest_1, node_plane(0)))

    weights = []
    for slot in (0, 1):
        weights.append(
            filter_terms(
                inverse[slot, pl.ds(0, 8), :],
                inverse[slot, pl.ds(1, 8), :],
                inverse[slot, pl.ds(2, 8), :],
                first,
                last,
            )
        )
    (side_inner, rest_inner), (side_edge, rest_edge) = weights

    def spread_terms(plane):
        return filter_terms(
            spread[plane, pl.ds(0, 8), :],
            spread[plane, pl.ds(1, 8), :],
            spread[plane, pl.ds(2, 8), :],
            first,
            last,
        )

    def side_of(plane):
        return jnp.where(
            ((plane == 1) & first_x) | ((plane == NXL) & last_x),
            side_edge,
            jnp.where(
                ((plane == 0) & first_x) | ((plane == NXL + 1) & last_x), 0.0, side_inner
            ),
        )

    def out_plane(x, carry):
        side_before, side_here, rest_here = carry
        side_after, rest_after = spread_terms(x + 2)
        sens = rest_here + side_before + side_after
        rest_weight = jnp.where(
            ((x == 0) & first_x) | ((x == NXL - 1) & last_x), rest_edge, rest_inner
        )
        weight = rest_weight + side_of(x) + side_of(x + 2)
        here = density[x]
        kind = passive[x]
        sensitivity[x] = sens
        scaled[x] = here * jnp.sqrt(-sens / weight)
        fixed = jnp.where(kind == 1, 1.0, 0.0)
        lower[x] = jnp.where(kind == 0, jnp.maximum(here - MOVE_LIMIT, 0.0), fixed)
        upper[x] = jnp.where(kind == 0, jnp.minimum(here + MOVE_LIMIT, 1.0), fixed)
        return side_here, side_after, rest_after

    side_0, _ = spread_terms(0)
    side_1, rest_1 = spread_terms(1)
    lax.fori_loop(0, NXL, out_plane, (side_0, side_1, rest_1))

    def volume_group(g, carry):
        scales = [factors[8 * g + k] for k in range(8)]
        totals = [jnp.zeros((8, NZ), jnp.float32) for _ in range(8)]
        for x in range(NXL):
            values, floor, ceiling = scaled[x], lower[x], upper[x]
            for k in range(8):
                totals[k] += jnp.minimum(jnp.maximum(values * scales[k], floor), ceiling)
        for k in range(8):
            partial[pl.ds(pl.multiple_of(64 * g + 8 * k, 8), 8), :] = totals[k]
        return carry

    lax.fori_loop(0, SLOTS // 8, volume_group, 0)
    rows_of = [partial[pl.ds(s, SLOTS, stride=8), :] for s in range(8)]
    lines = ((rows_of[0] + rows_of[1]) + (rows_of[2] + rows_of[3])) + (
        (rows_of[4] + rows_of[5]) + (rows_of[6] + rows_of[7])
    )
    volumes = lax.dot_general(
        jnp.ones((8, NZ), jnp.float32),
        lines,
        (((1,), (1,)), ((), ())),
        precision=lax.Precision.HIGHEST,
        preferred_element_type=jnp.float32,
    )
    for copy in range(copies):
        for half in (0, 1):
            sums_out[copy, pl.ds(half, 1), :] = volumes[0:1, half * NZ : (half + 1) * NZ]


def add_copies(received, out, *, copies):
    total = jnp.sum(received[...], axis=0)
    for copy in range(copies):
        out[copy] = total


def finish(received, scaled, density, passive, new_density, *, target):
    volumes = jnp.sum(received[...], axis=0)
    slot = lax.broadcasted_iota(jnp.int32, (2, NZ), 0) * NZ + lax.broadcasted_iota(
        jnp.int32, (2, NZ), 1
    )
    above = jnp.sum(jnp.where((volumes > target) & (slot < TRIALS), 1.0, 0.0))
    middle = -BRACKET + STEP * above + 0.5 * STEP
    factor = jnp.exp(jnp.full((8, NZ), -0.5, jnp.float32) * middle)
    here = density[...]
    kind = passive[...]
    fixed = jnp.where(kind == 1, 1.0, 0.0)
    lower = jnp.where(kind == 0, jnp.maximum(here - MOVE_LIMIT, 0.0), fixed)
    upper = jnp.where(kind == 0, jnp.minimum(here + MOVE_LIMIT, 1.0), fixed)
    new_density[...] = jnp.minimum(jnp.maximum(scaled[...] * factor[None], lower), upper)


def f32(*shape):
    return jax.ShapeDtypeStruct(shape, jnp.float32)


def call(kernel, inputs, outputs, scratch=(), specs=None):
    return pl.pallas_call(
        kernel,
        out_shape=outputs,
        in_specs=specs or [VMEM] * inputs,
        out_specs=jax.tree.map(lambda _: VMEM, outputs),
        scratch_shapes=list(scratch),
    )


def shifted(block, axis, distance):
    devices = range(lax.axis_size(axis))
    route = [(i - distance, i) for i in devices if i - distance in devices]
    return lax.ppermute(block, axis, route)


def per_device(density, displacement, passive):
    count_x, count_y = lax.axis_size("gx"), lax.axis_size("gy")
    assert density.shape == (NXL, NYL, NZ)
    to_low, to_high = call(pack_y, 3, (f32(9 * NXL, NZ), f32(6 * NXL, NZ)))(
        density, displacement, passive
    )
    y_high = shifted(to_low, "gy", -1)
    y_low = shifted(to_high, "gy", 1)
    to_low, to_high = call(pack_x, 5, (f32(104, NZ), f32(80, NZ)))(
        density, displacement, passive, y_high, y_low
    )
    x_high = shifted(to_low, "gx", -1)
    x_low = shifted(to_high, "gx", 1)

    block = (NXL, NYL, NZ)
    plane = 2 * count_y
    layers = count_x // 2
    sensitivity, scaled, volumes = call(
        functools.partial(update, copies=plane),
        8,
        (f32(*block), f32(*block), f32(plane, 2, NZ)),
        (
            pltpu.VMEM((NXL + 4, 24, NZ), jnp.float32),
            pltpu.VMEM((3, NXL + 3, 24, NZ), jnp.float32),
            pltpu.VMEM((NXL + 2, 16, NZ), jnp.float32),
            pltpu.VMEM((NXL + 2, 16, NZ), jnp.float32),
            pltpu.VMEM((2, 16, NZ), jnp.float32),
            pltpu.VMEM(block, jnp.float32),
            pltpu.VMEM(block, jnp.float32),
            pltpu.VMEM((8 * SLOTS, NZ), jnp.float32),
        ),
        specs=[SMEM] + [VMEM] * 7,
    )(trial_factors(), density, displacement, passive, y_high, y_low, x_high, x_low)

    across = [
        [(2 * z + core) * count_y + y for core in (0, 1) for y in range(count_y)]
        for z in range(layers)
    ]
    along = [
        [(2 * z + core) * count_y + y for z in range(layers)]
        for core in (0, 1)
        for y in range(count_y)
    ]
    volumes = lax.all_to_all(volumes, ("gx", "gy"), 0, 0, axis_index_groups=across)
    volumes = call(functools.partial(add_copies, copies=layers), 1, f32(layers, 2, NZ))(volumes)
    volumes = lax.all_to_all(volumes, ("gx", "gy"), 0, 0, axis_index_groups=along)
    target = VOLUME_SHARE * (count_x * NXL) * (count_y * NYL) * NZ
    new_density = call(functools.partial(finish, target=target), 4, f32(*block))(
        volumes, scaled, density, passive
    )
    return new_density, sensitivity


def solution(mesh):
    return jax.shard_map(
        per_device,
        mesh=mesh,
        in_specs=(P("gx", "gy", None), P(None, "gx", "gy", None), P("gx", "gy", None)),
        out_specs=(P("gx", "gy", None), P("gx", "gy", None)),
        check_vma=False,
    )
```

```python
import functools
import math

import jax
import jax.numpy as jnp
import numpy as np
from jax import lax
from jax.experimental import pallas as pl
from jax.experimental.pallas import tpu as pltpu
from jax.sharding import PartitionSpec as P

BISECT = 8
BRACKET = 8.0
MOVE_LIMIT = 0.2
VOLUME_SHARE = 0.35
DERIVATIVE = 3.0 * (1.0 - 1e-09)
EDGE_WEIGHT = 1.5 - math.sqrt(2.0)
POISSON = 0.3
LAME = POISSON / ((1.0 + POISSON) * (1.0 - 2.0 * POISSON))
SHEAR = 0.5 / (1.0 + POISSON)

NXL = 16
NYL = 8
NZ = 128
TRIALS = 2 ** BISECT - 1
SLOTS = TRIALS + 1
STEP = 2.0 * BRACKET / 2 ** BISECT

VMEM = pl.BlockSpec(memory_space=pltpu.VMEM)
SMEM = pl.BlockSpec(memory_space=pltpu.SMEM)


def trial_factors():
    middles = -BRACKET + STEP * np.arange(1, SLOTS + 1, dtype=np.float64)
    return np.exp(-0.5 * middles).astype(np.float32)


def pack_y(
    density_far, displacement_far, passive_far, density, displacement, passive, to_low, to_high, sems
):
    copies = [
        pltpu.make_async_copy(far, local, sems.at[i])
        for i, (far, local) in enumerate(
            (
                (density_far, density),
                (displacement_far, displacement),
                (passive_far, passive),
            )
        )
    ]
    for copy in copies:
        copy.start()
    for copy in copies:
        copy.wait()
    for row in (0, 1):
        to_low[pl.ds(row * NXL, NXL), :] = density[:, row, :]
        to_high[pl.ds(row * NXL, NXL), :] = density[:, NYL - 2 + row, :]
    for c in range(3):
        for row in (0, 1):
            to_low[pl.ds((2 + 2 * c + row) * NXL, NXL), :] = displacement[c, :, row, :]
        to_high[pl.ds((2 + c) * NXL, NXL), :] = displacement[c, :, NYL - 1, :]
    to_low[pl.ds(8 * NXL, NXL), :] = passive[:, 0, :].astype(jnp.float32)
    to_high[pl.ds(5 * NXL, NXL), :] = passive[:, NYL - 1, :].astype(jnp.float32)


def pack_x(density, displacement, passive, y_high, y_low, to_low, to_high):
    for k in (0, 1):
        to_low[pl.ds(8 * k, 8), :] = density[k]
        to_high[pl.ds(8 * k, 8), :] = density[NXL - 2 + k]
    for c in range(3):
        for k in (0, 1):
            to_low[pl.ds(8 * (2 + 2 * c + k), 8), :] = displacement[c, k]
        to_high[pl.ds(8 * (2 + c), 8), :] = displacement[c, NXL - 1]
    to_low[pl.ds(64, 8), :] = passive[0].astype(jnp.float32)
    to_high[pl.ds(40, 8), :] = passive[NXL - 1].astype(jnp.float32)
    for base, first, out in ((72, 0, to_low), (48, NXL - 2, to_high)):
        for kind in range(9):
            out[pl.ds(base + 2 * kind, 2), :] = y_high[pl.ds(NXL * kind + first, 2), :]
        for kind in range(6):
            out[pl.ds(base + 18 + 2 * kind, 2), :] = y_low[pl.ds(NXL * kind + first, 2), :]
        out[pl.ds(base + 30, 2), :] = jnp.zeros((2, NZ), jnp.float32)


def z_sum(f, first, last):
    return jnp.where(first, 0.0, pltpu.roll(f, 1, 1)) + jnp.where(
        last, 0.0, pltpu.roll(f, NZ - 1, 1)
    )


def filter_terms(low, mid, high, first, last):
    across = z_sum(mid, first, last)
    along = low + high
    both = across + along
    side = 0.5 * mid + EDGE_WEIGHT * both
    rest = 1.5 * mid + 0.5 * both + EDGE_WEIGHT * z_sum(along, first, last)
    return side, rest


def corner_sums(here, above, last):
    total = here + above
    slope = above - here
    total_next = jnp.where(last, 0.0, pltpu.roll(total, NZ - 1, 1))
    slope_next = jnp.where(last, 0.0, pltpu.roll(slope, NZ - 1, 1))
    return (total + total_next, total_next - total, slope + slope_next, slope_next - slope)


def element_energy(before, after):
    modes = []
    for c in range(3):
        for k in range(4):
            low, high = before[4 * c + k], after[4 * c + k]
            modes.append((low + high, high - low))
    u, v, w = (
        {(a, k // 2, k % 2): modes[4 * c + k][a] for a in (0, 1) for k in range(4)}
        for c in range(3)
    )

    def sq(x):
        return x * x

    trace = sq(u[1, 0, 0] + v[0, 1, 0] + w[0, 0, 1]) + (1.0 / 3.0) * (
        sq(v[1, 1, 0] + w[1, 0, 1]) + sq(u[1, 1, 0] + w[0, 1, 1]) + sq(u[1, 0, 1] + v[0, 1, 1])
    )
    normal = sq(u[1, 0, 0]) + sq(v[0, 1, 0]) + sq(w[0, 0, 1])
    linear = (
        sq(v[1, 1, 0])
        + sq(w[1, 0, 1])
        + sq(u[1, 1, 0])
        + sq(w[0, 1, 1])
        + sq(u[1, 0, 1])
        + sq(v[0, 1, 1])
    )
    bilinear = sq(u[1, 1, 1]) + sq(v[1, 1, 1]) + sq(w[1, 1, 1])
    shear = (
        sq(u[0, 1, 0] + v[1, 0, 0]) + sq(u[0, 0, 1] + w[1, 0, 0]) + sq(v[0, 0, 1] + w[0, 1, 0])
    )
    twist = (
        sq(u[0, 1, 1] + v[1, 0, 1]) + sq(u[0, 1, 1] + w[1, 1, 0]) + sq(v[1, 0, 1] + w[1, 1, 0])
    )
    return (
        (LAME / 16.0) * trace
        + (SHEAR / 8.0) * normal
        + (SHEAR / 16.0) * (linear + shear)
        + ((LAME + 4.0 * SHEAR) / 144.0) * bilinear
        + (SHEAR / 48.0) * twist
    )


def update(
    factors,
    density,
    displacement,
    passive,
    y_high,
    y_low,
    x_high,
    x_low,
    sensitivity,
    scaled,
    sums_out,
    dens,
    disp,
    kind_of,
    spread,
    inverse,
    lower,
    upper,
    partial,
    *,
    copies,
):
    last_x = lax.axis_index("gx") == lax.axis_size("gx") - 1
    first_x = lax.axis_index("gx") == 0
    start_y = lax.axis_index("gy") * NYL
    total_y = lax.axis_size("gy") * NYL

    dens[pl.ds(2, NXL), pl.ds(2, NYL), :] = density[...]
    disp[:, pl.ds(1, NXL), pl.ds(1, NYL), :] = displacement[...]
    kind_of[pl.ds(1, NXL), pl.ds(1, NYL), :] = passive[...].astype(jnp.float32)
    for k in (0, 1):
        dens[pl.ds(2, NXL), NYL + 2 + k, :] = y_high[pl.ds(k * NXL, NXL), :]
        dens[pl.ds(2, NXL), k, :] = y_low[pl.ds(k * NXL, NXL), :]
        dens[NXL + 2 + k, pl.ds(2, NYL), :] = x_high[pl.ds(8 * k, 8), :]
        dens[k, pl.ds(2, NYL), :] = x_low[pl.ds(8 * k, 8), :]
        for row in (0, 1):
            dens[NXL + 2 + k, pl.ds(NYL + 2 + row, 1), :] = x_high[pl.ds(72 + 2 * row + k, 1), :]
            dens[NXL + 2 + k, pl.ds(row, 1), :] = x_high[pl.ds(90 + 2 * row + k, 1), :]
            dens[k, pl.ds(NYL + 2 + row, 1), :] = x_low[pl.ds(48 + 2 * row + k, 1), :]
            dens[k, pl.ds(row, 1), :] = x_low[pl.ds(66 + 2 * row + k, 1), :]
    for c in range(3):
        for k in (0, 1):
            at = 2 + 2 * c + k
            disp[c, pl.ds(1, NXL), NYL + 1 + k, :] = y_high[pl.ds(at * NXL, NXL), :]
            disp[c, NXL + 1 + k, pl.ds(1, NYL), :] = x_high[pl.ds(8 * at, 8), :]
            for row in (0, 1):
                disp[c, NXL + 1 + k, pl.ds(NYL + 1 + row, 1), :] = x_high[
                    pl.ds(72 + 2 * (2 + 2 * c + row) + k, 1), :
                ]
            disp[c, NXL + 1 + k, pl.ds(0, 1), :] = x_high[pl.ds(90 + 2 * (2 + c) + k, 1), :]
            disp[c, 0, pl.ds(NYL + 1 + k, 1), :] = x_low[pl.ds(48 + 2 * at + 1, 1), :]
        disp[c, pl.ds(1, NXL), 0, :] = y_low[pl.ds((2 + c) * NXL, NXL), :]
        disp[c, 0, pl.ds(1, NYL), :] = x_low[pl.ds(8 * (2 + c), 8), :]
        disp[c, 0, pl.ds(0, 1), :] = x_low[pl.ds(66 + 2 * (2 + c) + 1, 1), :]
    kind_of[pl.ds(1, NXL), NYL + 1, :] = y_high[pl.ds(8 * NXL, NXL), :]
    kind_of[pl.ds(1, NXL), 0, :] = y_low[pl.ds(5 * NXL, NXL), :]
    kind_of[NXL + 1, pl.ds(1, NYL), :] = x_high[pl.ds(64, 8), :]
    kind_of[0, pl.ds(1, NYL), :] = x_low[pl.ds(40, 8), :]
    kind_of[NXL + 1, pl.ds(NYL + 1, 1), :] = x_high[pl.ds(72 + 16, 1), :]
    kind_of[NXL + 1, pl.ds(0, 1), :] = x_high[pl.ds(90 + 10, 1), :]
    kind_of[0, pl.ds(NYL + 1, 1), :] = x_low[pl.ds(48 + 17, 1), :]
    kind_of[0, pl.ds(0, 1), :] = x_low[pl.ds(66 + 11, 1), :]

    lane = lax.broadcasted_iota(jnp.int32, (8, NZ), 1)
    first = lane == 0
    last = lane == NZ - 1
    along_z = jnp.where(first | last, 1.0, 2.0)

    for v in (0, 1):
        index_y = start_y - 1 + 8 * v + lax.broadcasted_iota(jnp.int32, (8, NZ), 0)
        inside = (index_y >= 0) & (index_y < total_y)
        along_y = jnp.where((index_y == 0) | (index_y == total_y - 1), 1.0, 2.0)
        base = 1.5 + 0.5 * (along_y + along_z) + EDGE_WEIGHT * along_y * along_z
        slope = 0.5 + EDGE_WEIGHT * (along_y + along_z)
        for slot, along_x in ((0, 2.0), (1, 1.0)):
            inverse[slot, pl.ds(8 * v, 8), :] = jnp.where(
                inside, 1.0 / (base + along_x * slope), 0.0
            )

    for v in (0, 1):
        rows = pl.ds(8 * v, 8)

        def density_terms(plane):
            return filter_terms(
                dens[plane, rows, :],
                dens[plane, pl.ds(8 * v + 1, 8), :],
                dens[plane, pl.ds(8 * v + 2, 8), :],
                first,
                last,
            )

        def node_plane(plane):
            return sum(
                (
                    corner_sums(
                        disp[c, plane, rows, :], disp[c, plane, pl.ds(8 * v + 1, 8), :], last
                    )
                    for c in range(3)
                ),
                (),
            )

        def rim_plane(j, carry):
            side_before, side_here, rest_here, nodes = carry
            side_after, rest_after = density_terms(j + 2)
            nodes_after = node_plane(j + 1)
            inner = inverse[0, rows, :]
            edge = inverse[1, rows, :]
            weight = jnp.where(
                ((j == 1) & first_x) | ((j == NXL) & last_x),
                edge,
                jnp.where(((j == 0) & first_x) | ((j == NXL + 1) & last_x), 0.0, inner),
            )
            physical = (rest_here + side_before + side_after) * weight
            kind = kind_of[j, rows, :]
            physical = jnp.where(kind == 1.0, 1.0, jnp.where(kind == 2.0, 0.0, physical))
            energy = element_energy(nodes, nodes_after)
            spread[j, rows, :] = -DERIVATIVE * physical * physical * energy * weight
            return side_here, side_after, rest_after, nodes_after

        side_0, _ = density_terms(0)
        side_1, rest_1 = density_terms(1)
        lax.fori_loop(0, NXL + 2, rim_plane, (side_0, side_1, rest_1, node_plane(0)))

    weights = []
    for slot in (0, 1):
        weights.append(
            filter_terms(
                inverse[slot, pl.ds(0, 8), :],
                inverse[slot, pl.ds(1, 8), :],
                inverse[slot, pl.ds(2, 8), :],
                first,
                last,
            )
        )
    (side_inner, rest_inner), (side_edge, rest_edge) = weights

    def spread_terms(plane):
        return filter_terms(
            spread[plane, pl.ds(0, 8), :],
            spread[plane, pl.ds(1, 8), :],
            spread[plane, pl.ds(2, 8), :],
            first,
            last,
        )

    def side_of(plane):
        return jnp.where(
            ((plane == 1) & first_x) | ((plane == NXL) & last_x),
            side_edge,
            jnp.where(
                ((plane == 0) & first_x) | ((plane == NXL + 1) & last_x), 0.0, side_inner
            ),
        )

    def out_plane(x, carry):
        side_before, side_here, rest_here = carry
        side_after, rest_after = spread_terms(x + 2)
        sens = rest_here + side_before + side_after
        rest_weight = jnp.where(
            ((x == 0) & first_x) | ((x == NXL - 1) & last_x), rest_edge, rest_inner
        )
        weight = rest_weight + side_of(x) + side_of(x + 2)
        here = density[x]
        kind = passive[x]
        sensitivity[x] = sens
        scaled[x] = here * jnp.sqrt(-sens / weight)
        fixed = jnp.where(kind == 1, 1.0, 0.0)
        lower[x] = jnp.where(kind == 0, jnp.maximum(here - MOVE_LIMIT, 0.0), fixed)
        upper[x] = jnp.where(kind == 0, jnp.minimum(here + MOVE_LIMIT, 1.0), fixed)
        return side_here, side_after, rest_after

    side_0, _ = spread_terms(0)
    side_1, rest_1 = spread_terms(1)
    lax.fori_loop(0, NXL, out_plane, (side_0, side_1, rest_1))

    def volume_group(g, carry):
        scales = [factors[8 * g + k] for k in range(8)]
        totals = [jnp.zeros((8, NZ), jnp.float32) for _ in range(8)]
        for x in range(NXL):
            values, floor, ceiling = scaled[x], lower[x], upper[x]
            for k in range(8):
                totals[k] += jnp.minimum(jnp.maximum(values * scales[k], floor), ceiling)
        for k in range(8):
            partial[pl.ds(pl.multiple_of(64 * g + 8 * k, 8), 8), :] = totals[k]
        return carry

    lax.fori_loop(0, SLOTS // 8, volume_group, 0)
    rows_of = [partial[pl.ds(s, SLOTS, stride=8), :] for s in range(8)]
    lines = ((rows_of[0] + rows_of[1]) + (rows_of[2] + rows_of[3])) + (
        (rows_of[4] + rows_of[5]) + (rows_of[6] + rows_of[7])
    )
    volumes = lax.dot_general(
        jnp.ones((8, NZ), jnp.float32),
        lines,
        (((1,), (1,)), ((), ())),
        precision=lax.Precision.HIGHEST,
        preferred_element_type=jnp.float32,
    )
    for copy in range(copies):
        for half in (0, 1):
            sums_out[copy, pl.ds(half, 1), :] = volumes[0:1, half * NZ : (half + 1) * NZ]


def add_copies(received, out, *, copies):
    total = jnp.sum(received[...], axis=0)
    for copy in range(copies):
        out[copy] = total


def finish(received, scaled, density, passive, new_density, *, target):
    volumes = jnp.sum(received[...], axis=0)
    slot = lax.broadcasted_iota(jnp.int32, (2, NZ), 0) * NZ + lax.broadcasted_iota(
        jnp.int32, (2, NZ), 1
    )
    above = jnp.sum(jnp.where((volumes > target) & (slot < TRIALS), 1.0, 0.0))
    middle = -BRACKET + STEP * above + 0.5 * STEP
    factor = jnp.exp(jnp.full((8, NZ), -0.5, jnp.float32) * middle)
    here = density[...]
    kind = passive[...]
    fixed = jnp.where(kind == 1, 1.0, 0.0)
    lower = jnp.where(kind == 0, jnp.maximum(here - MOVE_LIMIT, 0.0), fixed)
    upper = jnp.where(kind == 0, jnp.minimum(here + MOVE_LIMIT, 1.0), fixed)
    new_density[...] = jnp.minimum(jnp.maximum(scaled[...] * factor[None], lower), upper)


def f32(*shape):
    return jax.ShapeDtypeStruct(shape, jnp.float32)


def near(*shape):
    return pltpu.VMEM(shape, jnp.float32)


def far(array):
    return pltpu.with_memory_space_constraint(array, pltpu.HBM)


def held(array):
    return pltpu.with_memory_space_constraint(array, pltpu.VMEM)


def call(kernel, inputs, outputs, scratch=(), specs=None):
    return pl.pallas_call(
        kernel,
        out_shape=outputs,
        in_specs=specs or [VMEM] * inputs,
        out_specs=jax.tree.map(lambda _: VMEM, outputs),
        scratch_shapes=list(scratch),
        compiler_params=pltpu.CompilerParams(vmem_limit_bytes=16 << 20),
    )


def shifted(block, axis, distance):
    devices = range(lax.axis_size(axis))
    route = [(i - distance, i) for i in devices if i - distance in devices]
    return lax.ppermute(block, axis, route)


def per_device(density, displacement, passive):
    count_x, count_y = lax.axis_size("gx"), lax.axis_size("gy")
    assert density.shape == (NXL, NYL, NZ)
    block = (NXL, NYL, NZ)
    density, displacement, passive, to_low, to_high = call(
        pack_y,
        3,
        (
            near(*block),
            near(3, *block),
            pltpu.VMEM(block, jnp.int32),
            near(9 * NXL, NZ),
            near(6 * NXL, NZ),
        ),
        [pltpu.SemaphoreType.DMA((3,))],
        specs=[pl.BlockSpec(memory_space=pltpu.HBM)] * 3,
    )(far(density), far(displacement), far(passive))
    y_high = held(shifted(to_low, "gy", -1))
    y_low = held(shifted(to_high, "gy", 1))
    to_low, to_high = call(pack_x, 5, (near(104, NZ), near(80, NZ)))(
        density, displacement, passive, y_high, y_low
    )
    x_high = held(shifted(to_low, "gx", -1))
    x_low = held(shifted(to_high, "gx", 1))

    plane = 2 * count_y
    layers = count_x // 2
    sensitivity, scaled, volumes = call(
        functools.partial(update, copies=plane),
        8,
        (f32(*block), near(*block), near(plane, 2, NZ)),
        (
            pltpu.VMEM((NXL + 4, 24, NZ), jnp.float32),
            pltpu.VMEM((3, NXL + 3, 24, NZ), jnp.float32),
            pltpu.VMEM((NXL + 2, 16, NZ), jnp.float32),
            pltpu.VMEM((NXL + 2, 16, NZ), jnp.float32),
            pltpu.VMEM((2, 16, NZ), jnp.float32),
            pltpu.VMEM(block, jnp.float32),
            pltpu.VMEM(block, jnp.float32),
            pltpu.VMEM((8 * SLOTS, NZ), jnp.float32),
        ),
        specs=[SMEM] + [VMEM] * 7,
    )(trial_factors(), density, displacement, passive, y_high, y_low, x_high, x_low)

    across = [
        [(2 * z + core) * count_y + y for core in (0, 1) for y in range(count_y)]
        for z in range(layers)
    ]
    along = [
        [(2 * z + core) * count_y + y for z in range(layers)]
        for core in (0, 1)
        for y in range(count_y)
    ]
    volumes = lax.all_to_all(volumes, ("gx", "gy"), 0, 0, axis_index_groups=across)
    volumes = call(functools.partial(add_copies, copies=layers), 1, near(layers, 2, NZ))(held(volumes))
    volumes = lax.all_to_all(volumes, ("gx", "gy"), 0, 0, axis_index_groups=along)
    target = VOLUME_SHARE * (count_x * NXL) * (count_y * NYL) * NZ
    new_density = call(functools.partial(finish, target=target), 4, f32(*block))(
        held(volumes), scaled, density, passive
    )
    return new_density, sensitivity


def solution(mesh):
    return jax.shard_map(
        per_device,
        mesh=mesh,
        in_specs=(P("gx", "gy", None), P(None, "gx", "gy", None), P("gx", "gy", None)),
        out_specs=(P("gx", "gy", None), P("gx", "gy", None)),
        check_vma=False,
    )
```

```python
import functools
import math

import jax
import jax.numpy as jnp
from jax import lax
from jax.experimental import pallas as pl
from jax.experimental.pallas import tpu as pltpu
from jax.sharding import PartitionSpec as P

BISECT = 8
BRACKET = 8.0
MOVE_LIMIT = 0.2
VOLUME_SHARE = 0.35
DERIVATIVE = 3.0 * (1.0 - 1e-09)
EDGE_WEIGHT = 1.5 - math.sqrt(2.0)
POISSON = 0.3
LAME = POISSON / ((1.0 + POISSON) * (1.0 - 2.0 * POISSON))
SHEAR = 0.5 / (1.0 + POISSON)

NXL = 16
NYL = 8
NZ = 128
TRIALS = 2 ** BISECT - 1
SLOTS = TRIALS + 1
STEP = 2.0 * BRACKET / 2 ** BISECT
GROUP = 16

VMEM = pl.BlockSpec(memory_space=pltpu.VMEM)


def pack_y(
    density_far, displacement_far, passive_far, density, displacement, passive, to_low, to_high, sems
):
    copies = [
        pltpu.make_async_copy(far, local, sems.at[i])
        for i, (far, local) in enumerate(
            (
                (density_far, density),
                (displacement_far, displacement),
                (passive_far, passive),
            )
        )
    ]
    for copy in copies:
        copy.start()
    for copy in copies:
        copy.wait()
    for row in (0, 1):
        to_low[pl.ds(row * NXL, NXL), :] = density[:, row, :]
        to_high[pl.ds(row * NXL, NXL), :] = density[:, NYL - 2 + row, :]
    for c in range(3):
        for row in (0, 1):
            to_low[pl.ds((2 + 2 * c + row) * NXL, NXL), :] = displacement[c, :, row, :]
        to_high[pl.ds((2 + c) * NXL, NXL), :] = displacement[c, :, NYL - 1, :]
    to_low[pl.ds(8 * NXL, NXL), :] = passive[:, 0, :].astype(jnp.float32)
    to_high[pl.ds(5 * NXL, NXL), :] = passive[:, NYL - 1, :].astype(jnp.float32)


def pack_x(density, displacement, passive, y_high, y_low, after, to_low, to_high):
    del after
    for k in (0, 1):
        to_low[pl.ds(8 * k, 8), :] = density[k]
        to_high[pl.ds(8 * k, 8), :] = density[NXL - 2 + k]
    for c in range(3):
        for k in (0, 1):
            to_low[pl.ds(8 * (2 + 2 * c + k), 8), :] = displacement[c, k]
        to_high[pl.ds(8 * (2 + c), 8), :] = displacement[c, NXL - 1]
    to_low[pl.ds(64, 8), :] = passive[0].astype(jnp.float32)
    to_high[pl.ds(40, 8), :] = passive[NXL - 1].astype(jnp.float32)
    for base, first, out in ((72, 0, to_low), (48, NXL - 2, to_high)):
        for kind in range(9):
            out[pl.ds(base + 2 * kind, 2), :] = y_high[pl.ds(NXL * kind + first, 2), :]
        for kind in range(6):
            out[pl.ds(base + 18 + 2 * kind, 2), :] = y_low[pl.ds(NXL * kind + first, 2), :]
        out[pl.ds(base + 30, 2), :] = jnp.zeros((2, NZ), jnp.float32)


def lane_ends(height):
    lane = lax.broadcasted_iota(jnp.int32, (height, NZ), 1)
    return lane == 0, lane == NZ - 1


def z_sum(f, first, last):
    return jnp.where(first, 0.0, pltpu.roll(f, 1, 1)) + jnp.where(
        last, 0.0, pltpu.roll(f, NZ - 1, 1)
    )


def filter_terms(low, mid, high, first, last):
    across = z_sum(mid, first, last)
    along = low + high
    both = across + along
    side = 0.5 * mid + EDGE_WEIGHT * both
    rest = 1.5 * mid + 0.5 * both + EDGE_WEIGHT * z_sum(along, first, last)
    return side, rest


def corner_sums(here, above, last):
    total = here + above
    slope = above - here
    total_next = jnp.where(last, 0.0, pltpu.roll(total, NZ - 1, 1))
    slope_next = jnp.where(last, 0.0, pltpu.roll(slope, NZ - 1, 1))
    return (total + total_next, total_next - total, slope + slope_next, slope_next - slope)


def element_energy(before, after):
    modes = []
    for c in range(3):
        for k in range(4):
            low, high = before[4 * c + k], after[4 * c + k]
            modes.append((low + high, high - low))
    u, v, w = (
        {(a, k // 2, k % 2): modes[4 * c + k][a] for a in (0, 1) for k in range(4)}
        for c in range(3)
    )

    def sq(x):
        return x * x

    trace = sq(u[1, 0, 0] + v[0, 1, 0] + w[0, 0, 1]) + (1.0 / 3.0) * (
        sq(v[1, 1, 0] + w[1, 0, 1]) + sq(u[1, 1, 0] + w[0, 1, 1]) + sq(u[1, 0, 1] + v[0, 1, 1])
    )
    normal = sq(u[1, 0, 0]) + sq(v[0, 1, 0]) + sq(w[0, 0, 1])
    linear = (
        sq(v[1, 1, 0])
        + sq(w[1, 0, 1])
        + sq(u[1, 1, 0])
        + sq(w[0, 1, 1])
        + sq(u[1, 0, 1])
        + sq(v[0, 1, 1])
    )
    bilinear = sq(u[1, 1, 1]) + sq(v[1, 1, 1]) + sq(w[1, 1, 1])
    shear = (
        sq(u[0, 1, 0] + v[1, 0, 0]) + sq(u[0, 0, 1] + w[1, 0, 0]) + sq(v[0, 0, 1] + w[0, 1, 0])
    )
    twist = (
        sq(u[0, 1, 1] + v[1, 0, 1]) + sq(u[0, 1, 1] + w[1, 1, 0]) + sq(v[1, 0, 1] + w[1, 1, 0])
    )
    return (
        (LAME / 16.0) * trace
        + (SHEAR / 8.0) * normal
        + (SHEAR / 16.0) * (linear + shear)
        + ((LAME + 4.0 * SHEAR) / 144.0) * bilinear
        + (SHEAR / 48.0) * twist
    )


def interior_energy(displacement, energy, inverse, weights, factors):
    start_y = lax.axis_index("gy") * NYL
    total_y = lax.axis_size("gy") * NYL
    first, last = lane_ends(NYL)

    def nodes(plane):
        here = []
        for c in range(3):
            f = displacement[c, plane]
            here.extend(corner_sums(f, pltpu.roll(f, NYL - 1, 0), last))
        return tuple(here)

    def plane_energy(x, before):
        after = nodes(x + 1)
        energy[x] = element_energy(before, after)
        return after

    lax.fori_loop(0, NXL - 1, plane_energy, nodes(0))
    energy[NXL - 1] = jnp.zeros((NYL, NZ), jnp.float32)
    trial = lax.broadcasted_iota(jnp.int32, (SLOTS, NZ), 0).astype(jnp.float32)
    factors[...] = jnp.exp(-0.5 * (-BRACKET + STEP * (trial + 1.0)))

    along_z = jnp.where(first | last, 1.0, 2.0)
    for v in (0, 1):
        index_y = start_y - 1 + 8 * v + lax.broadcasted_iota(jnp.int32, (8, NZ), 0)
        inside = (index_y >= 0) & (index_y < total_y)
        along_y = jnp.where((index_y == 0) | (index_y == total_y - 1), 1.0, 2.0)
        base = 1.5 + 0.5 * (along_y + along_z) + EDGE_WEIGHT * along_y * along_z
        slope = 0.5 + EDGE_WEIGHT * (along_y + along_z)
        for slot, along_x in ((0, 2.0), (1, 1.0)):
            inverse[slot, pl.ds(8 * v, 8), :] = jnp.where(
                inside, 1.0 / (base + along_x * slope), 0.0
            )
    for slot in (0, 1):
        side, rest = filter_terms(
            inverse[slot, pl.ds(0, 8), :],
            inverse[slot, pl.ds(1, 8), :],
            inverse[slot, pl.ds(2, 8), :],
            first,
            last,
        )
        weights[2 * slot] = side
        weights[2 * slot + 1] = rest


def spread_of(filtered, weight, kind, energy):
    physical = filtered * weight
    physical = jnp.where(kind == 1.0, 1.0, jnp.where(kind == 2.0, 0.0, physical))
    return -DERIVATIVE * physical * physical * energy * weight


def around(ref, plane, first, last):
    return filter_terms(
        ref[plane, pl.ds(7, 8), :],
        ref[plane, pl.ds(8, 8), :],
        ref[plane, pl.ds(9, 8), :],
        first,
        last,
    )


def add_volumes(planes, factors, scaled, lower, upper, start, partial):
    def volume_group(g, carry):
        base = pl.multiple_of(8 * GROUP * g, 8 * GROUP)
        scales = [
            jnp.broadcast_to(factors[pl.ds(GROUP * g + k, 1), :], (8, NZ)) for k in range(GROUP)
        ]
        if start is None:
            totals = [jnp.zeros((8, NZ), jnp.float32) for _ in range(GROUP)]
        else:
            totals = [start[pl.ds(base + 8 * k, 8), :] for k in range(GROUP)]
        for place, x in planes:
            values, floor, ceiling = scaled[place], lower[x], upper[x]
            for k in range(GROUP):
                totals[k] += jnp.minimum(jnp.maximum(values * scales[k], floor), ceiling)
        for k in range(GROUP):
            partial[pl.ds(base + 8 * k, 8), :] = totals[k]
        return carry

    lax.fori_loop(0, SLOTS // GROUP, volume_group, 0)


def middle(
    factors,
    density,
    passive,
    own_energy,
    inverse,
    weights,
    y_high,
    y_low,
    to_low,
    to_high,
    spread,
    sensitivity,
    scaled,
    lower,
    upper,
    partial,
    dens,
    energy,
):
    def rows(ref, kind):
        return ref[pl.ds(kind * NXL, NXL), :]

    first, last = lane_ends(NXL)

    def row_nodes(ref, step, at):
        return [rows(ref, at + step * c) for c in range(3)]

    def row_energy(here, above):
        before, after = [], []
        for c in range(3):
            sums = corner_sums(here[c], above[c], last)
            before.extend(sums)
            after.extend(pltpu.roll(f, NXL - 1, 0) for f in sums)
        return element_energy(before, after)

    nodes_8 = row_nodes(y_high, 2, 2)
    energy_low = row_energy(row_nodes(y_low, 1, 2), row_nodes(to_low, 2, 2))
    energy_7 = row_energy(row_nodes(to_high, 1, 2), nodes_8)
    energy_high = row_energy(nodes_8, row_nodes(y_high, 2, 3))

    dens[:, pl.ds(8, NYL), :] = density[...]
    dens[:, 7, :] = rows(y_low, 1)
    dens[:, 16, :] = rows(y_high, 0)
    energy[...] = own_energy[...]
    energy[:, 7, :] = energy_7

    for row, low, mid, high, kind, row_energies in (
        (0, rows(y_low, 0), rows(y_low, 1), rows(to_low, 0), rows(y_low, 5), energy_low),
        (9, rows(to_high, 1), rows(y_high, 0), rows(y_high, 1), rows(y_high, 8), energy_high),
    ):
        side, rest = filter_terms(low, mid, high, first, last)
        filtered = rest + pltpu.roll(side, 1, 0) + pltpu.roll(side, NXL - 1, 0)
        weight = jnp.broadcast_to(inverse[0, pl.ds(row, 1), :], (NXL, NZ))
        spread[:, row + 7, :] = spread_of(filtered, weight, kind, row_energies)

    first, last = lane_ends(NYL)
    weight = inverse[0, pl.ds(1, 8), :]

    def spread_plane(x, carry):
        side_before, side_here, rest_here = carry
        side_after, rest_after = around(dens, x + 1, first, last)
        spread[x, pl.ds(8, 8), :] = spread_of(
            rest_here + side_before + side_after,
            weight,
            passive[x].astype(jnp.float32),
            energy[x],
        )
        return side_here, side_after, rest_after

    side_0, _ = around(dens, 0, first, last)
    lax.fori_loop(
        1, NXL - 1, spread_plane, (side_0,) + around(dens, 1, first, last), unroll=2
    )

    scale = 1.0 / (weights[1] + 2.0 * weights[0])

    def out_plane(x, carry):
        side_before, side_here, rest_here = carry
        side_after, rest_after = around(spread, x + 1, first, last)
        sens = rest_here + side_before + side_after
        sensitivity[x] = sens
        scaled[x] = density[x] * jnp.sqrt(-sens * scale)
        return side_here, side_after, rest_after

    side_1, _ = around(spread, 1, first, last)
    lax.fori_loop(
        2, NXL - 2, out_plane, (side_1,) + around(spread, 2, first, last), unroll=2
    )

    here = density[...]
    kind = passive[...]
    fixed = jnp.where(kind == 1, 1.0, 0.0)
    lower[...] = jnp.where(kind == 0, jnp.maximum(here - MOVE_LIMIT, 0.0), fixed)
    upper[...] = jnp.where(kind == 0, jnp.minimum(here + MOVE_LIMIT, 1.0), fixed)
    add_volumes(
        [(x, x) for x in range(2, NXL - 2)], factors, scaled, lower, upper, None, partial
    )


def edges(
    factors,
    density,
    displacement,
    passive,
    y_high,
    y_low,
    x_high,
    x_low,
    inverse,
    weights,
    spread,
    lower,
    upper,
    start,
    sensitivity,
    scaled,
    sums_out,
    dens,
    disp,
    kind_of,
    rim,
    partial,
    *,
    copies,
):
    first, last = lane_ends(NYL)
    at_end = (
        lax.axis_index("gx") == 0,
        lax.axis_index("gx") == lax.axis_size("gx") - 1,
    )
    for side, (own, far, slabs, low_rows, pick) in enumerate(
        ((0, x_low, 48, 66, 1), (NXL - 2, x_high, 72, 90, 0))
    ):
        for k in (0, 1):
            own_at, far_at = (2 + k, k) if side == 0 else (k, 2 + k)
            dens[side, own_at, pl.ds(2, NYL), :] = density[own + k]
            dens[side, far_at, pl.ds(2, NYL), :] = far[pl.ds(8 * k, 8), :]
            for row in (0, 1):
                dens[side, own_at, pl.ds(NYL + 2 + row, 1), :] = y_high[
                    pl.ds(row * NXL + own + k, 1), :
                ]
                dens[side, own_at, pl.ds(row, 1), :] = y_low[pl.ds(row * NXL + own + k, 1), :]
                dens[side, far_at, pl.ds(NYL + 2 + row, 1), :] = far[
                    pl.ds(slabs + 2 * row + k, 1), :
                ]
                dens[side, far_at, pl.ds(row, 1), :] = far[pl.ds(low_rows + 2 * row + k, 1), :]
        for c in range(3):
            mine = ((1, 0), (2, 1)) if side == 0 else ((0, NXL - 1),)
            theirs = ((0, 2 + c, 1),) if side == 0 else ((1, 2 + 2 * c, 0), (2, 3 + 2 * c, 1))
            for at, x in mine:
                disp[side, c, at, pl.ds(1, NYL), :] = displacement[c, x]
                disp[side, c, at, pl.ds(0, 1), :] = y_low[pl.ds((2 + c) * NXL + x, 1), :]
                for row in (0, 1):
                    disp[side, c, at, pl.ds(NYL + 1 + row, 1), :] = y_high[
                        pl.ds((2 + 2 * c + row) * NXL + x, 1), :
                    ]
            for at, slab, k in theirs:
                disp[side, c, at, pl.ds(1, NYL), :] = far[pl.ds(8 * slab, 8), :]
                disp[side, c, at, pl.ds(0, 1), :] = far[pl.ds(low_rows + 2 * (2 + c) + k, 1), :]
                for row in (0, 1):
                    disp[side, c, at, pl.ds(NYL + 1 + row, 1), :] = far[
                        pl.ds(slabs + 2 * (2 + 2 * c + row) + k, 1), :
                    ]
        own_at, far_at, x = (1, 0, 0) if side == 0 else (0, 1, NXL - 1)
        kind_of[side, own_at, pl.ds(1, NYL), :] = passive[x].astype(jnp.float32)
        kind_of[side, own_at, pl.ds(0, 1), :] = y_low[pl.ds(5 * NXL + x, 1), :]
        kind_of[side, own_at, pl.ds(NYL + 1, 1), :] = y_high[pl.ds(8 * NXL + x, 1), :]
        kind_of[side, far_at, pl.ds(1, NYL), :] = far[pl.ds(40 if side == 0 else 64, 8), :]
        kind_of[side, far_at, pl.ds(0, 1), :] = far[pl.ds(low_rows + 10 + pick, 1), :]
        kind_of[side, far_at, pl.ds(NYL + 1, 1), :] = far[pl.ds(slabs + 16 + pick, 1), :]

        for v in (0, 1):
            rows = pl.ds(8 * v, 8)
            terms = [
                filter_terms(
                    dens[side, p, rows, :],
                    dens[side, p, pl.ds(8 * v + 1, 8), :],
                    dens[side, p, pl.ds(8 * v + 2, 8), :],
                    first,
                    last,
                )
                for p in range(4)
            ]
            nodes = []
            for p in range(3):
                sums = []
                for c in range(3):
                    sums.extend(
                        corner_sums(
                            disp[side, c, p, rows, :],
                            disp[side, c, p, pl.ds(8 * v + 1, 8), :],
                            last,
                        )
                    )
                nodes.append(sums)
            inner = inverse[0, rows, :]
            by_place = (
                jnp.where(at_end[side], 0.0, inner),
                jnp.where(at_end[side], inverse[1, rows, :], inner),
            )
            for k in (0, 1):
                weight = by_place[k] if side == 0 else by_place[1 - k]
                rim[side, (k if side == 0 else 2 + k), pl.ds(7 + 8 * v, 8), :] = spread_of(
                    terms[k + 1][1] + terms[k][0] + terms[k + 2][0],
                    weight,
                    kind_of[side, k, rows, :],
                    element_energy(nodes[k], nodes[k + 1]),
                )
        for k in (0, 1):
            rim[side, (2 + k if side == 0 else k), :, :] = spread[1 + k if side == 0 else 13 + k]

    side_inner, rest_inner, side_edge, rest_edge = (weights[i] for i in range(4))
    for side in (0, 1):
        outer_side = jnp.where(at_end[side], 0.0, side_inner)
        next_side = jnp.where(at_end[side], side_edge, side_inner)
        outer = jnp.where(at_end[side], rest_edge, rest_inner) + outer_side + side_inner
        inner = rest_inner + next_side + side_inner
        terms = [around(rim.at[side], p, first, last) for p in range(4)]
        for k in (0, 1):
            x = k if side == 0 else NXL - 2 + k
            sens = terms[k + 1][1] + terms[k][0] + terms[k + 2][0]
            weight = outer if k == side else inner
            sensitivity[2 * side + k] = sens
            scaled[2 * side + k] = density[x] * jnp.sqrt(-sens / weight)

    add_volumes(
        [(0, 0), (1, 1), (2, NXL - 2), (3, NXL - 1)],
        factors,
        scaled,
        lower,
        upper,
        start,
        partial,
    )
    rows_of = [partial[pl.ds(s, SLOTS, stride=8), :] for s in range(8)]
    lines = ((rows_of[0] + rows_of[1]) + (rows_of[2] + rows_of[3])) + (
        (rows_of[4] + rows_of[5]) + (rows_of[6] + rows_of[7])
    )
    volumes = lax.dot_general(
        jnp.ones((8, NZ), jnp.float32),
        lines,
        (((1,), (1,)), ((), ())),
        precision=lax.Precision.HIGHEST,
        preferred_element_type=jnp.float32,
    )
    odd = lax.broadcasted_iota(jnp.int32, (8, NZ), 0) > 0
    pair = jnp.where(odd, volumes[:, NZ:], volumes[:, :NZ])[0:2]
    for copy in range(copies):
        sums_out[copy] = pair


def add_copies(received, out, *, copies):
    total = jnp.sum(received[...], axis=0)
    for copy in range(copies):
        out[copy] = total


def finish(
    received,
    scaled,
    scaled_edge,
    lower,
    upper,
    sensitivity,
    sensitivity_edge,
    new_density,
    sensitivity_out,
    sems,
    *,
    target,
):
    inner = pl.ds(2, NXL - 4)
    ends = ((pl.ds(0, 2), pl.ds(0, 2)), (pl.ds(2, 2), pl.ds(NXL - 2, 2)))
    copies = [pltpu.make_async_copy(sensitivity.at[inner], sensitivity_out.at[inner], sems.at[0])]
    for i, (place, planes) in enumerate(ends):
        copies.append(
            pltpu.make_async_copy(
                sensitivity_edge.at[place], sensitivity_out.at[planes], sems.at[1 + i]
            )
        )
    for copy in copies:
        copy.start()
    volumes = jnp.sum(received[...], axis=0)
    slot = lax.broadcasted_iota(jnp.int32, (2, NZ), 0) * NZ + lax.broadcasted_iota(
        jnp.int32, (2, NZ), 1
    )
    above = jnp.sum(jnp.where((volumes > target) & (slot < TRIALS), 1.0, 0.0))
    middle_end = -BRACKET + STEP * above + 0.5 * STEP
    factor = jnp.exp(jnp.full((8, NZ), -0.5, jnp.float32) * middle_end)[None]
    for ref, place, planes in ((scaled, inner, inner),) + tuple(
        (scaled_edge, place, planes) for place, planes in ends
    ):
        new_density[planes] = jnp.minimum(
            jnp.maximum(ref[place] * factor, lower[planes]), upper[planes]
        )
    for copy in copies:
        copy.wait()


def f32(*shape):
    return jax.ShapeDtypeStruct(shape, jnp.float32)


def near(*shape, dtype=jnp.float32):
    return pltpu.VMEM(shape, dtype)


def far(array):
    return pltpu.with_memory_space_constraint(array, pltpu.HBM)


def held(array):
    return pltpu.with_memory_space_constraint(array, pltpu.VMEM)


def call(kernel, outputs, inputs, scratch=(), specs=None, out_specs=None, cost=0):
    return pl.pallas_call(
        kernel,
        out_shape=outputs,
        in_specs=specs or [VMEM] * len(inputs),
        out_specs=out_specs or jax.tree.map(lambda _: VMEM, outputs),
        scratch_shapes=list(scratch),
        cost_estimate=pl.CostEstimate(
            flops=cost * 4000, bytes_accessed=cost * 1000, transcendentals=0
        ),
        compiler_params=pltpu.CompilerParams(vmem_limit_bytes=16 << 20),
    )(*inputs)


def shifted(block, axis, distance):
    devices = range(lax.axis_size(axis))
    route = [(i - distance, i) for i in devices if i - distance in devices]
    return lax.ppermute(block, axis, route)


def per_device(density, displacement, passive):
    count_x, count_y = lax.axis_size("gx"), lax.axis_size("gy")
    assert density.shape == (NXL, NYL, NZ)
    block = (NXL, NYL, NZ)
    density, displacement, passive, y_to_low, y_to_high = call(
        pack_y,
        (
            near(*block),
            near(3, *block),
            near(*block, dtype=jnp.int32),
            near(9 * NXL, NZ),
            near(6 * NXL, NZ),
        ),
        (far(density), far(displacement), far(passive)),
        [pltpu.SemaphoreType.DMA((3,))],
        specs=[pl.BlockSpec(memory_space=pltpu.HBM)] * 3,
        cost=1000,
    )
    y_high = held(shifted(y_to_low, "gy", -1))
    y_low = held(shifted(y_to_high, "gy", 1))
    own_energy, inverse, weights, factors = call(
        interior_energy,
        (near(*block), near(2, 16, NZ), near(4, NYL, NZ), near(SLOTS, NZ)),
        (displacement,),
        cost=1000,
    )
    to_low, to_high = call(
        pack_x,
        (near(104, NZ), near(80, NZ)),
        (density, displacement, passive, y_high, y_low, weights),
        cost=500,
    )
    x_high = held(shifted(to_low, "gx", -1))
    x_low = held(shifted(to_high, "gx", 1))
    spread, sensitivity, scaled, lower, upper, partial = call(
        middle,
        (near(NXL, 24, NZ),) + (near(*block),) * 4 + (near(8 * SLOTS, NZ),),
        (
            factors,
            density,
            passive,
            own_energy,
            inverse,
            weights,
            y_high,
            y_low,
            y_to_low,
            y_to_high,
        ),
        [pltpu.VMEM((NXL, 24, NZ), jnp.float32), pltpu.VMEM(block, jnp.float32)],
        cost=5000,
    )
    plane = 2 * count_y
    layers = count_x // 2
    sensitivity_edge, scaled_edge, volumes = call(
        functools.partial(edges, copies=plane),
        (near(4, NYL, NZ), near(4, NYL, NZ), near(plane, 2, NZ)),
        (
            factors,
            density,
            displacement,
            passive,
            y_high,
            y_low,
            x_high,
            x_low,
            inverse,
            weights,
            spread,
            lower,
            upper,
            partial,
        ),
        [
            pltpu.VMEM((2, 4, 24, NZ), jnp.float32),
            pltpu.VMEM((2, 3, 3, 24, NZ), jnp.float32),
            pltpu.VMEM((2, 2, 16, NZ), jnp.float32),
            pltpu.VMEM((2, 4, 24, NZ), jnp.float32),
            pltpu.VMEM((8 * SLOTS, NZ), jnp.float32),
        ],
        cost=3000,
    )

    across = [
        [(2 * z + core) * count_y + y for core in (0, 1) for y in range(count_y)]
        for z in range(layers)
    ]
    along = [
        [(2 * z + core) * count_y + y for z in range(layers)]
        for core in (0, 1)
        for y in range(count_y)
    ]
    volumes = lax.all_to_all(volumes, ("gx", "gy"), 0, 0, axis_index_groups=across)
    volumes = call(
        functools.partial(add_copies, copies=layers),
        near(layers, 2, NZ),
        (held(volumes),),
        cost=300,
    )
    volumes = lax.all_to_all(volumes, ("gx", "gy"), 0, 0, axis_index_groups=along)
    target = VOLUME_SHARE * (count_x * NXL) * (count_y * NYL) * NZ
    new_density, sensitivity = call(
        functools.partial(finish, target=target),
        (f32(*block), f32(*block)),
        (held(volumes), scaled, scaled_edge, lower, upper, sensitivity, sensitivity_edge),
        [pltpu.SemaphoreType.DMA((3,))],
        out_specs=(VMEM, pl.BlockSpec(memory_space=pltpu.HBM)),
        cost=500,
    )
    return new_density, sensitivity


def solution(mesh):
    return jax.shard_map(
        per_device,
        mesh=mesh,
        in_specs=(P("gx", "gy", None), P(None, "gx", "gy", None), P("gx", "gy", None)),
        out_specs=(P("gx", "gy", None), P("gx", "gy", None)),
        check_vma=False,
    )
```

```python
import functools
import math

import jax
import jax.numpy as jnp
from jax import lax
from jax.experimental import pallas as pl
from jax.experimental.pallas import tpu as pltpu
from jax.sharding import PartitionSpec as P

BISECT = 8
BRACKET = 8.0
MOVE_LIMIT = 0.2
VOLUME_SHARE = 0.35
DERIVATIVE = 3.0 * (1.0 - 1e-09)
EDGE_WEIGHT = 1.5 - math.sqrt(2.0)
POISSON = 0.3
LAME = POISSON / ((1.0 + POISSON) * (1.0 - 2.0 * POISSON))
SHEAR = 0.5 / (1.0 + POISSON)

NXL = 16
NYL = 8
NZ = 128
TRIALS = 2 ** BISECT - 1
SLOTS = TRIALS + 1
STEP = 2.0 * BRACKET / 2 ** BISECT
GROUP = 16

VMEM = pl.BlockSpec(memory_space=pltpu.VMEM)


def is_even(axis):
    return lax.rem(lax.axis_index(axis), 2) == 0


def pack_y(
    density_far, displacement_far, passive_far, density, displacement, passive, send_a, send_b, sems
):
    copies = [
        pltpu.make_async_copy(far, local, sems.at[i])
        for i, (far, local) in enumerate(
            (
                (density_far, density),
                (displacement_far, displacement),
                (passive_far, passive),
            )
        )
    ]
    for copy in copies:
        copy.start()
    for copy in copies:
        copy.wait()

    def fill(to_low, to_high):
        for row in (0, 1):
            to_low[pl.ds(row * NXL, NXL), :] = density[:, row, :]
            to_high[pl.ds(row * NXL, NXL), :] = density[:, NYL - 2 + row, :]
        for c in range(3):
            for row in (0, 1):
                to_low[pl.ds((2 + 2 * c + row) * NXL, NXL), :] = displacement[c, :, row, :]
            to_high[pl.ds((2 + c) * NXL, NXL), :] = displacement[c, :, NYL - 1, :]
        to_low[pl.ds(8 * NXL, NXL), :] = passive[:, 0, :].astype(jnp.float32)
        to_high[pl.ds(5 * NXL, NXL), :] = passive[:, NYL - 1, :].astype(jnp.float32)
        to_high[pl.ds(6 * NXL, 3 * NXL), :] = jnp.zeros((3 * NXL, NZ), jnp.float32)

    even = is_even("gy")
    pl.when(even)(lambda: fill(send_b, send_a))
    pl.when(jnp.logical_not(even))(lambda: fill(send_a, send_b))


def pack_x(
    density, displacement, passive, received_a, received_b, after, y_high, y_low, send_a, send_b
):
    del after
    even = is_even("gy")
    y_high[...] = jnp.where(even, received_a[...], received_b[...])
    low = pl.ds(0, 6 * NXL)
    y_low[...] = jnp.where(even, received_b[low, :], received_a[low, :])

    def fill(to_low, to_high):
        for k in (0, 1):
            to_low[pl.ds(8 * k, 8), :] = density[k]
            to_high[pl.ds(8 * k, 8), :] = density[NXL - 2 + k]
        for c in range(3):
            for k in (0, 1):
                to_low[pl.ds(8 * (2 + 2 * c + k), 8), :] = displacement[c, k]
            to_high[pl.ds(8 * (2 + c), 8), :] = displacement[c, NXL - 1]
        to_low[pl.ds(64, 8), :] = passive[0].astype(jnp.float32)
        to_high[pl.ds(40, 8), :] = passive[NXL - 1].astype(jnp.float32)
        for base, first, out in ((72, 0, to_low), (48, NXL - 2, to_high)):
            for kind in range(9):
                out[pl.ds(base + 2 * kind, 2), :] = y_high[pl.ds(NXL * kind + first, 2), :]
            for kind in range(6):
                out[pl.ds(base + 18 + 2 * kind, 2), :] = y_low[pl.ds(NXL * kind + first, 2), :]
            out[pl.ds(base + 30, 2), :] = jnp.zeros((2, NZ), jnp.float32)
        to_high[pl.ds(80, 24), :] = jnp.zeros((24, NZ), jnp.float32)

    even_x = is_even("gx")
    pl.when(even_x)(lambda: fill(send_b, send_a))
    pl.when(jnp.logical_not(even_x))(lambda: fill(send_a, send_b))


def lane_ends(height):
    lane = lax.broadcasted_iota(jnp.int32, (height, NZ), 1)
    return lane == 0, lane == NZ - 1


def z_sum(f, first, last):
    return jnp.where(first, 0.0, pltpu.roll(f, 1, 1)) + jnp.where(
        last, 0.0, pltpu.roll(f, NZ - 1, 1)
    )


def filter_terms(low, mid, high, first, last):
    across = z_sum(mid, first, last)
    along = low + high
    both = across + along
    side = 0.5 * mid + EDGE_WEIGHT * both
    rest = 1.5 * mid + 0.5 * both + EDGE_WEIGHT * z_sum(along, first, last)
    return side, rest


def corner_sums(here, above, last):
    total = here + above
    slope = above - here
    total_next = jnp.where(last, 0.0, pltpu.roll(total, NZ - 1, 1))
    slope_next = jnp.where(last, 0.0, pltpu.roll(slope, NZ - 1, 1))
    return (total + total_next, total_next - total, slope + slope_next, slope_next - slope)


def element_energy(before, after):
    modes = []
    for c in range(3):
        for k in range(4):
            low, high = before[4 * c + k], after[4 * c + k]
            modes.append((low + high, high - low))
    u, v, w = (
        {(a, k // 2, k % 2): modes[4 * c + k][a] for a in (0, 1) for k in range(4)}
        for c in range(3)
    )

    def sq(x):
        return x * x

    trace = sq(u[1, 0, 0] + v[0, 1, 0] + w[0, 0, 1]) + (1.0 / 3.0) * (
        sq(v[1, 1, 0] + w[1, 0, 1]) + sq(u[1, 1, 0] + w[0, 1, 1]) + sq(u[1, 0, 1] + v[0, 1, 1])
    )
    normal = sq(u[1, 0, 0]) + sq(v[0, 1, 0]) + sq(w[0, 0, 1])
    linear = (
        sq(v[1, 1, 0])
        + sq(w[1, 0, 1])
        + sq(u[1, 1, 0])
        + sq(w[0, 1, 1])
        + sq(u[1, 0, 1])
        + sq(v[0, 1, 1])
    )
    bilinear = sq(u[1, 1, 1]) + sq(v[1, 1, 1]) + sq(w[1, 1, 1])
    shear = (
        sq(u[0, 1, 0] + v[1, 0, 0]) + sq(u[0, 0, 1] + w[1, 0, 0]) + sq(v[0, 0, 1] + w[0, 1, 0])
    )
    twist = (
        sq(u[0, 1, 1] + v[1, 0, 1]) + sq(u[0, 1, 1] + w[1, 1, 0]) + sq(v[1, 0, 1] + w[1, 1, 0])
    )
    return (
        (LAME / 16.0) * trace
        + (SHEAR / 8.0) * normal
        + (SHEAR / 16.0) * (linear + shear)
        + ((LAME + 4.0 * SHEAR) / 144.0) * bilinear
        + (SHEAR / 48.0) * twist
    )


def interior_energy(displacement, energy, inverse, weights, factors):
    start_y = lax.axis_index("gy") * NYL
    total_y = lax.axis_size("gy") * NYL
    first, last = lane_ends(NYL)

    def nodes(plane):
        here = []
        for c in range(3):
            f = displacement[c, plane]
            here.extend(corner_sums(f, pltpu.roll(f, NYL - 1, 0), last))
        return tuple(here)

    def plane_energy(x, before):
        after = nodes(x + 1)
        energy[x] = element_energy(before, after)
        return after

    lax.fori_loop(0, NXL - 1, plane_energy, nodes(0))
    energy[NXL - 1] = jnp.zeros((NYL, NZ), jnp.float32)
    trial = lax.broadcasted_iota(jnp.int32, (SLOTS, NZ), 0).astype(jnp.float32)
    factors[...] = jnp.exp(-0.5 * (-BRACKET + STEP * (trial + 1.0)))

    along_z = jnp.where(first | last, 1.0, 2.0)
    for v in (0, 1):
        index_y = start_y - 1 + 8 * v + lax.broadcasted_iota(jnp.int32, (8, NZ), 0)
        inside = (index_y >= 0) & (index_y < total_y)
        along_y = jnp.where((index_y == 0) | (index_y == total_y - 1), 1.0, 2.0)
        base = 1.5 + 0.5 * (along_y + along_z) + EDGE_WEIGHT * along_y * along_z
        slope = 0.5 + EDGE_WEIGHT * (along_y + along_z)
        for slot, along_x in ((0, 2.0), (1, 1.0)):
            inverse[slot, pl.ds(8 * v, 8), :] = jnp.where(
                inside, 1.0 / (base + along_x * slope), 0.0
            )
    for slot in (0, 1):
        side, rest = filter_terms(
            inverse[slot, pl.ds(0, 8), :],
            inverse[slot, pl.ds(1, 8), :],
            inverse[slot, pl.ds(2, 8), :],
            first,
            last,
        )
        weights[2 * slot] = side
        weights[2 * slot + 1] = rest


def spread_of(filtered, weight, kind, energy):
    physical = filtered * weight
    physical = jnp.where(kind == 1.0, 1.0, jnp.where(kind == 2.0, 0.0, physical))
    return -DERIVATIVE * physical * physical * energy * weight


def around(ref, plane, first, last):
    return filter_terms(
        ref[plane, pl.ds(7, 8), :],
        ref[plane, pl.ds(8, 8), :],
        ref[plane, pl.ds(9, 8), :],
        first,
        last,
    )


def add_volumes(planes, factors, scaled, lower, upper, start, partial):
    def volume_group(g, carry):
        base = pl.multiple_of(8 * GROUP * g, 8 * GROUP)
        scales = [
            jnp.broadcast_to(factors[pl.ds(GROUP * g + k, 1), :], (8, NZ)) for k in range(GROUP)
        ]
        if start is None:
            totals = [jnp.zeros((8, NZ), jnp.float32) for _ in range(GROUP)]
        else:
            totals = [start[pl.ds(base + 8 * k, 8), :] for k in range(GROUP)]
        for place, x in planes:
            values, floor, ceiling = scaled[place], lower[x], upper[x]
            for k in range(GROUP):
                totals[k] += jnp.minimum(jnp.maximum(values * scales[k], floor), ceiling)
        for k in range(GROUP):
            partial[pl.ds(base + 8 * k, 8), :] = totals[k]
        return carry

    lax.fori_loop(0, SLOTS // GROUP, volume_group, 0)


def middle(
    factors,
    density,
    passive,
    own_energy,
    inverse,
    weights,
    y_high,
    y_low,
    sent_a,
    sent_b,
    spread,
    sensitivity,
    scaled,
    lower,
    upper,
    partial,
    dens,
    energy,
):
    def rows(ref, kind):
        return ref[pl.ds(kind * NXL, NXL), :]

    even = is_even("gy")

    def sent_low(kind):
        return jnp.where(even, rows(sent_b, kind), rows(sent_a, kind))

    def sent_high(kind):
        return jnp.where(even, rows(sent_a, kind), rows(sent_b, kind))

    first, last = lane_ends(NXL)

    def row_nodes(ref, step, at):
        return [rows(ref, at + step * c) for c in range(3)]

    def row_energy(here, above):
        before, after = [], []
        for c in range(3):
            sums = corner_sums(here[c], above[c], last)
            before.extend(sums)
            after.extend(pltpu.roll(f, NXL - 1, 0) for f in sums)
        return element_energy(before, after)

    nodes_8 = row_nodes(y_high, 2, 2)
    energy_low = row_energy(row_nodes(y_low, 1, 2), [sent_low(2 + 2 * c) for c in range(3)])
    energy_7 = row_energy([sent_high(2 + c) for c in range(3)], nodes_8)
    energy_high = row_energy(nodes_8, row_nodes(y_high, 2, 3))

    dens[:, pl.ds(8, NYL), :] = density[...]
    dens[:, 7, :] = rows(y_low, 1)
    dens[:, 16, :] = rows(y_high, 0)
    energy[...] = own_energy[...]
    energy[:, 7, :] = energy_7

    for row, low, mid, high, kind, row_energies in (
        (0, rows(y_low, 0), rows(y_low, 1), sent_low(0), rows(y_low, 5), energy_low),
        (9, sent_high(1), rows(y_high, 0), rows(y_high, 1), rows(y_high, 8), energy_high),
    ):
        side, rest = filter_terms(low, mid, high, first, last)
        filtered = rest + pltpu.roll(side, 1, 0) + pltpu.roll(side, NXL - 1, 0)
        weight = jnp.broadcast_to(inverse[0, pl.ds(row, 1), :], (NXL, NZ))
        spread[:, row + 7, :] = spread_of(filtered, weight, kind, row_energies)

    first, last = lane_ends(NYL)
    weight = inverse[0, pl.ds(1, 8), :]

    def spread_plane(x, carry):
        side_before, side_here, rest_here = carry
        side_after, rest_after = around(dens, x + 1, first, last)
        spread[x, pl.ds(8, 8), :] = spread_of(
            rest_here + side_before + side_after,
            weight,
            passive[x].astype(jnp.float32),
            energy[x],
        )
        return side_here, side_after, rest_after

    side_0, _ = around(dens, 0, first, last)
    lax.fori_loop(
        1, NXL - 1, spread_plane, (side_0,) + around(dens, 1, first, last), unroll=2
    )

    scale = 1.0 / (weights[1] + 2.0 * weights[0])

    def out_plane(x, carry):
        side_before, side_here, rest_here = carry
        side_after, rest_after = around(spread, x + 1, first, last)
        sens = rest_here + side_before + side_after
        sensitivity[x] = sens
        scaled[x] = density[x] * jnp.sqrt(-sens * scale)
        return side_here, side_after, rest_after

    side_1, _ = around(spread, 1, first, last)
    lax.fori_loop(
        2, NXL - 2, out_plane, (side_1,) + around(spread, 2, first, last), unroll=2
    )

    here = density[...]
    kind = passive[...]
    fixed = jnp.where(kind == 1, 1.0, 0.0)
    lower[...] = jnp.where(kind == 0, jnp.maximum(here - MOVE_LIMIT, 0.0), fixed)
    upper[...] = jnp.where(kind == 0, jnp.minimum(here + MOVE_LIMIT, 1.0), fixed)
    add_volumes(
        [(x, x) for x in range(2, NXL - 2)], factors, scaled, lower, upper, None, partial
    )


def edges(
    factors,
    density,
    displacement,
    passive,
    y_high,
    y_low,
    received_a,
    received_b,
    inverse,
    weights,
    spread,
    lower,
    upper,
    start,
    sensitivity,
    scaled,
    sums_out,
    dens,
    disp,
    kind_of,
    rim,
    partial,
    x_high,
    x_low,
    *,
    copies,
):
    even = is_even("gx")
    x_high[...] = jnp.where(even, received_a[...], received_b[...])
    x_low[...] = jnp.where(even, received_b[...], received_a[...])
    first, last = lane_ends(NYL)
    at_end = (
        lax.axis_index("gx") == 0,
        lax.axis_index("gx") == lax.axis_size("gx") - 1,
    )
    for side, (own, far, slabs, low_rows, pick) in enumerate(
        ((0, x_low, 48, 66, 1), (NXL - 2, x_high, 72, 90, 0))
    ):
        for k in (0, 1):
            own_at, far_at = (2 + k, k) if side == 0 else (k, 2 + k)
            dens[side, own_at, pl.ds(2, NYL), :] = density[own + k]
            dens[side, far_at, pl.ds(2, NYL), :] = far[pl.ds(8 * k, 8), :]
            for row in (0, 1):
                dens[side, own_at, pl.ds(NYL + 2 + row, 1), :] = y_high[
                    pl.ds(row * NXL + own + k, 1), :
                ]
                dens[side, own_at, pl.ds(row, 1), :] = y_low[pl.ds(row * NXL + own + k, 1), :]
                dens[side, far_at, pl.ds(NYL + 2 + row, 1), :] = far[
                    pl.ds(slabs + 2 * row + k, 1), :
                ]
                dens[side, far_at, pl.ds(row, 1), :] = far[pl.ds(low_rows + 2 * row + k, 1), :]
        for c in range(3):
            mine = ((1, 0), (2, 1)) if side == 0 else ((0, NXL - 1),)
            theirs = ((0, 2 + c, 1),) if side == 0 else ((1, 2 + 2 * c, 0), (2, 3 + 2 * c, 1))
            for at, x in mine:
                disp[side, c, at, pl.ds(1, NYL), :] = displacement[c, x]
                disp[side, c, at, pl.ds(0, 1), :] = y_low[pl.ds((2 + c) * NXL + x, 1), :]
                for row in (0, 1):
                    disp[side, c, at, pl.ds(NYL + 1 + row, 1), :] = y_high[
                        pl.ds((2 + 2 * c + row) * NXL + x, 1), :
                    ]
            for at, slab, k in theirs:
                disp[side, c, at, pl.ds(1, NYL), :] = far[pl.ds(8 * slab, 8), :]
                disp[side, c, at, pl.ds(0, 1), :] = far[pl.ds(low_rows + 2 * (2 + c) + k, 1), :]
                for row in (0, 1):
                    disp[side, c, at, pl.ds(NYL + 1 + row, 1), :] = far[
                        pl.ds(slabs + 2 * (2 + 2 * c + row) + k, 1), :
                    ]
        own_at, far_at, x = (1, 0, 0) if side == 0 else (0, 1, NXL - 1)
        kind_of[side, own_at, pl.ds(1, NYL), :] = passive[x].astype(jnp.float32)
        kind_of[side, own_at, pl.ds(0, 1), :] = y_low[pl.ds(5 * NXL + x, 1), :]
        kind_of[side, own_at, pl.ds(NYL + 1, 1), :] = y_high[pl.ds(8 * NXL + x, 1), :]
        kind_of[side, far_at, pl.ds(1, NYL), :] = far[pl.ds(40 if side == 0 else 64, 8), :]
        kind_of[side, far_at, pl.ds(0, 1), :] = far[pl.ds(low_rows + 10 + pick, 1), :]
        kind_of[side, far_at, pl.ds(NYL + 1, 1), :] = far[pl.ds(slabs + 16 + pick, 1), :]

        for v in (0, 1):
            rows = pl.ds(8 * v, 8)
            terms = [
                filter_terms(
                    dens[side, p, rows, :],
                    dens[side, p, pl.ds(8 * v + 1, 8), :],
                    dens[side, p, pl.ds(8 * v + 2, 8), :],
                    first,
                    last,
                )
                for p in range(4)
            ]
            nodes = []
            for p in range(3):
                sums = []
                for c in range(3):
                    sums.extend(
                        corner_sums(
                            disp[side, c, p, rows, :],
                            disp[side, c, p, pl.ds(8 * v + 1, 8), :],
                            last,
                        )
                    )
                nodes.append(sums)
            inner = inverse[0, rows, :]
            by_place = (
                jnp.where(at_end[side], 0.0, inner),
                jnp.where(at_end[side], inverse[1, rows, :], inner),
            )
            for k in (0, 1):
                weight = by_place[k] if side == 0 else by_place[1 - k]
                rim[side, (k if side == 0 else 2 + k), pl.ds(7 + 8 * v, 8), :] = spread_of(
                    terms[k + 1][1] + terms[k][0] + terms[k + 2][0],
                    weight,
                    kind_of[side, k, rows, :],
                    element_energy(nodes[k], nodes[k + 1]),
                )
        for k in (0, 1):
            rim[side, (2 + k if side == 0 else k), :, :] = spread[1 + k if side == 0 else 13 + k]

    side_inner, rest_inner, side_edge, rest_edge = (weights[i] for i in range(4))
    for side in (0, 1):
        outer_side = jnp.where(at_end[side], 0.0, side_inner)
        next_side = jnp.where(at_end[side], side_edge, side_inner)
        outer = jnp.where(at_end[side], rest_edge, rest_inner) + outer_side + side_inner
        inner = rest_inner + next_side + side_inner
        terms = [around(rim.at[side], p, first, last) for p in range(4)]
        for k in (0, 1):
            x = k if side == 0 else NXL - 2 + k
            sens = terms[k + 1][1] + terms[k][0] + terms[k + 2][0]
            weight = outer if k == side else inner
            sensitivity[2 * side + k] = sens
            scaled[2 * side + k] = density[x] * jnp.sqrt(-sens / weight)

    add_volumes(
        [(0, 0), (1, 1), (2, NXL - 2), (3, NXL - 1)],
        factors,
        scaled,
        lower,
        upper,
        start,
        partial,
    )
    rows_of = [partial[pl.ds(s, SLOTS, stride=8), :] for s in range(8)]
    lines = ((rows_of[0] + rows_of[1]) + (rows_of[2] + rows_of[3])) + (
        (rows_of[4] + rows_of[5]) + (rows_of[6] + rows_of[7])
    )
    volumes = lax.dot_general(
        jnp.ones((8, NZ), jnp.float32),
        lines,
        (((1,), (1,)), ((), ())),
        precision=lax.Precision.HIGHEST,
        preferred_element_type=jnp.float32,
    )
    odd = lax.broadcasted_iota(jnp.int32, (8, NZ), 0) > 0
    pair = jnp.where(odd, volumes[:, NZ:], volumes[:, :NZ])[0:2]
    for copy in range(copies):
        sums_out[copy] = pair


def add_copies(received, out, *, copies):
    total = jnp.sum(received[...], axis=0)
    for copy in range(copies):
        out[copy] = total


def finish(
    received,
    scaled,
    scaled_edge,
    lower,
    upper,
    sensitivity,
    sensitivity_edge,
    new_density,
    sensitivity_out,
    sems,
    *,
    target,
):
    inner = pl.ds(2, NXL - 4)
    ends = ((pl.ds(0, 2), pl.ds(0, 2)), (pl.ds(2, 2), pl.ds(NXL - 2, 2)))
    copies = [pltpu.make_async_copy(sensitivity.at[inner], sensitivity_out.at[inner], sems.at[0])]
    for i, (place, planes) in enumerate(ends):
        copies.append(
            pltpu.make_async_copy(
                sensitivity_edge.at[place], sensitivity_out.at[planes], sems.at[1 + i]
            )
        )
    for copy in copies:
        copy.start()
    volumes = jnp.sum(received[...], axis=0)
    slot = lax.broadcasted_iota(jnp.int32, (2, NZ), 0) * NZ + lax.broadcasted_iota(
        jnp.int32, (2, NZ), 1
    )
    above = jnp.sum(jnp.where((volumes > target) & (slot < TRIALS), 1.0, 0.0))
    middle_end = -BRACKET + STEP * above + 0.5 * STEP
    factor = jnp.exp(jnp.full((8, NZ), -0.5, jnp.float32) * middle_end)[None]
    for ref, place, planes in ((scaled, inner, inner),) + tuple(
        (scaled_edge, place, planes) for place, planes in ends
    ):
        new_density[planes] = jnp.minimum(
            jnp.maximum(ref[place] * factor, lower[planes]), upper[planes]
        )
    for copy in copies:
        copy.wait()


def f32(*shape):
    return jax.ShapeDtypeStruct(shape, jnp.float32)


def near(*shape, dtype=jnp.float32):
    return pltpu.VMEM(shape, dtype)


def far(array):
    return pltpu.with_memory_space_constraint(array, pltpu.HBM)


def held(array):
    return pltpu.with_memory_space_constraint(array, pltpu.VMEM)


def call(kernel, outputs, inputs, scratch=(), specs=None, out_specs=None, cost=0):
    return pl.pallas_call(
        kernel,
        out_shape=outputs,
        in_specs=specs or [VMEM] * len(inputs),
        out_specs=out_specs or jax.tree.map(lambda _: VMEM, outputs),
        scratch_shapes=list(scratch),
        cost_estimate=pl.CostEstimate(
            flops=cost * 4000, bytes_accessed=cost * 1000, transcendentals=0
        ),
        compiler_params=pltpu.CompilerParams(vmem_limit_bytes=16 << 20),
    )(*inputs)


def swapped(block, axis, start):
    pairs = [(i, i + 1) for i in range(start, lax.axis_size(axis) - 1, 2)]
    return lax.ppermute(block, axis, pairs + [(j, i) for i, j in pairs])


def per_device(density, displacement, passive):
    count_x, count_y = lax.axis_size("gx"), lax.axis_size("gy")
    assert density.shape == (NXL, NYL, NZ)
    block = (NXL, NYL, NZ)
    density, displacement, passive, sent_a, sent_b = call(
        pack_y,
        (
            near(*block),
            near(3, *block),
            near(*block, dtype=jnp.int32),
            near(9 * NXL, NZ),
            near(9 * NXL, NZ),
        ),
        (far(density), far(displacement), far(passive)),
        [pltpu.SemaphoreType.DMA((3,))],
        specs=[pl.BlockSpec(memory_space=pltpu.HBM)] * 3,
        cost=1000,
    )
    received_a = held(swapped(sent_a, "gy", 0))
    received_b = held(swapped(sent_b, "gy", 1))
    own_energy, inverse, weights, factors = call(
        interior_energy,
        (near(*block), near(2, 16, NZ), near(4, NYL, NZ), near(SLOTS, NZ)),
        (displacement,),
        cost=1000,
    )
    y_high, y_low, to_a, to_b = call(
        pack_x,
        (near(9 * NXL, NZ), near(6 * NXL, NZ), near(104, NZ), near(104, NZ)),
        (density, displacement, passive, received_a, received_b, weights),
        cost=500,
    )
    received_a = held(swapped(to_a, "gx", 0))
    received_b = held(swapped(to_b, "gx", 1))
    spread, sensitivity, scaled, lower, upper, partial = call(
        middle,
        (near(NXL, 24, NZ),) + (near(*block),) * 4 + (near(8 * SLOTS, NZ),),
        (
            factors,
            density,
            passive,
            own_energy,
            inverse,
            weights,
            y_high,
            y_low,
            sent_a,
            sent_b,
        ),
        [pltpu.VMEM((NXL, 24, NZ), jnp.float32), pltpu.VMEM(block, jnp.float32)],
        cost=5000,
    )
    plane = 2 * count_y
    layers = count_x // 2
    sensitivity_edge, scaled_edge, volumes = call(
        functools.partial(edges, copies=plane),
        (near(4, NYL, NZ), near(4, NYL, NZ), near(plane, 2, NZ)),
        (
            factors,
            density,
            displacement,
            passive,
            y_high,
            y_low,
            received_a,
            received_b,
            inverse,
            weights,
            spread,
            lower,
            upper,
            partial,
        ),
        [
            pltpu.VMEM((2, 4, 24, NZ), jnp.float32),
            pltpu.VMEM((2, 3, 3, 24, NZ), jnp.float32),
            pltpu.VMEM((2, 2, 16, NZ), jnp.float32),
            pltpu.VMEM((2, 4, 24, NZ), jnp.float32),
            pltpu.VMEM((8 * SLOTS, NZ), jnp.float32),
            pltpu.VMEM((104, NZ), jnp.float32),
            pltpu.VMEM((104, NZ), jnp.float32),
        ],
        cost=3000,
    )

    across = [
        [(2 * z + core) * count_y + y for core in (0, 1) for y in range(count_y)]
        for z in range(layers)
    ]
    along = [
        [(2 * z + core) * count_y + y for z in range(layers)]
        for core in (0, 1)
        for y in range(count_y)
    ]
    volumes = lax.all_to_all(volumes, ("gx", "gy"), 0, 0, axis_index_groups=across)
    volumes = call(
        functools.partial(add_copies, copies=layers),
        near(layers, 2, NZ),
        (held(volumes),),
        cost=300,
    )
    volumes = lax.all_to_all(volumes, ("gx", "gy"), 0, 0, axis_index_groups=along)
    target = VOLUME_SHARE * (count_x * NXL) * (count_y * NYL) * NZ
    new_density, sensitivity = call(
        functools.partial(finish, target=target),
        (f32(*block), f32(*block)),
        (held(volumes), scaled, scaled_edge, lower, upper, sensitivity, sensitivity_edge),
        [pltpu.SemaphoreType.DMA((3,))],
        out_specs=(VMEM, pl.BlockSpec(memory_space=pltpu.HBM)),
        cost=500,
    )
    return new_density, sensitivity


def solution(mesh):
    return jax.shard_map(
        per_device,
        mesh=mesh,
        in_specs=(P("gx", "gy", None), P(None, "gx", "gy", None), P("gx", "gy", None)),
        out_specs=(P("gx", "gy", None), P("gx", "gy", None)),
        check_vma=False,
    )
```

```python
import functools
import math

import jax
import jax.numpy as jnp
from jax import lax
from jax.experimental import pallas as pl
from jax.experimental.pallas import tpu as pltpu
from jax.sharding import PartitionSpec as P

BISECT = 8
BRACKET = 8.0
MOVE_LIMIT = 0.2
VOLUME_SHARE = 0.35
DERIVATIVE = 3.0 * (1.0 - 1e-09)
EDGE_WEIGHT = 1.5 - math.sqrt(2.0)
POISSON = 0.3
LAME = POISSON / ((1.0 + POISSON) * (1.0 - 2.0 * POISSON))
SHEAR = 0.5 / (1.0 + POISSON)

NXL = 16
NYL = 8
NZ = 128
TRIALS = 2 ** BISECT - 1
SLOTS = TRIALS + 1
STEP = 2.0 * BRACKET / 2 ** BISECT
GROUP = 16
SIDE = 4

VMEM = pl.BlockSpec(memory_space=pltpu.VMEM)


def is_odd(axis):
    return lax.rem(lax.axis_index(axis), 2) == 1


def pack_y(
    density_far, displacement_far, passive_far, density, displacement, passive, send_a, send_b, sems
):
    copies = [
        pltpu.make_async_copy(far, local, sems.at[i])
        for i, (far, local) in enumerate(
            (
                (density_far, density),
                (displacement_far, displacement),
                (passive_far, passive),
            )
        )
    ]
    for copy in copies:
        copy.start()
    for copy in copies:
        copy.wait()

    def fill(to_low, to_high):
        for row in (0, 1):
            to_low[pl.ds(row * NXL, NXL), :] = density[:, row, :]
            to_high[pl.ds(row * NXL, NXL), :] = density[:, NYL - 2 + row, :]
        for c in range(3):
            for row in (0, 1):
                to_low[pl.ds((2 + 2 * c + row) * NXL, NXL), :] = displacement[c, :, row, :]
            to_high[pl.ds((2 + c) * NXL, NXL), :] = displacement[c, :, NYL - 1, :]
        to_low[pl.ds(8 * NXL, NXL), :] = passive[:, 0, :].astype(jnp.float32)
        to_high[pl.ds(5 * NXL, NXL), :] = passive[:, NYL - 1, :].astype(jnp.float32)
        to_high[pl.ds(6 * NXL, 3 * NXL), :] = jnp.zeros((3 * NXL, NZ), jnp.float32)

    odd = is_odd("gy")
    pl.when(odd)(lambda: fill(send_b, send_a))
    pl.when(jnp.logical_not(odd))(lambda: fill(send_a, send_b))


def pack_x(
    density, displacement, passive, received_a, received_b, after, y_high, y_low, send_a, send_b
):
    del after
    odd = is_odd("gy")
    y_high[...] = jnp.where(odd, received_a[...], received_b[...])
    low = pl.ds(0, 6 * NXL)
    y_low[...] = jnp.where(odd, received_b[low, :], received_a[low, :])

    def fill(to_low, to_high):
        for k in (0, 1):
            to_low[pl.ds(8 * k, 8), :] = density[k]
            to_high[pl.ds(8 * k, 8), :] = density[NXL - 2 + k]
        for c in range(3):
            for k in (0, 1):
                to_low[pl.ds(8 * (2 + 2 * c + k), 8), :] = displacement[c, k]
            to_high[pl.ds(8 * (2 + c), 8), :] = displacement[c, NXL - 1]
        to_low[pl.ds(64, 8), :] = passive[0].astype(jnp.float32)
        to_high[pl.ds(40, 8), :] = passive[NXL - 1].astype(jnp.float32)
        for base, first, out in ((72, 0, to_low), (48, NXL - 2, to_high)):
            for kind in range(9):
                out[pl.ds(base + 2 * kind, 2), :] = y_high[pl.ds(NXL * kind + first, 2), :]
            for kind in range(6):
                out[pl.ds(base + 18 + 2 * kind, 2), :] = y_low[pl.ds(NXL * kind + first, 2), :]
            out[pl.ds(base + 30, 2), :] = jnp.zeros((2, NZ), jnp.float32)
        to_high[pl.ds(80, 24), :] = jnp.zeros((24, NZ), jnp.float32)

    odd_x = is_odd("gx")
    pl.when(odd_x)(lambda: fill(send_b, send_a))
    pl.when(jnp.logical_not(odd_x))(lambda: fill(send_a, send_b))


def lane_ends(height):
    lane = lax.broadcasted_iota(jnp.int32, (height, NZ), 1)
    return lane == 0, lane == NZ - 1


def z_sum(f, first, last):
    return jnp.where(first, 0.0, pltpu.roll(f, 1, 1)) + jnp.where(
        last, 0.0, pltpu.roll(f, NZ - 1, 1)
    )


def filter_terms(low, mid, high, first, last):
    across = z_sum(mid, first, last)
    along = low + high
    both = across + along
    side = 0.5 * mid + EDGE_WEIGHT * both
    rest = 1.5 * mid + 0.5 * both + EDGE_WEIGHT * z_sum(along, first, last)
    return side, rest


def corner_sums(here, above, last):
    total = here + above
    slope = above - here
    total_next = jnp.where(last, 0.0, pltpu.roll(total, NZ - 1, 1))
    slope_next = jnp.where(last, 0.0, pltpu.roll(slope, NZ - 1, 1))
    return (total + total_next, total_next - total, slope + slope_next, slope_next - slope)


def element_energy(before, after):
    modes = []
    for c in range(3):
        for k in range(4):
            low, high = before[4 * c + k], after[4 * c + k]
            modes.append((low + high, high - low))
    u, v, w = (
        {(a, k // 2, k % 2): modes[4 * c + k][a] for a in (0, 1) for k in range(4)}
        for c in range(3)
    )

    def sq(x):
        return x * x

    trace = sq(u[1, 0, 0] + v[0, 1, 0] + w[0, 0, 1]) + (1.0 / 3.0) * (
        sq(v[1, 1, 0] + w[1, 0, 1]) + sq(u[1, 1, 0] + w[0, 1, 1]) + sq(u[1, 0, 1] + v[0, 1, 1])
    )
    normal = sq(u[1, 0, 0]) + sq(v[0, 1, 0]) + sq(w[0, 0, 1])
    linear = (
        sq(v[1, 1, 0])
        + sq(w[1, 0, 1])
        + sq(u[1, 1, 0])
        + sq(w[0, 1, 1])
        + sq(u[1, 0, 1])
        + sq(v[0, 1, 1])
    )
    bilinear = sq(u[1, 1, 1]) + sq(v[1, 1, 1]) + sq(w[1, 1, 1])
    shear = (
        sq(u[0, 1, 0] + v[1, 0, 0]) + sq(u[0, 0, 1] + w[1, 0, 0]) + sq(v[0, 0, 1] + w[0, 1, 0])
    )
    twist = (
        sq(u[0, 1, 1] + v[1, 0, 1]) + sq(u[0, 1, 1] + w[1, 1, 0]) + sq(v[1, 0, 1] + w[1, 1, 0])
    )
    return (
        (LAME / 16.0) * trace
        + (SHEAR / 8.0) * normal
        + (SHEAR / 16.0) * (linear + shear)
        + ((LAME + 4.0 * SHEAR) / 144.0) * bilinear
        + (SHEAR / 48.0) * twist
    )


def interior_energy(displacement, energy, inverse, weights, factors):
    start_y = lax.axis_index("gy") * NYL
    total_y = lax.axis_size("gy") * NYL
    first, last = lane_ends(NYL)

    def nodes(plane):
        here = []
        for c in range(3):
            f = displacement[c, plane]
            here.extend(corner_sums(f, pltpu.roll(f, NYL - 1, 0), last))
        return tuple(here)

    def plane_energy(x, before):
        after = nodes(x + 1)
        energy[x] = element_energy(before, after)
        return after

    lax.fori_loop(0, NXL - 1, plane_energy, nodes(0))
    energy[NXL - 1] = jnp.zeros((NYL, NZ), jnp.float32)
    trial = lax.broadcasted_iota(jnp.int32, (SLOTS, NZ), 0).astype(jnp.float32)
    factors[...] = jnp.exp(-0.5 * (-BRACKET + STEP * (trial + 1.0)))

    along_z = jnp.where(first | last, 1.0, 2.0)
    for v in (0, 1):
        index_y = start_y - 1 + 8 * v + lax.broadcasted_iota(jnp.int32, (8, NZ), 0)
        inside = (index_y >= 0) & (index_y < total_y)
        along_y = jnp.where((index_y == 0) | (index_y == total_y - 1), 1.0, 2.0)
        base = 1.5 + 0.5 * (along_y + along_z) + EDGE_WEIGHT * along_y * along_z
        slope = 0.5 + EDGE_WEIGHT * (along_y + along_z)
        for slot, along_x in ((0, 2.0), (1, 1.0)):
            inverse[slot, pl.ds(8 * v, 8), :] = jnp.where(
                inside, 1.0 / (base + along_x * slope), 0.0
            )
    for slot in (0, 1):
        side, rest = filter_terms(
            inverse[slot, pl.ds(0, 8), :],
            inverse[slot, pl.ds(1, 8), :],
            inverse[slot, pl.ds(2, 8), :],
            first,
            last,
        )
        weights[2 * slot] = side
        weights[2 * slot + 1] = rest


def spread_of(filtered, weight, kind, energy):
    physical = filtered * weight
    physical = jnp.where(kind == 1.0, 1.0, jnp.where(kind == 2.0, 0.0, physical))
    return -DERIVATIVE * physical * physical * energy * weight


def around(ref, plane, first, last):
    return filter_terms(
        ref[plane, pl.ds(7, 8), :],
        ref[plane, pl.ds(8, 8), :],
        ref[plane, pl.ds(9, 8), :],
        first,
        last,
    )


def add_volumes(planes, factors, scaled, lower, upper, start, partial):
    def volume_group(g, carry):
        base = pl.multiple_of(8 * GROUP * g, 8 * GROUP)
        scales = [
            jnp.broadcast_to(factors[pl.ds(GROUP * g + k, 1), :], (8, NZ)) for k in range(GROUP)
        ]
        if start is None:
            totals = [jnp.zeros((8, NZ), jnp.float32) for _ in range(GROUP)]
        else:
            totals = [start[pl.ds(base + 8 * k, 8), :] for k in range(GROUP)]
        for place, x in planes:
            values, floor, ceiling = scaled[place], lower[x], upper[x]
            for k in range(GROUP):
                totals[k] += jnp.minimum(jnp.maximum(values * scales[k], floor), ceiling)
        for k in range(GROUP):
            partial[pl.ds(base + 8 * k, 8), :] = totals[k]
        return carry

    lax.fori_loop(0, SLOTS // GROUP, volume_group, 0)


def middle(
    factors,
    density,
    passive,
    own_energy,
    inverse,
    weights,
    y_high,
    y_low,
    sent_a,
    sent_b,
    spread,
    sensitivity,
    scaled,
    lower,
    upper,
    partial,
    dens,
    energy,
):
    def rows(ref, kind):
        return ref[pl.ds(kind * NXL, NXL), :]

    odd = is_odd("gy")

    def sent_low(kind):
        return jnp.where(odd, rows(sent_b, kind), rows(sent_a, kind))

    def sent_high(kind):
        return jnp.where(odd, rows(sent_a, kind), rows(sent_b, kind))

    first, last = lane_ends(NXL)

    def row_nodes(ref, step, at):
        return [rows(ref, at + step * c) for c in range(3)]

    def row_energy(here, above):
        before, after = [], []
        for c in range(3):
            sums = corner_sums(here[c], above[c], last)
            before.extend(sums)
            after.extend(pltpu.roll(f, NXL - 1, 0) for f in sums)
        return element_energy(before, after)

    nodes_8 = row_nodes(y_high, 2, 2)
    energy_low = row_energy(row_nodes(y_low, 1, 2), [sent_low(2 + 2 * c) for c in range(3)])
    energy_7 = row_energy([sent_high(2 + c) for c in range(3)], nodes_8)
    energy_high = row_energy(nodes_8, row_nodes(y_high, 2, 3))

    dens[:, pl.ds(8, NYL), :] = density[...]
    dens[:, 7, :] = rows(y_low, 1)
    dens[:, 16, :] = rows(y_high, 0)
    energy[...] = own_energy[...]
    energy[:, 7, :] = energy_7

    for row, low, mid, high, kind, row_energies in (
        (0, rows(y_low, 0), rows(y_low, 1), sent_low(0), rows(y_low, 5), energy_low),
        (9, sent_high(1), rows(y_high, 0), rows(y_high, 1), rows(y_high, 8), energy_high),
    ):
        side, rest = filter_terms(low, mid, high, first, last)
        filtered = rest + pltpu.roll(side, 1, 0) + pltpu.roll(side, NXL - 1, 0)
        weight = jnp.broadcast_to(inverse[0, pl.ds(row, 1), :], (NXL, NZ))
        spread[:, row + 7, :] = spread_of(filtered, weight, kind, row_energies)

    first, last = lane_ends(NYL)
    weight = inverse[0, pl.ds(1, 8), :]

    def spread_plane(x, carry):
        side_before, side_here, rest_here = carry
        side_after, rest_after = around(dens, x + 1, first, last)
        spread[x, pl.ds(8, 8), :] = spread_of(
            rest_here + side_before + side_after,
            weight,
            passive[x].astype(jnp.float32),
            energy[x],
        )
        return side_here, side_after, rest_after

    side_0, _ = around(dens, 0, first, last)
    lax.fori_loop(
        1, NXL - 1, spread_plane, (side_0,) + around(dens, 1, first, last), unroll=2
    )

    scale = 1.0 / (weights[1] + 2.0 * weights[0])

    def out_plane(x, carry):
        side_before, side_here, rest_here = carry
        side_after, rest_after = around(spread, x + 1, first, last)
        sens = rest_here + side_before + side_after
        sensitivity[x] = sens
        scaled[x] = density[x] * jnp.sqrt(-sens * scale)
        return side_here, side_after, rest_after

    side_1, _ = around(spread, 1, first, last)
    lax.fori_loop(
        2, NXL - 2, out_plane, (side_1,) + around(spread, 2, first, last), unroll=2
    )

    here = density[...]
    kind = passive[...]
    fixed = jnp.where(kind == 1, 1.0, 0.0)
    lower[...] = jnp.where(kind == 0, jnp.maximum(here - MOVE_LIMIT, 0.0), fixed)
    upper[...] = jnp.where(kind == 0, jnp.minimum(here + MOVE_LIMIT, 1.0), fixed)
    add_volumes(
        [(x, x) for x in range(2, NXL - 2)], factors, scaled, lower, upper, None, partial
    )


def edges(
    factors,
    density,
    displacement,
    passive,
    y_high,
    y_low,
    received_a,
    received_b,
    inverse,
    weights,
    spread,
    inner_sensitivity,
    lower,
    upper,
    start,
    sensitivity,
    scaled,
    sums_out,
    dens,
    disp,
    kind_of,
    rim,
    partial,
    x_high,
    x_low,
    *,
    copies,
):
    odd = is_odd("gx")
    x_high[...] = jnp.where(odd, received_a[...], received_b[...])
    x_low[...] = jnp.where(odd, received_b[...], received_a[...])
    first, last = lane_ends(NYL)
    at_end = (
        lax.axis_index("gx") == 0,
        lax.axis_index("gx") == lax.axis_size("gx") - 1,
    )
    for side, (own, far, slabs, low_rows, pick) in enumerate(
        ((0, x_low, 48, 66, 1), (NXL - 2, x_high, 72, 90, 0))
    ):
        for k in (0, 1):
            own_at, far_at = (2 + k, k) if side == 0 else (k, 2 + k)
            dens[side, own_at, pl.ds(2, NYL), :] = density[own + k]
            dens[side, far_at, pl.ds(2, NYL), :] = far[pl.ds(8 * k, 8), :]
            for row in (0, 1):
                dens[side, own_at, pl.ds(NYL + 2 + row, 1), :] = y_high[
                    pl.ds(row * NXL + own + k, 1), :
                ]
                dens[side, own_at, pl.ds(row, 1), :] = y_low[pl.ds(row * NXL + own + k, 1), :]
                dens[side, far_at, pl.ds(NYL + 2 + row, 1), :] = far[
                    pl.ds(slabs + 2 * row + k, 1), :
                ]
                dens[side, far_at, pl.ds(row, 1), :] = far[pl.ds(low_rows + 2 * row + k, 1), :]
        for c in range(3):
            mine = ((1, 0), (2, 1)) if side == 0 else ((0, NXL - 1),)
            theirs = ((0, 2 + c, 1),) if side == 0 else ((1, 2 + 2 * c, 0), (2, 3 + 2 * c, 1))
            for at, x in mine:
                disp[side, c, at, pl.ds(1, NYL), :] = displacement[c, x]
                disp[side, c, at, pl.ds(0, 1), :] = y_low[pl.ds((2 + c) * NXL + x, 1), :]
                for row in (0, 1):
                    disp[side, c, at, pl.ds(NYL + 1 + row, 1), :] = y_high[
                        pl.ds((2 + 2 * c + row) * NXL + x, 1), :
                    ]
            for at, slab, k in theirs:
                disp[side, c, at, pl.ds(1, NYL), :] = far[pl.ds(8 * slab, 8), :]
                disp[side, c, at, pl.ds(0, 1), :] = far[pl.ds(low_rows + 2 * (2 + c) + k, 1), :]
                for row in (0, 1):
                    disp[side, c, at, pl.ds(NYL + 1 + row, 1), :] = far[
                        pl.ds(slabs + 2 * (2 + 2 * c + row) + k, 1), :
                    ]
        own_at, far_at, x = (1, 0, 0) if side == 0 else (0, 1, NXL - 1)
        kind_of[side, own_at, pl.ds(1, NYL), :] = passive[x].astype(jnp.float32)
        kind_of[side, own_at, pl.ds(0, 1), :] = y_low[pl.ds(5 * NXL + x, 1), :]
        kind_of[side, own_at, pl.ds(NYL + 1, 1), :] = y_high[pl.ds(8 * NXL + x, 1), :]
        kind_of[side, far_at, pl.ds(1, NYL), :] = far[pl.ds(40 if side == 0 else 64, 8), :]
        kind_of[side, far_at, pl.ds(0, 1), :] = far[pl.ds(low_rows + 10 + pick, 1), :]
        kind_of[side, far_at, pl.ds(NYL + 1, 1), :] = far[pl.ds(slabs + 16 + pick, 1), :]

        for v in (0, 1):
            rows = pl.ds(8 * v, 8)
            terms = [
                filter_terms(
                    dens[side, p, rows, :],
                    dens[side, p, pl.ds(8 * v + 1, 8), :],
                    dens[side, p, pl.ds(8 * v + 2, 8), :],
                    first,
                    last,
                )
                for p in range(4)
            ]
            nodes = []
            for p in range(3):
                sums = []
                for c in range(3):
                    sums.extend(
                        corner_sums(
                            disp[side, c, p, rows, :],
                            disp[side, c, p, pl.ds(8 * v + 1, 8), :],
                            last,
                        )
                    )
                nodes.append(sums)
            inner = inverse[0, rows, :]
            by_place = (
                jnp.where(at_end[side], 0.0, inner),
                jnp.where(at_end[side], inverse[1, rows, :], inner),
            )
            for k in (0, 1):
                weight = by_place[k] if side == 0 else by_place[1 - k]
                rim[side, (k if side == 0 else 2 + k), pl.ds(7 + 8 * v, 8), :] = spread_of(
                    terms[k + 1][1] + terms[k][0] + terms[k + 2][0],
                    weight,
                    kind_of[side, k, rows, :],
                    element_energy(nodes[k], nodes[k + 1]),
                )
        for k in (0, 1):
            rim[side, (2 + k if side == 0 else k), :, :] = spread[1 + k if side == 0 else 13 + k]

    inner_planes = pl.ds(2, NXL - 4)
    sensitivity[inner_planes] = inner_sensitivity[inner_planes]
    side_inner, rest_inner, side_edge, rest_edge = (weights[i] for i in range(4))
    for side in (0, 1):
        outer_side = jnp.where(at_end[side], 0.0, side_inner)
        next_side = jnp.where(at_end[side], side_edge, side_inner)
        outer = jnp.where(at_end[side], rest_edge, rest_inner) + outer_side + side_inner
        inner = rest_inner + next_side + side_inner
        terms = [around(rim.at[side], p, first, last) for p in range(4)]
        for k in (0, 1):
            x = k if side == 0 else NXL - 2 + k
            sens = terms[k + 1][1] + terms[k][0] + terms[k + 2][0]
            weight = outer if k == side else inner
            sensitivity[x] = sens
            scaled[2 * side + k] = density[x] * jnp.sqrt(-sens / weight)

    add_volumes(
        [(0, 0), (1, 1), (2, NXL - 2), (3, NXL - 1)],
        factors,
        scaled,
        lower,
        upper,
        start,
        partial,
    )
    rows_of = [partial[pl.ds(s, SLOTS, stride=8), :] for s in range(8)]
    lines = ((rows_of[0] + rows_of[1]) + (rows_of[2] + rows_of[3])) + (
        (rows_of[4] + rows_of[5]) + (rows_of[6] + rows_of[7])
    )
    volumes = lax.dot_general(
        jnp.ones((8, NZ), jnp.float32),
        lines,
        (((1,), (1,)), ((), ())),
        precision=lax.Precision.HIGHEST,
        preferred_element_type=jnp.float32,
    )
    second = lax.broadcasted_iota(jnp.int32, (8, NZ), 0) > 0
    pair = jnp.where(second, volumes[:, NZ:], volumes[:, :NZ])[0:2]
    for copy in range(copies):
        sums_out[copy] = pair


def add_copies(received, out, *, copies):
    total = jnp.sum(received[...], axis=0)
    for copy in range(copies):
        out[copy] = total


def finish(received, scaled, scaled_edge, lower, upper, new_density, *, target):
    volumes = jnp.sum(received[...], axis=0)
    slot = lax.broadcasted_iota(jnp.int32, (2, NZ), 0) * NZ + lax.broadcasted_iota(
        jnp.int32, (2, NZ), 1
    )
    above = jnp.sum(jnp.where((volumes > target) & (slot < TRIALS), 1.0, 0.0))
    middle_end = -BRACKET + STEP * above + 0.5 * STEP
    factor = jnp.exp(jnp.full((8, NZ), -0.5, jnp.float32) * middle_end)[None]
    inner = pl.ds(2, NXL - 4)
    for ref, place, planes in (
        (scaled, inner, inner),
        (scaled_edge, pl.ds(0, 2), pl.ds(0, 2)),
        (scaled_edge, pl.ds(2, 2), pl.ds(NXL - 2, 2)),
    ):
        new_density[planes] = jnp.minimum(
            jnp.maximum(ref[place] * factor, lower[planes]), upper[planes]
        )


def f32(*shape):
    return jax.ShapeDtypeStruct(shape, jnp.float32)


def near(*shape, dtype=jnp.float32):
    return pltpu.VMEM(shape, dtype)


def far(array):
    return pltpu.with_memory_space_constraint(array, pltpu.HBM)


def held(array):
    return pltpu.with_memory_space_constraint(array, pltpu.VMEM)


def call(kernel, outputs, inputs, scratch=(), specs=None, cost=0):
    return pl.pallas_call(
        kernel,
        out_shape=outputs,
        in_specs=specs or [VMEM] * len(inputs),
        out_specs=jax.tree.map(lambda _: VMEM, outputs),
        scratch_shapes=list(scratch),
        cost_estimate=pl.CostEstimate(
            flops=cost * 4000, bytes_accessed=cost * 1000, transcendentals=0
        ),
        compiler_params=pltpu.CompilerParams(vmem_limit_bytes=16 << 20),
    )(*inputs)


def swapped(block, axis, start):
    pairs = [(i, i + 1) for i in range(start, lax.axis_size(axis) - 1, 2)]
    return lax.ppermute(block, axis, pairs + [(j, i) for i, j in pairs])


def reduction_groups(count_x, count_y):
    across, along = {}, {}
    for gx in range(count_x):
        for gy in range(count_y):
            device = gx * count_y + gy
            across.setdefault((gx // 2, gy // SIDE), []).append(device)
            along.setdefault((gx % 2, gy % SIDE), []).append(device)
    return list(across.values()), list(along.values())


def per_device(density, displacement, passive):
    count_x, count_y = lax.axis_size("gx"), lax.axis_size("gy")
    assert density.shape == (NXL, NYL, NZ)
    block = (NXL, NYL, NZ)
    density, displacement, passive, sent_a, sent_b = call(
        pack_y,
        (
            near(*block),
            near(3, *block),
            near(*block, dtype=jnp.int32),
            near(9 * NXL, NZ),
            near(9 * NXL, NZ),
        ),
        (far(density), far(displacement), far(passive)),
        [pltpu.SemaphoreType.DMA((3,))],
        specs=[pl.BlockSpec(memory_space=pltpu.HBM)] * 3,
        cost=1000,
    )
    received_a = held(swapped(sent_a, "gy", 1))
    received_b = held(swapped(sent_b, "gy", 0))
    own_energy, inverse, weights, factors = call(
        interior_energy,
        (near(*block), near(2, 16, NZ), near(4, NYL, NZ), near(SLOTS, NZ)),
        (displacement,),
        cost=1000,
    )
    y_high, y_low, to_a, to_b = call(
        pack_x,
        (near(9 * NXL, NZ), near(6 * NXL, NZ), near(104, NZ), near(104, NZ)),
        (density, displacement, passive, received_a, received_b, weights),
        cost=500,
    )
    received_a = held(swapped(to_a, "gx", 1))
    received_b = held(swapped(to_b, "gx", 0))
    spread, sensitivity, scaled, lower, upper, partial = call(
        middle,
        (near(NXL, 24, NZ),) + (near(*block),) * 4 + (near(8 * SLOTS, NZ),),
        (
            factors,
            density,
            passive,
            own_energy,
            inverse,
            weights,
            y_high,
            y_low,
            sent_a,
            sent_b,
        ),
        [pltpu.VMEM((NXL, 24, NZ), jnp.float32), pltpu.VMEM(block, jnp.float32)],
        cost=5000,
    )
    first_group, second_group = 2 * SIDE, count_x * count_y // (2 * SIDE)
    sensitivity, scaled_edge, volumes = call(
        functools.partial(edges, copies=first_group),
        (near(*block), near(4, NYL, NZ), near(first_group, 2, NZ)),
        (
            factors,
            density,
            displacement,
            passive,
            y_high,
            y_low,
            received_a,
            received_b,
            inverse,
            weights,
            spread,
            sensitivity,
            lower,
            upper,
            partial,
        ),
        [
            pltpu.VMEM((2, 4, 24, NZ), jnp.float32),
            pltpu.VMEM((2, 3, 3, 24, NZ), jnp.float32),
            pltpu.VMEM((2, 2, 16, NZ), jnp.float32),
            pltpu.VMEM((2, 4, 24, NZ), jnp.float32),
            pltpu.VMEM((8 * SLOTS, NZ), jnp.float32),
            pltpu.VMEM((104, NZ), jnp.float32),
            pltpu.VMEM((104, NZ), jnp.float32),
        ],
        cost=3000,
    )

    across, along = reduction_groups(count_x, count_y)
    volumes = lax.all_to_all(volumes, ("gx", "gy"), 0, 0, axis_index_groups=across)
    volumes = call(
        functools.partial(add_copies, copies=second_group),
        near(second_group, 2, NZ),
        (held(volumes),),
        cost=300,
    )
    volumes = lax.all_to_all(volumes, ("gx", "gy"), 0, 0, axis_index_groups=along)
    target = VOLUME_SHARE * (count_x * NXL) * (count_y * NYL) * NZ
    new_density = call(
        functools.partial(finish, target=target),
        f32(*block),
        (held(volumes), scaled, scaled_edge, lower, upper),
        cost=500,
    )
    return new_density, sensitivity


def solution(mesh):
    return jax.shard_map(
        per_device,
        mesh=mesh,
        in_specs=(P("gx", "gy", None), P(None, "gx", "gy", None), P("gx", "gy", None)),
        out_specs=(P("gx", "gy", None), P("gx", "gy", None)),
        check_vma=False,
    )
```

```python
import functools
import math

import jax
import jax.numpy as jnp
from jax import lax
from jax.experimental import pallas as pl
from jax.experimental.pallas import tpu as pltpu
from jax.sharding import PartitionSpec as P

BISECT = 8
BRACKET = 8.0
MOVE_LIMIT = 0.2
VOLUME_SHARE = 0.35
DERIVATIVE = 3.0 * (1.0 - 1e-09)
EDGE_WEIGHT = 1.5 - math.sqrt(2.0)
POISSON = 0.3
LAME = POISSON / ((1.0 + POISSON) * (1.0 - 2.0 * POISSON))
SHEAR = 0.5 / (1.0 + POISSON)

NXL = 16
NYL = 8
NZ = 128
TRIALS = 2 ** BISECT - 1
SLOTS = TRIALS + 1
STEP = 2.0 * BRACKET / 2 ** BISECT
GROUP = 16
SIDE = 4

VMEM = pl.BlockSpec(memory_space=pltpu.VMEM)


def is_odd(axis):
    return lax.rem(lax.axis_index(axis), 2) == 1


def pack_y(
    density_far, displacement_far, passive_far, density, displacement, passive, send_a, send_b, sems
):
    copies = [
        pltpu.make_async_copy(far, local, sems.at[i])
        for i, (far, local) in enumerate(
            (
                (density_far, density),
                (displacement_far, displacement),
                (passive_far, passive),
            )
        )
    ]
    for copy in copies:
        copy.start()
    for copy in copies:
        copy.wait()

    def fill(to_low, to_high):
        for row in (0, 1):
            to_low[pl.ds(row * NXL, NXL), :] = density[:, row, :]
            to_high[pl.ds(row * NXL, NXL), :] = density[:, NYL - 2 + row, :]
        for c in range(3):
            for row in (0, 1):
                to_low[pl.ds((2 + 2 * c + row) * NXL, NXL), :] = displacement[c, :, row, :]
            to_high[pl.ds((2 + c) * NXL, NXL), :] = displacement[c, :, NYL - 1, :]
        to_low[pl.ds(8 * NXL, NXL), :] = passive[:, 0, :].astype(jnp.float32)
        to_high[pl.ds(5 * NXL, NXL), :] = passive[:, NYL - 1, :].astype(jnp.float32)
        to_high[pl.ds(6 * NXL, 3 * NXL), :] = jnp.zeros((3 * NXL, NZ), jnp.float32)

    odd = is_odd("gy")
    pl.when(odd)(lambda: fill(send_b, send_a))
    pl.when(jnp.logical_not(odd))(lambda: fill(send_a, send_b))


def pack_x(
    density, displacement, passive, received_a, received_b, after, y_high, y_low, send_a, send_b
):
    del after
    odd = is_odd("gy")
    y_high[...] = jnp.where(odd, received_a[...], received_b[...])
    low = pl.ds(0, 6 * NXL)
    y_low[...] = jnp.where(odd, received_b[low, :], received_a[low, :])

    def fill(to_low, to_high):
        for k in (0, 1):
            to_low[pl.ds(8 * k, 8), :] = density[k]
            to_high[pl.ds(8 * k, 8), :] = density[NXL - 2 + k]
        for c in range(3):
            for k in (0, 1):
                to_low[pl.ds(8 * (2 + 2 * c + k), 8), :] = displacement[c, k]
            to_high[pl.ds(8 * (2 + c), 8), :] = displacement[c, NXL - 1]
        to_low[pl.ds(64, 8), :] = passive[0].astype(jnp.float32)
        to_high[pl.ds(40, 8), :] = passive[NXL - 1].astype(jnp.float32)
        for base, first, out in ((72, 0, to_low), (48, NXL - 2, to_high)):
            for kind in range(9):
                out[pl.ds(base + 2 * kind, 2), :] = y_high[pl.ds(NXL * kind + first, 2), :]
            for kind in range(6):
                out[pl.ds(base + 18 + 2 * kind, 2), :] = y_low[pl.ds(NXL * kind + first, 2), :]
            out[pl.ds(base + 30, 2), :] = jnp.zeros((2, NZ), jnp.float32)
        to_high[pl.ds(80, 24), :] = jnp.zeros((24, NZ), jnp.float32)

    odd_x = is_odd("gx")
    pl.when(odd_x)(lambda: fill(send_b, send_a))
    pl.when(jnp.logical_not(odd_x))(lambda: fill(send_a, send_b))


def lane_ends(height):
    lane = lax.broadcasted_iota(jnp.int32, (height, NZ), 1)
    return lane == 0, lane == NZ - 1


def z_sum(f, first, last):
    return jnp.where(first, 0.0, pltpu.roll(f, 1, 1)) + jnp.where(
        last, 0.0, pltpu.roll(f, NZ - 1, 1)
    )


def filter_terms(low, mid, high, first, last):
    across = z_sum(mid, first, last)
    along = low + high
    both = across + along
    side = 0.5 * mid + EDGE_WEIGHT * both
    rest = 1.5 * mid + 0.5 * both + EDGE_WEIGHT * z_sum(along, first, last)
    return side, rest


def corner_sums(here, above, last):
    total = here + above
    slope = above - here
    total_next = jnp.where(last, 0.0, pltpu.roll(total, NZ - 1, 1))
    slope_next = jnp.where(last, 0.0, pltpu.roll(slope, NZ - 1, 1))
    return (total + total_next, total_next - total, slope + slope_next, slope_next - slope)


def element_energy(before, after):
    modes = []
    for c in range(3):
        for k in range(4):
            low, high = before[4 * c + k], after[4 * c + k]
            modes.append((low + high, high - low))
    u, v, w = (
        {(a, k // 2, k % 2): modes[4 * c + k][a] for a in (0, 1) for k in range(4)}
        for c in range(3)
    )

    def sq(x):
        return x * x

    trace = sq(u[1, 0, 0] + v[0, 1, 0] + w[0, 0, 1]) + (1.0 / 3.0) * (
        sq(v[1, 1, 0] + w[1, 0, 1]) + sq(u[1, 1, 0] + w[0, 1, 1]) + sq(u[1, 0, 1] + v[0, 1, 1])
    )
    normal = sq(u[1, 0, 0]) + sq(v[0, 1, 0]) + sq(w[0, 0, 1])
    linear = (
        sq(v[1, 1, 0])
        + sq(w[1, 0, 1])
        + sq(u[1, 1, 0])
        + sq(w[0, 1, 1])
        + sq(u[1, 0, 1])
        + sq(v[0, 1, 1])
    )
    bilinear = sq(u[1, 1, 1]) + sq(v[1, 1, 1]) + sq(w[1, 1, 1])
    shear = (
        sq(u[0, 1, 0] + v[1, 0, 0]) + sq(u[0, 0, 1] + w[1, 0, 0]) + sq(v[0, 0, 1] + w[0, 1, 0])
    )
    twist = (
        sq(u[0, 1, 1] + v[1, 0, 1]) + sq(u[0, 1, 1] + w[1, 1, 0]) + sq(v[1, 0, 1] + w[1, 1, 0])
    )
    return (
        (LAME / 16.0) * trace
        + (SHEAR / 8.0) * normal
        + (SHEAR / 16.0) * (linear + shear)
        + ((LAME + 4.0 * SHEAR) / 144.0) * bilinear
        + (SHEAR / 48.0) * twist
    )


def interior_energy(displacement, energy, inverse, weights, factors):
    start_y = lax.axis_index("gy") * NYL
    total_y = lax.axis_size("gy") * NYL
    first, last = lane_ends(NYL)

    def nodes(plane):
        here = []
        for c in range(3):
            f = displacement[c, plane]
            here.extend(corner_sums(f, pltpu.roll(f, NYL - 1, 0), last))
        return tuple(here)

    def plane_energy(x, before):
        after = nodes(x + 1)
        energy[x] = element_energy(before, after)
        return after

    lax.fori_loop(0, NXL - 1, plane_energy, nodes(0))
    energy[NXL - 1] = jnp.zeros((NYL, NZ), jnp.float32)
    trial = lax.broadcasted_iota(jnp.int32, (SLOTS, NZ), 0).astype(jnp.float32)
    factors[...] = jnp.exp(-0.5 * (-BRACKET + STEP * (trial + 1.0)))

    along_z = jnp.where(first | last, 1.0, 2.0)
    for v in (0, 1):
        index_y = start_y - 1 + 8 * v + lax.broadcasted_iota(jnp.int32, (8, NZ), 0)
        inside = (index_y >= 0) & (index_y < total_y)
        along_y = jnp.where((index_y == 0) | (index_y == total_y - 1), 1.0, 2.0)
        base = 1.5 + 0.5 * (along_y + along_z) + EDGE_WEIGHT * along_y * along_z
        slope = 0.5 + EDGE_WEIGHT * (along_y + along_z)
        for slot, along_x in ((0, 2.0), (1, 1.0)):
            inverse[slot, pl.ds(8 * v, 8), :] = jnp.where(
                inside, 1.0 / (base + along_x * slope), 0.0
            )
    for slot in (0, 1):
        side, rest = filter_terms(
            inverse[slot, pl.ds(0, 8), :],
            inverse[slot, pl.ds(1, 8), :],
            inverse[slot, pl.ds(2, 8), :],
            first,
            last,
        )
        weights[2 * slot] = side
        weights[2 * slot + 1] = rest


def spread_of(filtered, weight, kind, energy):
    physical = filtered * weight
    physical = jnp.where(kind == 1.0, 1.0, jnp.where(kind == 2.0, 0.0, physical))
    return -DERIVATIVE * physical * physical * energy * weight


def around(ref, plane, first, last):
    return filter_terms(
        ref[plane, pl.ds(7, 8), :],
        ref[plane, pl.ds(8, 8), :],
        ref[plane, pl.ds(9, 8), :],
        first,
        last,
    )


def add_volumes(planes, factors, scaled, lower, upper, start, partial):
    def volume_group(g, carry):
        base = pl.multiple_of(8 * GROUP * g, 8 * GROUP)
        scales = [
            jnp.broadcast_to(factors[pl.ds(GROUP * g + k, 1), :], (8, NZ)) for k in range(GROUP)
        ]
        if start is None:
            totals = [jnp.zeros((8, NZ), jnp.float32) for _ in range(GROUP)]
        else:
            totals = [start[pl.ds(base + 8 * k, 8), :] for k in range(GROUP)]
        for place, x in planes:
            values, floor, ceiling = scaled[place], lower[x], upper[x]
            for k in range(GROUP):
                totals[k] += jnp.minimum(jnp.maximum(values * scales[k], floor), ceiling)
        for k in range(GROUP):
            partial[pl.ds(base + 8 * k, 8), :] = totals[k]
        return carry

    lax.fori_loop(0, SLOTS // GROUP, volume_group, 0)


def middle(
    factors,
    density,
    passive,
    own_energy,
    inverse,
    weights,
    y_high,
    y_low,
    sent_a,
    sent_b,
    spread,
    sensitivity,
    scaled,
    lower,
    upper,
    partial,
    dens,
    energy,
):
    def rows(ref, kind):
        return ref[pl.ds(kind * NXL, NXL), :]

    odd = is_odd("gy")

    def sent_low(kind):
        return jnp.where(odd, rows(sent_b, kind), rows(sent_a, kind))

    def sent_high(kind):
        return jnp.where(odd, rows(sent_a, kind), rows(sent_b, kind))

    first, last = lane_ends(NXL)

    def row_nodes(ref, step, at):
        return [rows(ref, at + step * c) for c in range(3)]

    def row_energy(here, above):
        before, after = [], []
        for c in range(3):
            sums = corner_sums(here[c], above[c], last)
            before.extend(sums)
            after.extend(pltpu.roll(f, NXL - 1, 0) for f in sums)
        return element_energy(before, after)

    nodes_8 = row_nodes(y_high, 2, 2)
    energy_low = row_energy(row_nodes(y_low, 1, 2), [sent_low(2 + 2 * c) for c in range(3)])
    energy_7 = row_energy([sent_high(2 + c) for c in range(3)], nodes_8)
    energy_high = row_energy(nodes_8, row_nodes(y_high, 2, 3))

    dens[:, pl.ds(8, NYL), :] = density[...]
    dens[:, 7, :] = rows(y_low, 1)
    dens[:, 16, :] = rows(y_high, 0)
    energy[...] = own_energy[...]
    energy[:, 7, :] = energy_7

    for row, low, mid, high, kind, row_energies in (
        (0, rows(y_low, 0), rows(y_low, 1), sent_low(0), rows(y_low, 5), energy_low),
        (9, sent_high(1), rows(y_high, 0), rows(y_high, 1), rows(y_high, 8), energy_high),
    ):
        side, rest = filter_terms(low, mid, high, first, last)
        filtered = rest + pltpu.roll(side, 1, 0) + pltpu.roll(side, NXL - 1, 0)
        weight = jnp.broadcast_to(inverse[0, pl.ds(row, 1), :], (NXL, NZ))
        spread[:, row + 7, :] = spread_of(filtered, weight, kind, row_energies)

    first, last = lane_ends(NYL)
    weight = inverse[0, pl.ds(1, 8), :]

    def spread_plane(x, carry):
        side_before, side_here, rest_here = carry
        side_after, rest_after = around(dens, x + 1, first, last)
        spread[x, pl.ds(8, 8), :] = spread_of(
            rest_here + side_before + side_after,
            weight,
            passive[x].astype(jnp.float32),
            energy[x],
        )
        return side_here, side_after, rest_after

    side_0, _ = around(dens, 0, first, last)
    lax.fori_loop(
        1, NXL - 1, spread_plane, (side_0,) + around(dens, 1, first, last), unroll=2
    )

    scale = 1.0 / (weights[1] + 2.0 * weights[0])

    def out_plane(x, carry):
        side_before, side_here, rest_here = carry
        side_after, rest_after = around(spread, x + 1, first, last)
        sens = rest_here + side_before + side_after
        sensitivity[x] = sens
        scaled[x] = density[x] * jnp.sqrt(-sens * scale)
        return side_here, side_after, rest_after

    side_1, _ = around(spread, 1, first, last)
    lax.fori_loop(
        2, NXL - 2, out_plane, (side_1,) + around(spread, 2, first, last), unroll=2
    )

    here = density[...]
    kind = passive[...]
    fixed = jnp.where(kind == 1, 1.0, 0.0)
    lower[...] = jnp.where(kind == 0, jnp.maximum(here - MOVE_LIMIT, 0.0), fixed)
    upper[...] = jnp.where(kind == 0, jnp.minimum(here + MOVE_LIMIT, 1.0), fixed)
    add_volumes(
        [(x, x) for x in range(2, NXL - 2)], factors, scaled, lower, upper, None, partial
    )


def edges(
    factors,
    density,
    displacement,
    passive,
    y_high,
    y_low,
    received_a,
    received_b,
    inverse,
    weights,
    spread,
    inner_sensitivity,
    lower,
    upper,
    start,
    sensitivity,
    scaled,
    sums_out,
    dens,
    disp,
    kind_of,
    rim,
    partial,
    x_high,
    x_low,
    *,
    copies,
):
    odd = is_odd("gx")
    x_high[...] = jnp.where(odd, received_a[...], received_b[...])
    x_low[...] = jnp.where(odd, received_b[...], received_a[...])
    first, last = lane_ends(NYL)
    at_end = (
        lax.axis_index("gx") == 0,
        lax.axis_index("gx") == lax.axis_size("gx") - 1,
    )
    for side, (own, far, slabs, low_rows, pick) in enumerate(
        ((0, x_low, 48, 66, 1), (NXL - 2, x_high, 72, 90, 0))
    ):
        for k in (0, 1):
            own_at, far_at = (2 + k, k) if side == 0 else (k, 2 + k)
            dens[side, own_at, pl.ds(2, NYL), :] = density[own + k]
            dens[side, far_at, pl.ds(2, NYL), :] = far[pl.ds(8 * k, 8), :]
            for row in (0, 1):
                dens[side, own_at, pl.ds(NYL + 2 + row, 1), :] = y_high[
                    pl.ds(row * NXL + own + k, 1), :
                ]
                dens[side, own_at, pl.ds(row, 1), :] = y_low[pl.ds(row * NXL + own + k, 1), :]
                dens[side, far_at, pl.ds(NYL + 2 + row, 1), :] = far[
                    pl.ds(slabs + 2 * row + k, 1), :
                ]
                dens[side, far_at, pl.ds(row, 1), :] = far[pl.ds(low_rows + 2 * row + k, 1), :]
        for c in range(3):
            mine = ((1, 0), (2, 1)) if side == 0 else ((0, NXL - 1),)
            theirs = ((0, 2 + c, 1),) if side == 0 else ((1, 2 + 2 * c, 0), (2, 3 + 2 * c, 1))
            for at, x in mine:
                disp[side, c, at, pl.ds(1, NYL), :] = displacement[c, x]
                disp[side, c, at, pl.ds(0, 1), :] = y_low[pl.ds((2 + c) * NXL + x, 1), :]
                for row in (0, 1):
                    disp[side, c, at, pl.ds(NYL + 1 + row, 1), :] = y_high[
                        pl.ds((2 + 2 * c + row) * NXL + x, 1), :
                    ]
            for at, slab, k in theirs:
                disp[side, c, at, pl.ds(1, NYL), :] = far[pl.ds(8 * slab, 8), :]
                disp[side, c, at, pl.ds(0, 1), :] = far[pl.ds(low_rows + 2 * (2 + c) + k, 1), :]
                for row in (0, 1):
                    disp[side, c, at, pl.ds(NYL + 1 + row, 1), :] = far[
                        pl.ds(slabs + 2 * (2 + 2 * c + row) + k, 1), :
                    ]
        own_at, far_at, x = (1, 0, 0) if side == 0 else (0, 1, NXL - 1)
        kind_of[side, own_at, pl.ds(1, NYL), :] = passive[x].astype(jnp.float32)
        kind_of[side, own_at, pl.ds(0, 1), :] = y_low[pl.ds(5 * NXL + x, 1), :]
        kind_of[side, own_at, pl.ds(NYL + 1, 1), :] = y_high[pl.ds(8 * NXL + x, 1), :]
        kind_of[side, far_at, pl.ds(1, NYL), :] = far[pl.ds(40 if side == 0 else 64, 8), :]
        kind_of[side, far_at, pl.ds(0, 1), :] = far[pl.ds(low_rows + 10 + pick, 1), :]
        kind_of[side, far_at, pl.ds(NYL + 1, 1), :] = far[pl.ds(slabs + 16 + pick, 1), :]

        for v in (0, 1):
            rows = pl.ds(8 * v, 8)
            terms = [
                filter_terms(
                    dens[side, p, rows, :],
                    dens[side, p, pl.ds(8 * v + 1, 8), :],
                    dens[side, p, pl.ds(8 * v + 2, 8), :],
                    first,
                    last,
                )
                for p in range(4)
            ]
            nodes = []
            for p in range(3):
                sums = []
                for c in range(3):
                    sums.extend(
                        corner_sums(
                            disp[side, c, p, rows, :],
                            disp[side, c, p, pl.ds(8 * v + 1, 8), :],
                            last,
                        )
                    )
                nodes.append(sums)
            inner = inverse[0, rows, :]
            by_place = (
                jnp.where(at_end[side], 0.0, inner),
                jnp.where(at_end[side], inverse[1, rows, :], inner),
            )
            for k in (0, 1):
                weight = by_place[k] if side == 0 else by_place[1 - k]
                rim[side, (k if side == 0 else 2 + k), pl.ds(7 + 8 * v, 8), :] = spread_of(
                    terms[k + 1][1] + terms[k][0] + terms[k + 2][0],
                    weight,
                    kind_of[side, k, rows, :],
                    element_energy(nodes[k], nodes[k + 1]),
                )
        for k in (0, 1):
            rim[side, (2 + k if side == 0 else k), :, :] = spread[1 + k if side == 0 else 13 + k]

    inner_planes = pl.ds(2, NXL - 4)
    sensitivity[inner_planes] = inner_sensitivity[inner_planes]
    side_inner, rest_inner, side_edge, rest_edge = (weights[i] for i in range(4))
    for side in (0, 1):
        outer_side = jnp.where(at_end[side], 0.0, side_inner)
        next_side = jnp.where(at_end[side], side_edge, side_inner)
        outer = jnp.where(at_end[side], rest_edge, rest_inner) + outer_side + side_inner
        inner = rest_inner + next_side + side_inner
        terms = [around(rim.at[side], p, first, last) for p in range(4)]
        for k in (0, 1):
            x = k if side == 0 else NXL - 2 + k
            sens = terms[k + 1][1] + terms[k][0] + terms[k + 2][0]
            weight = outer if k == side else inner
            sensitivity[x] = sens
            scaled[2 * side + k] = density[x] * jnp.sqrt(-sens / weight)

    add_volumes(
        [(0, 0), (1, 1), (2, NXL - 2), (3, NXL - 1)],
        factors,
        scaled,
        lower,
        upper,
        start,
        partial,
    )
    rows_of = [partial[pl.ds(s, SLOTS, stride=8), :] for s in range(8)]
    lines = ((rows_of[0] + rows_of[1]) + (rows_of[2] + rows_of[3])) + (
        (rows_of[4] + rows_of[5]) + (rows_of[6] + rows_of[7])
    )
    volumes = lax.dot_general(
        jnp.ones((8, NZ), jnp.float32),
        lines,
        (((1,), (1,)), ((), ())),
        precision=lax.Precision.HIGHEST,
        preferred_element_type=jnp.float32,
    )
    second = lax.broadcasted_iota(jnp.int32, (8, NZ), 0) > 0
    pair = jnp.where(second, volumes[:, NZ:], volumes[:, :NZ])[0:2]
    for copy in range(copies):
        sums_out[copy] = pair


def add_copies(received, out, *, copies):
    total = jnp.sum(received[...], axis=0)
    for copy in range(copies):
        out[copy] = total


def finish(
    received,
    scaled,
    scaled_edge,
    lower,
    upper,
    sensitivity,
    new_density_far,
    sensitivity_far,
    new_density,
    sems,
    *,
    target,
):
    copies = [
        pltpu.make_async_copy(sensitivity, sensitivity_far, sems.at[0]),
        pltpu.make_async_copy(new_density, new_density_far, sems.at[1]),
    ]
    copies[0].start()
    volumes = jnp.sum(received[...], axis=0)
    slot = lax.broadcasted_iota(jnp.int32, (2, NZ), 0) * NZ + lax.broadcasted_iota(
        jnp.int32, (2, NZ), 1
    )
    above = jnp.sum(jnp.where((volumes > target) & (slot < TRIALS), 1.0, 0.0))
    middle_end = -BRACKET + STEP * above + 0.5 * STEP
    factor = jnp.exp(jnp.full((8, NZ), -0.5, jnp.float32) * middle_end)[None]
    inner = pl.ds(2, NXL - 4)
    for ref, place, planes in (
        (scaled, inner, inner),
        (scaled_edge, pl.ds(0, 2), pl.ds(0, 2)),
        (scaled_edge, pl.ds(2, 2), pl.ds(NXL - 2, 2)),
    ):
        new_density[planes] = jnp.minimum(
            jnp.maximum(ref[place] * factor, lower[planes]), upper[planes]
        )
    copies[1].start()
    for copy in copies:
        copy.wait()


def f32(*shape):
    return jax.ShapeDtypeStruct(shape, jnp.float32)


def near(*shape, dtype=jnp.float32):
    return pltpu.VMEM(shape, dtype)


def far(array):
    return pltpu.with_memory_space_constraint(array, pltpu.HBM)


def held(array):
    return pltpu.with_memory_space_constraint(array, pltpu.VMEM)


def call(kernel, outputs, inputs, scratch=(), specs=None, out_specs=None, cost=0):
    return pl.pallas_call(
        kernel,
        out_shape=outputs,
        in_specs=specs or [VMEM] * len(inputs),
        out_specs=out_specs or jax.tree.map(lambda _: VMEM, outputs),
        scratch_shapes=list(scratch),
        cost_estimate=pl.CostEstimate(
            flops=cost * 4000, bytes_accessed=cost * 1000, transcendentals=0
        ),
        compiler_params=pltpu.CompilerParams(vmem_limit_bytes=16 << 20),
    )(*inputs)


def swapped(block, axis, start):
    pairs = [(i, i + 1) for i in range(start, lax.axis_size(axis) - 1, 2)]
    return lax.ppermute(block, axis, pairs + [(j, i) for i, j in pairs])


def reduction_groups(count_x, count_y):
    chips_x = count_y // SIDE
    across, along = {}, {}
    for gx in range(count_x):
        for gy in range(count_y):
            device = gx * count_y + gy
            x, y = gy // SIDE, gy % SIDE
            across.setdefault((gx // 2, x // 2), []).append(device)
            along.setdefault((gx % 2, y, min(x, chips_x - 1 - x)), []).append(device)
    return list(across.values()), list(along.values())


def per_device(density, displacement, passive):
    count_x, count_y = lax.axis_size("gx"), lax.axis_size("gy")
    assert density.shape == (NXL, NYL, NZ)
    block = (NXL, NYL, NZ)
    density, displacement, passive, sent_a, sent_b = call(
        pack_y,
        (
            near(*block),
            near(3, *block),
            near(*block, dtype=jnp.int32),
            near(9 * NXL, NZ),
            near(9 * NXL, NZ),
        ),
        (far(density), far(displacement), far(passive)),
        [pltpu.SemaphoreType.DMA((3,))],
        specs=[pl.BlockSpec(memory_space=pltpu.HBM)] * 3,
        cost=1000,
    )
    received_a = held(swapped(sent_a, "gy", 1))
    received_b = held(swapped(sent_b, "gy", 0))
    own_energy, inverse, weights, factors = call(
        interior_energy,
        (near(*block), near(2, 16, NZ), near(4, NYL, NZ), near(SLOTS, NZ)),
        (displacement,),
        cost=1000,
    )
    y_high, y_low, to_a, to_b = call(
        pack_x,
        (near(9 * NXL, NZ), near(6 * NXL, NZ), near(104, NZ), near(104, NZ)),
        (density, displacement, passive, received_a, received_b, weights),
        cost=500,
    )
    received_a = held(swapped(to_a, "gx", 1))
    received_b = held(swapped(to_b, "gx", 0))
    spread, sensitivity, scaled, lower, upper, partial = call(
        middle,
        (near(NXL, 24, NZ),) + (near(*block),) * 4 + (near(8 * SLOTS, NZ),),
        (
            factors,
            density,
            passive,
            own_energy,
            inverse,
            weights,
            y_high,
            y_low,
            sent_a,
            sent_b,
        ),
        [pltpu.VMEM((NXL, 24, NZ), jnp.float32), pltpu.VMEM(block, jnp.float32)],
        cost=5000,
    )
    across, along = reduction_groups(count_x, count_y)
    first_group, second_group = len(across[0]), len(along[0])
    sensitivity, scaled_edge, volumes = call(
        functools.partial(edges, copies=first_group),
        (near(*block), near(4, NYL, NZ), near(first_group, 2, NZ)),
        (
            factors,
            density,
            displacement,
            passive,
            y_high,
            y_low,
            received_a,
            received_b,
            inverse,
            weights,
            spread,
            sensitivity,
            lower,
            upper,
            partial,
        ),
        [
            pltpu.VMEM((2, 4, 24, NZ), jnp.float32),
            pltpu.VMEM((2, 3, 3, 24, NZ), jnp.float32),
            pltpu.VMEM((2, 2, 16, NZ), jnp.float32),
            pltpu.VMEM((2, 4, 24, NZ), jnp.float32),
            pltpu.VMEM((8 * SLOTS, NZ), jnp.float32),
            pltpu.VMEM((104, NZ), jnp.float32),
            pltpu.VMEM((104, NZ), jnp.float32),
        ],
        cost=3000,
    )

    volumes = lax.all_to_all(volumes, ("gx", "gy"), 0, 0, axis_index_groups=across)
    volumes = call(
        functools.partial(add_copies, copies=second_group),
        near(second_group, 2, NZ),
        (held(volumes),),
        cost=300,
    )
    volumes = lax.all_to_all(volumes, ("gx", "gy"), 0, 0, axis_index_groups=along)
    target = VOLUME_SHARE * (count_x * NXL) * (count_y * NYL) * NZ
    new_density, sensitivity = call(
        functools.partial(finish, target=target),
        (f32(*block), f32(*block)),
        (held(volumes), scaled, scaled_edge, lower, upper, sensitivity),
        [pltpu.VMEM(block, jnp.float32), pltpu.SemaphoreType.DMA((2,))],
        out_specs=(pl.BlockSpec(memory_space=pltpu.HBM),) * 2,
        cost=500,
    )
    return new_density, sensitivity


def solution(mesh):
    return jax.shard_map(
        per_device,
        mesh=mesh,
        in_specs=(P("gx", "gy", None), P(None, "gx", "gy", None), P("gx", "gy", None)),
        out_specs=(P("gx", "gy", None), P("gx", "gy", None)),
        check_vma=False,
    )
```

```python
import functools
import math

import jax
import jax.numpy as jnp
from jax import lax
from jax.experimental import pallas as pl
from jax.experimental.pallas import tpu as pltpu
from jax.sharding import PartitionSpec as P

BISECT = 8
BRACKET = 8.0
MOVE_LIMIT = 0.2
VOLUME_SHARE = 0.35
DERIVATIVE = 3.0 * (1.0 - 1e-09)
EDGE_WEIGHT = 1.5 - math.sqrt(2.0)
POISSON = 0.3
LAME = POISSON / ((1.0 + POISSON) * (1.0 - 2.0 * POISSON))
SHEAR = 0.5 / (1.0 + POISSON)

NXL = 16
NYL = 8
NZ = 128
TRIALS = 2 ** BISECT - 1
SLOTS = TRIALS + 1
STEP = 2.0 * BRACKET / 2 ** BISECT
GROUP = 16
SIDE = 4

VMEM = pl.BlockSpec(memory_space=pltpu.VMEM)


def is_odd(axis):
    return lax.rem(lax.axis_index(axis), 2) == 1


def y_rows(density, displacement, passive, out, low):
    end = NYL - 1
    for row in (0, 1):
        out[pl.ds(row * NXL, NXL), :] = density[:, row if low else end - 1 + row, :]
    for c in range(3):
        if low:
            for row in (0, 1):
                out[pl.ds((2 + 2 * c + row) * NXL, NXL), :] = displacement[c, :, row, :]
        else:
            out[pl.ds((2 + c) * NXL, NXL), :] = displacement[c, :, end, :]
    out[pl.ds((8 if low else 5) * NXL, NXL), :] = passive[:, 0 if low else end, :].astype(
        jnp.float32
    )
    if not low:
        out[pl.ds(6 * NXL, 3 * NXL), :] = jnp.zeros((3 * NXL, NZ), jnp.float32)


def x_planes(density, displacement, passive, y_high, y_low, out, low):
    first = 0 if low else NXL - 2
    for k in (0, 1):
        out[pl.ds(8 * k, 8), :] = density[first + k]
    for c in range(3):
        if low:
            for k in (0, 1):
                out[pl.ds(8 * (2 + 2 * c + k), 8), :] = displacement[c, k]
        else:
            out[pl.ds(8 * (2 + c), 8), :] = displacement[c, NXL - 1]
    out[pl.ds(64 if low else 40, 8), :] = passive[0 if low else NXL - 1].astype(jnp.float32)
    base = 72 if low else 48
    for kind in range(9):
        out[pl.ds(base + 2 * kind, 2), :] = y_high[pl.ds(NXL * kind + first, 2), :]
    for kind in range(6):
        out[pl.ds(base + 18 + 2 * kind, 2), :] = y_low[pl.ds(NXL * kind + first, 2), :]
    out[pl.ds(base + 30, 2), :] = jnp.zeros((2, NZ), jnp.float32)
    if not low:
        out[pl.ds(80, 24), :] = jnp.zeros((24, NZ), jnp.float32)


def by_parity(axis, fill, low_if_odd):
    odd = is_odd(axis)
    pl.when(odd)(lambda: fill(low_if_odd))
    pl.when(jnp.logical_not(odd))(lambda: fill(not low_if_odd))


def pack_y(
    density_far, displacement_far, passive_far, density, displacement, passive, send_a, sems
):
    copies = [
        pltpu.make_async_copy(far, local, sems.at[i])
        for i, (far, local) in enumerate(
            (
                (density_far, density),
                (displacement_far, displacement),
                (passive_far, passive),
            )
        )
    ]
    for copy in copies:
        copy.start()
    for copy in copies:
        copy.wait()
    by_parity(
        "gy", lambda low: y_rows(density, displacement, passive, send_a, low), False
    )


def pack_x(
    density, displacement, passive, received_a, received_b, after, y_high, y_low, send_a
):
    del after
    odd = is_odd("gy")
    y_high[...] = jnp.where(odd, received_a[...], received_b[...])
    low_rows = pl.ds(0, 6 * NXL)
    y_low[...] = jnp.where(odd, received_b[low_rows, :], received_a[low_rows, :])
    by_parity(
        "gx",
        lambda low: x_planes(density, displacement, passive, y_high, y_low, send_a, low),
        False,
    )


def lane_ends(height):
    lane = lax.broadcasted_iota(jnp.int32, (height, NZ), 1)
    return lane == 0, lane == NZ - 1


def z_sum(f, first, last):
    return jnp.where(first, 0.0, pltpu.roll(f, 1, 1)) + jnp.where(
        last, 0.0, pltpu.roll(f, NZ - 1, 1)
    )


def filter_terms(low, mid, high, first, last):
    across = z_sum(mid, first, last)
    along = low + high
    both = across + along
    side = 0.5 * mid + EDGE_WEIGHT * both
    rest = 1.5 * mid + 0.5 * both + EDGE_WEIGHT * z_sum(along, first, last)
    return side, rest


def corner_sums(here, above, last):
    total = here + above
    slope = above - here
    total_next = jnp.where(last, 0.0, pltpu.roll(total, NZ - 1, 1))
    slope_next = jnp.where(last, 0.0, pltpu.roll(slope, NZ - 1, 1))
    return (total + total_next, total_next - total, slope + slope_next, slope_next - slope)


def element_energy(before, after):
    modes = []
    for c in range(3):
        for k in range(4):
            low, high = before[4 * c + k], after[4 * c + k]
            modes.append((low + high, high - low))
    u, v, w = (
        {(a, k // 2, k % 2): modes[4 * c + k][a] for a in (0, 1) for k in range(4)}
        for c in range(3)
    )

    def sq(x):
        return x * x

    trace = sq(u[1, 0, 0] + v[0, 1, 0] + w[0, 0, 1]) + (1.0 / 3.0) * (
        sq(v[1, 1, 0] + w[1, 0, 1]) + sq(u[1, 1, 0] + w[0, 1, 1]) + sq(u[1, 0, 1] + v[0, 1, 1])
    )
    normal = sq(u[1, 0, 0]) + sq(v[0, 1, 0]) + sq(w[0, 0, 1])
    linear = (
        sq(v[1, 1, 0])
        + sq(w[1, 0, 1])
        + sq(u[1, 1, 0])
        + sq(w[0, 1, 1])
        + sq(u[1, 0, 1])
        + sq(v[0, 1, 1])
    )
    bilinear = sq(u[1, 1, 1]) + sq(v[1, 1, 1]) + sq(w[1, 1, 1])
    shear = (
        sq(u[0, 1, 0] + v[1, 0, 0]) + sq(u[0, 0, 1] + w[1, 0, 0]) + sq(v[0, 0, 1] + w[0, 1, 0])
    )
    twist = (
        sq(u[0, 1, 1] + v[1, 0, 1]) + sq(u[0, 1, 1] + w[1, 1, 0]) + sq(v[1, 0, 1] + w[1, 1, 0])
    )
    return (
        (LAME / 16.0) * trace
        + (SHEAR / 8.0) * normal
        + (SHEAR / 16.0) * (linear + shear)
        + ((LAME + 4.0 * SHEAR) / 144.0) * bilinear
        + (SHEAR / 48.0) * twist
    )


def interior_energy(density, displacement, passive, energy, send_b):
    by_parity(
        "gy", lambda low: y_rows(density, displacement, passive, send_b, low), True
    )
    _, last = lane_ends(NYL)

    def nodes(plane):
        here = []
        for c in range(3):
            f = displacement[c, plane]
            here.extend(corner_sums(f, pltpu.roll(f, NYL - 1, 0), last))
        return tuple(here)

    def plane_energy(x, before):
        after = nodes(x + 1)
        energy[x] = element_energy(before, after)
        return after

    lax.fori_loop(0, NXL - 1, plane_energy, nodes(0))
    energy[NXL - 1] = jnp.zeros((NYL, NZ), jnp.float32)


def tables(after, inverse, weights, factors):
    del after
    start_y = lax.axis_index("gy") * NYL
    total_y = lax.axis_size("gy") * NYL
    first, last = lane_ends(NYL)
    trial = lax.broadcasted_iota(jnp.int32, (SLOTS, NZ), 0).astype(jnp.float32)
    factors[...] = jnp.exp(-0.5 * (-BRACKET + STEP * (trial + 1.0)))

    along_z = jnp.where(first | last, 1.0, 2.0)
    for v in (0, 1):
        index_y = start_y - 1 + 8 * v + lax.broadcasted_iota(jnp.int32, (8, NZ), 0)
        inside = (index_y >= 0) & (index_y < total_y)
        along_y = jnp.where((index_y == 0) | (index_y == total_y - 1), 1.0, 2.0)
        base = 1.5 + 0.5 * (along_y + along_z) + EDGE_WEIGHT * along_y * along_z
        slope = 0.5 + EDGE_WEIGHT * (along_y + along_z)
        for slot, along_x in ((0, 2.0), (1, 1.0)):
            inverse[slot, pl.ds(8 * v, 8), :] = jnp.where(
                inside, 1.0 / (base + along_x * slope), 0.0
            )
    for slot in (0, 1):
        side, rest = filter_terms(
            inverse[slot, pl.ds(0, 8), :],
            inverse[slot, pl.ds(1, 8), :],
            inverse[slot, pl.ds(2, 8), :],
            first,
            last,
        )
        weights[2 * slot] = side
        weights[2 * slot + 1] = rest


def spread_of(filtered, weight, kind, energy):
    physical = filtered * weight
    physical = jnp.where(kind == 1.0, 1.0, jnp.where(kind == 2.0, 0.0, physical))
    return -DERIVATIVE * physical * physical * energy * weight


def around(ref, plane, first, last):
    return filter_terms(
        ref[plane, pl.ds(7, 8), :],
        ref[plane, pl.ds(8, 8), :],
        ref[plane, pl.ds(9, 8), :],
        first,
        last,
    )


def add_volumes(planes, factors, scaled, lower, upper, start, partial):
    def volume_group(g, carry):
        base = pl.multiple_of(8 * GROUP * g, 8 * GROUP)
        scales = [
            jnp.broadcast_to(factors[pl.ds(GROUP * g + k, 1), :], (8, NZ)) for k in range(GROUP)
        ]
        if start is None:
            totals = [jnp.zeros((8, NZ), jnp.float32) for _ in range(GROUP)]
        else:
            totals = [start[pl.ds(base + 8 * k, 8), :] for k in range(GROUP)]
        for place, x in planes:
            values, floor, ceiling = scaled[place], lower[x], upper[x]
            for k in range(GROUP):
                totals[k] += jnp.minimum(jnp.maximum(values * scales[k], floor), ceiling)
        for k in range(GROUP):
            partial[pl.ds(base + 8 * k, 8), :] = totals[k]
        return carry

    lax.fori_loop(0, SLOTS // GROUP, volume_group, 0)


def middle(
    density,
    displacement,
    passive,
    own_energy,
    inverse,
    weights,
    y_high,
    y_low,
    sent_a,
    sent_b,
    send_b,
    spread,
    sensitivity,
    scaled,
    lower,
    upper,
    dens,
    energy,
):
    by_parity(
        "gx",
        lambda low: x_planes(density, displacement, passive, y_high, y_low, send_b, low),
        True,
    )
    def rows(ref, kind):
        return ref[pl.ds(kind * NXL, NXL), :]

    odd = is_odd("gy")

    def sent_low(kind):
        return jnp.where(odd, rows(sent_b, kind), rows(sent_a, kind))

    def sent_high(kind):
        return jnp.where(odd, rows(sent_a, kind), rows(sent_b, kind))

    first, last = lane_ends(NXL)

    def row_nodes(ref, step, at):
        return [rows(ref, at + step * c) for c in range(3)]

    def row_energy(here, above):
        before, after = [], []
        for c in range(3):
            sums = corner_sums(here[c], above[c], last)
            before.extend(sums)
            after.extend(pltpu.roll(f, NXL - 1, 0) for f in sums)
        return element_energy(before, after)

    nodes_8 = row_nodes(y_high, 2, 2)
    energy_low = row_energy(row_nodes(y_low, 1, 2), [sent_low(2 + 2 * c) for c in range(3)])
    energy_7 = row_energy([sent_high(2 + c) for c in range(3)], nodes_8)
    energy_high = row_energy(nodes_8, row_nodes(y_high, 2, 3))

    dens[:, pl.ds(8, NYL), :] = density[...]
    dens[:, 7, :] = rows(y_low, 1)
    dens[:, 16, :] = rows(y_high, 0)
    energy[...] = own_energy[...]
    energy[:, 7, :] = energy_7

    for row, low, mid, high, kind, row_energies in (
        (0, rows(y_low, 0), rows(y_low, 1), sent_low(0), rows(y_low, 5), energy_low),
        (9, sent_high(1), rows(y_high, 0), rows(y_high, 1), rows(y_high, 8), energy_high),
    ):
        side, rest = filter_terms(low, mid, high, first, last)
        filtered = rest + pltpu.roll(side, 1, 0) + pltpu.roll(side, NXL - 1, 0)
        weight = jnp.broadcast_to(inverse[0, pl.ds(row, 1), :], (NXL, NZ))
        spread[:, row + 7, :] = spread_of(filtered, weight, kind, row_energies)

    first, last = lane_ends(NYL)
    weight = inverse[0, pl.ds(1, 8), :]

    def spread_plane(x, carry):
        side_before, side_here, rest_here = carry
        side_after, rest_after = around(dens, x + 1, first, last)
        spread[x, pl.ds(8, 8), :] = spread_of(
            rest_here + side_before + side_after,
            weight,
            passive[x].astype(jnp.float32),
            energy[x],
        )
        return side_here, side_after, rest_after

    side_0, _ = around(dens, 0, first, last)
    lax.fori_loop(
        1, NXL - 1, spread_plane, (side_0,) + around(dens, 1, first, last), unroll=2
    )

    scale = 1.0 / (weights[1] + 2.0 * weights[0])

    def out_plane(x, carry):
        side_before, side_here, rest_here = carry
        side_after, rest_after = around(spread, x + 1, first, last)
        sens = rest_here + side_before + side_after
        sensitivity[x] = sens
        scaled[x] = density[x] * jnp.sqrt(-sens * scale)
        return side_here, side_after, rest_after

    side_1, _ = around(spread, 1, first, last)
    lax.fori_loop(
        2, NXL - 2, out_plane, (side_1,) + around(spread, 2, first, last), unroll=2
    )

    here = density[...]
    kind = passive[...]
    fixed = jnp.where(kind == 1, 1.0, 0.0)
    lower[...] = jnp.where(kind == 0, jnp.maximum(here - MOVE_LIMIT, 0.0), fixed)
    upper[...] = jnp.where(kind == 0, jnp.minimum(here + MOVE_LIMIT, 1.0), fixed)


def middle_volumes(factors, scaled, lower, upper, partial):
    add_volumes(
        [(x, x) for x in range(2, NXL - 2)], factors, scaled, lower, upper, None, partial
    )


def edges(
    factors,
    density,
    displacement,
    passive,
    y_high,
    y_low,
    received_a,
    received_b,
    inverse,
    weights,
    spread,
    inner_sensitivity,
    lower,
    upper,
    start,
    sensitivity,
    scaled,
    sums_out,
    dens,
    disp,
    kind_of,
    rim,
    partial,
    x_high,
    x_low,
    *,
    copies,
):
    odd = is_odd("gx")
    x_high[...] = jnp.where(odd, received_a[...], received_b[...])
    x_low[...] = jnp.where(odd, received_b[...], received_a[...])
    first, last = lane_ends(NYL)
    at_end = (
        lax.axis_index("gx") == 0,
        lax.axis_index("gx") == lax.axis_size("gx") - 1,
    )
    for side, (own, far, slabs, low_rows, pick) in enumerate(
        ((0, x_low, 48, 66, 1), (NXL - 2, x_high, 72, 90, 0))
    ):
        for k in (0, 1):
            own_at, far_at = (2 + k, k) if side == 0 else (k, 2 + k)
            dens[side, own_at, pl.ds(2, NYL), :] = density[own + k]
            dens[side, far_at, pl.ds(2, NYL), :] = far[pl.ds(8 * k, 8), :]
            for row in (0, 1):
                dens[side, own_at, pl.ds(NYL + 2 + row, 1), :] = y_high[
                    pl.ds(row * NXL + own + k, 1), :
                ]
                dens[side, own_at, pl.ds(row, 1), :] = y_low[pl.ds(row * NXL + own + k, 1), :]
                dens[side, far_at, pl.ds(NYL + 2 + row, 1), :] = far[
                    pl.ds(slabs + 2 * row + k, 1), :
                ]
                dens[side, far_at, pl.ds(row, 1), :] = far[pl.ds(low_rows + 2 * row + k, 1), :]
        for c in range(3):
            mine = ((1, 0), (2, 1)) if side == 0 else ((0, NXL - 1),)
            theirs = ((0, 2 + c, 1),) if side == 0 else ((1, 2 + 2 * c, 0), (2, 3 + 2 * c, 1))
            for at, x in mine:
                disp[side, c, at, pl.ds(1, NYL), :] = displacement[c, x]
                disp[side, c, at, pl.ds(0, 1), :] = y_low[pl.ds((2 + c) * NXL + x, 1), :]
                for row in (0, 1):
                    disp[side, c, at, pl.ds(NYL + 1 + row, 1), :] = y_high[
                        pl.ds((2 + 2 * c + row) * NXL + x, 1), :
                    ]
            for at, slab, k in theirs:
                disp[side, c, at, pl.ds(1, NYL), :] = far[pl.ds(8 * slab, 8), :]
                disp[side, c, at, pl.ds(0, 1), :] = far[pl.ds(low_rows + 2 * (2 + c) + k, 1), :]
                for row in (0, 1):
                    disp[side, c, at, pl.ds(NYL + 1 + row, 1), :] = far[
                        pl.ds(slabs + 2 * (2 + 2 * c + row) + k, 1), :
                    ]
        own_at, far_at, x = (1, 0, 0) if side == 0 else (0, 1, NXL - 1)
        kind_of[side, own_at, pl.ds(1, NYL), :] = passive[x].astype(jnp.float32)
        kind_of[side, own_at, pl.ds(0, 1), :] = y_low[pl.ds(5 * NXL + x, 1), :]
        kind_of[side, own_at, pl.ds(NYL + 1, 1), :] = y_high[pl.ds(8 * NXL + x, 1), :]
        kind_of[side, far_at, pl.ds(1, NYL), :] = far[pl.ds(40 if side == 0 else 64, 8), :]
        kind_of[side, far_at, pl.ds(0, 1), :] = far[pl.ds(low_rows + 10 + pick, 1), :]
        kind_of[side, far_at, pl.ds(NYL + 1, 1), :] = far[pl.ds(slabs + 16 + pick, 1), :]

        for v in (0, 1):
            rows = pl.ds(8 * v, 8)
            terms = [
                filter_terms(
                    dens[side, p, rows, :],
                    dens[side, p, pl.ds(8 * v + 1, 8), :],
                    dens[side, p, pl.ds(8 * v + 2, 8), :],
                    first,
                    last,
                )
                for p in range(4)
            ]
            nodes = []
            for p in range(3):
                sums = []
                for c in range(3):
                    sums.extend(
                        corner_sums(
                            disp[side, c, p, rows, :],
                            disp[side, c, p, pl.ds(8 * v + 1, 8), :],
                            last,
                        )
                    )
                nodes.append(sums)
            inner = inverse[0, rows, :]
            by_place = (
                jnp.where(at_end[side], 0.0, inner),
                jnp.where(at_end[side], inverse[1, rows, :], inner),
            )
            for k in (0, 1):
                weight = by_place[k] if side == 0 else by_place[1 - k]
                rim[side, (k if side == 0 else 2 + k), pl.ds(7 + 8 * v, 8), :] = spread_of(
                    terms[k + 1][1] + terms[k][0] + terms[k + 2][0],
                    weight,
                    kind_of[side, k, rows, :],
                    element_energy(nodes[k], nodes[k + 1]),
                )
        for k in (0, 1):
            rim[side, (2 + k if side == 0 else k), :, :] = spread[1 + k if side == 0 else 13 + k]

    inner_planes = pl.ds(2, NXL - 4)
    sensitivity[inner_planes] = inner_sensitivity[inner_planes]
    side_inner, rest_inner, side_edge, rest_edge = (weights[i] for i in range(4))
    for side in (0, 1):
        outer_side = jnp.where(at_end[side], 0.0, side_inner)
        next_side = jnp.where(at_end[side], side_edge, side_inner)
        outer = jnp.where(at_end[side], rest_edge, rest_inner) + outer_side + side_inner
        inner = rest_inner + next_side + side_inner
        terms = [around(rim.at[side], p, first, last) for p in range(4)]
        for k in (0, 1):
            x = k if side == 0 else NXL - 2 + k
            sens = terms[k + 1][1] + terms[k][0] + terms[k + 2][0]
            weight = outer if k == side else inner
            sensitivity[x] = sens
            scaled[2 * side + k] = density[x] * jnp.sqrt(-sens / weight)

    add_volumes(
        [(0, 0), (1, 1), (2, NXL - 2), (3, NXL - 1)],
        factors,
        scaled,
        lower,
        upper,
        start,
        partial,
    )
    rows_of = [partial[pl.ds(s, SLOTS, stride=8), :] for s in range(8)]
    lines = ((rows_of[0] + rows_of[1]) + (rows_of[2] + rows_of[3])) + (
        (rows_of[4] + rows_of[5]) + (rows_of[6] + rows_of[7])
    )
    volumes = lax.dot_general(
        jnp.ones((8, NZ), jnp.float32),
        lines,
        (((1,), (1,)), ((), ())),
        precision=lax.Precision.HIGHEST,
        preferred_element_type=jnp.float32,
    )
    second = lax.broadcasted_iota(jnp.int32, (8, NZ), 0) > 0
    pair = jnp.where(second, volumes[:, NZ:], volumes[:, :NZ])[0:2]
    for copy in range(copies):
        sums_out[copy] = pair


def add_copies(received, out, *, copies):
    total = jnp.sum(received[...], axis=0)
    for copy in range(copies):
        out[copy] = total


def finish(
    received,
    scaled,
    scaled_edge,
    lower,
    upper,
    sensitivity,
    new_density_far,
    sensitivity_far,
    new_density,
    sems,
    *,
    target,
):
    copies = [
        pltpu.make_async_copy(sensitivity, sensitivity_far, sems.at[0]),
        pltpu.make_async_copy(new_density, new_density_far, sems.at[1]),
    ]
    copies[0].start()
    volumes = jnp.sum(received[...], axis=0)
    slot = lax.broadcasted_iota(jnp.int32, (2, NZ), 0) * NZ + lax.broadcasted_iota(
        jnp.int32, (2, NZ), 1
    )
    above = jnp.sum(jnp.where((volumes > target) & (slot < TRIALS), 1.0, 0.0))
    middle_end = -BRACKET + STEP * above + 0.5 * STEP
    factor = jnp.exp(jnp.full((8, NZ), -0.5, jnp.float32) * middle_end)[None]
    inner = pl.ds(2, NXL - 4)
    for ref, place, planes in (
        (scaled, inner, inner),
        (scaled_edge, pl.ds(0, 2), pl.ds(0, 2)),
        (scaled_edge, pl.ds(2, 2), pl.ds(NXL - 2, 2)),
    ):
        new_density[planes] = jnp.minimum(
            jnp.maximum(ref[place] * factor, lower[planes]), upper[planes]
        )
    copies[1].start()
    for copy in copies:
        copy.wait()


def f32(*shape):
    return jax.ShapeDtypeStruct(shape, jnp.float32)


def near(*shape, dtype=jnp.float32):
    return pltpu.VMEM(shape, dtype)


def far(array):
    return pltpu.with_memory_space_constraint(array, pltpu.HBM)


def held(array):
    return pltpu.with_memory_space_constraint(array, pltpu.VMEM)


def call(kernel, outputs, inputs, scratch=(), specs=None, out_specs=None, cost=0):
    return pl.pallas_call(
        kernel,
        out_shape=outputs,
        in_specs=specs or [VMEM] * len(inputs),
        out_specs=out_specs or jax.tree.map(lambda _: VMEM, outputs),
        scratch_shapes=list(scratch),
        cost_estimate=pl.CostEstimate(
            flops=cost * 4000, bytes_accessed=cost * 1000, transcendentals=0
        ),
        compiler_params=pltpu.CompilerParams(vmem_limit_bytes=16 << 20),
    )(*inputs)


def swapped(block, axis, start):
    pairs = [(i, i + 1) for i in range(start, lax.axis_size(axis) - 1, 2)]
    return lax.ppermute(block, axis, pairs + [(j, i) for i, j in pairs])


def reduction_groups(count_x, count_y):
    chips_x = count_y // SIDE
    across, along = {}, {}
    for gx in range(count_x):
        for gy in range(count_y):
            device = gx * count_y + gy
            x, y = gy // SIDE, gy % SIDE
            across.setdefault((gx // 2, x // 2), []).append(device)
            along.setdefault((gx % 2, y, min(x, chips_x - 1 - x)), []).append(device)
    return list(across.values()), list(along.values())


def per_device(density, displacement, passive):
    count_x, count_y = lax.axis_size("gx"), lax.axis_size("gy")
    assert density.shape == (NXL, NYL, NZ)
    block = (NXL, NYL, NZ)
    density, displacement, passive, sent_a = call(
        pack_y,
        (
            near(*block),
            near(3, *block),
            near(*block, dtype=jnp.int32),
            near(9 * NXL, NZ),
        ),
        (far(density), far(displacement), far(passive)),
        [pltpu.SemaphoreType.DMA((3,))],
        specs=[pl.BlockSpec(memory_space=pltpu.HBM)] * 3,
        cost=1000,
    )
    received_a = held(swapped(sent_a, "gy", 1))
    own_energy, sent_b = call(
        interior_energy,
        (near(*block), near(9 * NXL, NZ)),
        (density, displacement, passive),
        cost=1000,
    )
    received_b = held(swapped(sent_b, "gy", 0))
    inverse, weights, factors = call(
        tables,
        (near(2, 16, NZ), near(4, NYL, NZ), near(SLOTS, NZ)),
        (own_energy,),
        cost=1000,
    )
    y_high, y_low, to_a = call(
        pack_x,
        (near(9 * NXL, NZ), near(6 * NXL, NZ), near(104, NZ)),
        (density, displacement, passive, received_a, received_b, weights),
        cost=500,
    )
    received_a = held(swapped(to_a, "gx", 1))
    to_b, spread, sensitivity, scaled, lower, upper = call(
        middle,
        (near(104, NZ), near(NXL, 24, NZ)) + (near(*block),) * 4,
        (
            density,
            displacement,
            passive,
            own_energy,
            inverse,
            weights,
            y_high,
            y_low,
            sent_a,
            sent_b,
        ),
        [pltpu.VMEM((NXL, 24, NZ), jnp.float32), pltpu.VMEM(block, jnp.float32)],
        cost=3000,
    )
    received_b = held(swapped(to_b, "gx", 0))
    partial = call(
        middle_volumes, near(8 * SLOTS, NZ), (factors, scaled, lower, upper), cost=3000
    )
    across, along = reduction_groups(count_x, count_y)
    first_group, second_group = len(across[0]), len(along[0])
    sensitivity, scaled_edge, volumes = call(
        functools.partial(edges, copies=first_group),
        (near(*block), near(4, NYL, NZ), near(first_group, 2, NZ)),
        (
            factors,
            density,
            displacement,
            passive,
            y_high,
            y_low,
            received_a,
            received_b,
            inverse,
            weights,
            spread,
            sensitivity,
            lower,
            upper,
            partial,
        ),
        [
            pltpu.VMEM((2, 4, 24, NZ), jnp.float32),
            pltpu.VMEM((2, 3, 3, 24, NZ), jnp.float32),
            pltpu.VMEM((2, 2, 16, NZ), jnp.float32),
            pltpu.VMEM((2, 4, 24, NZ), jnp.float32),
            pltpu.VMEM((8 * SLOTS, NZ), jnp.float32),
            pltpu.VMEM((104, NZ), jnp.float32),
            pltpu.VMEM((104, NZ), jnp.float32),
        ],
        cost=3000,
    )

    volumes = lax.all_to_all(volumes, ("gx", "gy"), 0, 0, axis_index_groups=across)
    volumes = call(
        functools.partial(add_copies, copies=second_group),
        near(second_group, 2, NZ),
        (held(volumes),),
        cost=300,
    )
    volumes = lax.all_to_all(volumes, ("gx", "gy"), 0, 0, axis_index_groups=along)
    target = VOLUME_SHARE * (count_x * NXL) * (count_y * NYL) * NZ
    new_density, sensitivity = call(
        functools.partial(finish, target=target),
        (f32(*block), f32(*block)),
        (held(volumes), scaled, scaled_edge, lower, upper, sensitivity),
        [pltpu.VMEM(block, jnp.float32), pltpu.SemaphoreType.DMA((2,))],
        out_specs=(pl.BlockSpec(memory_space=pltpu.HBM),) * 2,
        cost=500,
    )
    return new_density, sensitivity


def solution(mesh):
    return jax.shard_map(
        per_device,
        mesh=mesh,
        in_specs=(P("gx", "gy", None), P(None, "gx", "gy", None), P("gx", "gy", None)),
        out_specs=(P("gx", "gy", None), P("gx", "gy", None)),
        check_vma=False,
    )
```

```python
import functools
import math

import jax
import jax.numpy as jnp
from jax import lax
from jax.experimental import pallas as pl
from jax.experimental.pallas import tpu as pltpu
from jax.sharding import PartitionSpec as P

BISECT = 8
BRACKET = 8.0
MOVE_LIMIT = 0.2
VOLUME_SHARE = 0.35
DERIVATIVE = 3.0 * (1.0 - 1e-09)
EDGE_WEIGHT = 1.5 - math.sqrt(2.0)
POISSON = 0.3
LAME = POISSON / ((1.0 + POISSON) * (1.0 - 2.0 * POISSON))
SHEAR = 0.5 / (1.0 + POISSON)

NXL = 16
NYL = 8
NZ = 128
TRIALS = 2 ** BISECT - 1
SLOTS = TRIALS + 1
STEP = 2.0 * BRACKET / 2 ** BISECT
GROUP = 16
SIDE = 4

VMEM = pl.BlockSpec(memory_space=pltpu.VMEM)


def is_odd(axis):
    return lax.rem(lax.axis_index(axis), 2) == 1


def pack_y(
    density_far, displacement_far, passive_far, density, displacement, passive, send_a, send_b, sems
):
    copies = [
        pltpu.make_async_copy(far, local, sems.at[i])
        for i, (far, local) in enumerate(
            (
                (density_far, density),
                (displacement_far, displacement),
                (passive_far, passive),
            )
        )
    ]
    for copy in copies:
        copy.start()
    for copy in copies:
        copy.wait()

    def fill(to_low, to_high):
        for row in (0, 1):
            to_low[pl.ds(row * NXL, NXL), :] = density[:, row, :]
            to_high[pl.ds(row * NXL, NXL), :] = density[:, NYL - 2 + row, :]
        for c in range(3):
            for row in (0, 1):
                to_low[pl.ds((2 + 2 * c + row) * NXL, NXL), :] = displacement[c, :, row, :]
            to_high[pl.ds((2 + c) * NXL, NXL), :] = displacement[c, :, NYL - 1, :]
        to_low[pl.ds(8 * NXL, NXL), :] = passive[:, 0, :].astype(jnp.float32)
        to_high[pl.ds(5 * NXL, NXL), :] = passive[:, NYL - 1, :].astype(jnp.float32)
        to_high[pl.ds(6 * NXL, 3 * NXL), :] = jnp.zeros((3 * NXL, NZ), jnp.float32)

    odd = is_odd("gy")
    pl.when(odd)(lambda: fill(send_b, send_a))
    pl.when(jnp.logical_not(odd))(lambda: fill(send_a, send_b))


def pack_x(
    density, displacement, passive, received_a, received_b, after, y_high, y_low, send_a, send_b
):
    del after
    odd = is_odd("gy")
    y_high[...] = jnp.where(odd, received_a[...], received_b[...])
    low = pl.ds(0, 6 * NXL)
    y_low[...] = jnp.where(odd, received_b[low, :], received_a[low, :])

    def fill(to_low, to_high):
        for k in (0, 1):
            to_low[pl.ds(8 * k, 8), :] = density[k]
            to_high[pl.ds(8 * k, 8), :] = density[NXL - 2 + k]
        for c in range(3):
            for k in (0, 1):
                to_low[pl.ds(8 * (2 + 2 * c + k), 8), :] = displacement[c, k]
            to_high[pl.ds(8 * (2 + c), 8), :] = displacement[c, NXL - 1]
        to_low[pl.ds(64, 8), :] = passive[0].astype(jnp.float32)
        to_high[pl.ds(40, 8), :] = passive[NXL - 1].astype(jnp.float32)
        for base, first, out in ((72, 0, to_low), (48, NXL - 2, to_high)):
            for kind in range(9):
                out[pl.ds(base + 2 * kind, 2), :] = y_high[pl.ds(NXL * kind + first, 2), :]
            for kind in range(6):
                out[pl.ds(base + 18 + 2 * kind, 2), :] = y_low[pl.ds(NXL * kind + first, 2), :]
            out[pl.ds(base + 30, 2), :] = jnp.zeros((2, NZ), jnp.float32)
        to_high[pl.ds(80, 24), :] = jnp.zeros((24, NZ), jnp.float32)

    odd_x = is_odd("gx")
    pl.when(odd_x)(lambda: fill(send_b, send_a))
    pl.when(jnp.logical_not(odd_x))(lambda: fill(send_a, send_b))


def lane_ends(height):
    lane = lax.broadcasted_iota(jnp.int32, (height, NZ), 1)
    return lane == 0, lane == NZ - 1


def z_sum(f, first, last):
    return jnp.where(first, 0.0, pltpu.roll(f, 1, 1)) + jnp.where(
        last, 0.0, pltpu.roll(f, NZ - 1, 1)
    )


def filter_terms(low, mid, high, first, last):
    across = z_sum(mid, first, last)
    along = low + high
    both = across + along
    side = 0.5 * mid + EDGE_WEIGHT * both
    rest = 1.5 * mid + 0.5 * both + EDGE_WEIGHT * z_sum(along, first, last)
    return side, rest


def corner_sums(here, above, last):
    total = here + above
    slope = above - here
    total_next = jnp.where(last, 0.0, pltpu.roll(total, NZ - 1, 1))
    slope_next = jnp.where(last, 0.0, pltpu.roll(slope, NZ - 1, 1))
    return (total + total_next, total_next - total, slope + slope_next, slope_next - slope)


def element_energy(before, after):
    modes = []
    for c in range(3):
        for k in range(4):
            low, high = before[4 * c + k], after[4 * c + k]
            modes.append((low + high, high - low))
    u, v, w = (
        {(a, k // 2, k % 2): modes[4 * c + k][a] for a in (0, 1) for k in range(4)}
        for c in range(3)
    )

    def sq(x):
        return x * x

    trace = sq(u[1, 0, 0] + v[0, 1, 0] + w[0, 0, 1]) + (1.0 / 3.0) * (
        sq(v[1, 1, 0] + w[1, 0, 1]) + sq(u[1, 1, 0] + w[0, 1, 1]) + sq(u[1, 0, 1] + v[0, 1, 1])
    )
    normal = sq(u[1, 0, 0]) + sq(v[0, 1, 0]) + sq(w[0, 0, 1])
    linear = (
        sq(v[1, 1, 0])
        + sq(w[1, 0, 1])
        + sq(u[1, 1, 0])
        + sq(w[0, 1, 1])
        + sq(u[1, 0, 1])
        + sq(v[0, 1, 1])
    )
    bilinear = sq(u[1, 1, 1]) + sq(v[1, 1, 1]) + sq(w[1, 1, 1])
    shear = (
        sq(u[0, 1, 0] + v[1, 0, 0]) + sq(u[0, 0, 1] + w[1, 0, 0]) + sq(v[0, 0, 1] + w[0, 1, 0])
    )
    twist = (
        sq(u[0, 1, 1] + v[1, 0, 1]) + sq(u[0, 1, 1] + w[1, 1, 0]) + sq(v[1, 0, 1] + w[1, 1, 0])
    )
    return (
        (LAME / 16.0) * trace
        + (SHEAR / 8.0) * normal
        + (SHEAR / 16.0) * (linear + shear)
        + ((LAME + 4.0 * SHEAR) / 144.0) * bilinear
        + (SHEAR / 48.0) * twist
    )


def interior_energy(displacement, energy, inverse, weights, factors):
    start_y = lax.axis_index("gy") * NYL
    total_y = lax.axis_size("gy") * NYL
    first, last = lane_ends(NYL)

    def nodes(plane):
        here = []
        for c in range(3):
            f = displacement[c, plane]
            here.extend(corner_sums(f, pltpu.roll(f, NYL - 1, 0), last))
        return tuple(here)

    def plane_energy(x, before):
        after = nodes(x + 1)
        energy[x] = element_energy(before, after)
        return after

    before = nodes(0)
    for x in range(NXL - 1):
        before = plane_energy(x, before)
    energy[NXL - 1] = jnp.zeros((NYL, NZ), jnp.float32)
    trial = lax.broadcasted_iota(jnp.int32, (SLOTS, NZ), 0).astype(jnp.float32)
    factors[...] = jnp.exp(-0.5 * (-BRACKET + STEP * (trial + 1.0)))

    along_z = jnp.where(first | last, 1.0, 2.0)
    for v in (0, 1):
        index_y = start_y - 1 + 8 * v + lax.broadcasted_iota(jnp.int32, (8, NZ), 0)
        inside = (index_y >= 0) & (index_y < total_y)
        along_y = jnp.where((index_y == 0) | (index_y == total_y - 1), 1.0, 2.0)
        base = 1.5 + 0.5 * (along_y + along_z) + EDGE_WEIGHT * along_y * along_z
        slope = 0.5 + EDGE_WEIGHT * (along_y + along_z)
        for slot, along_x in ((0, 2.0), (1, 1.0)):
            inverse[slot, pl.ds(8 * v, 8), :] = jnp.where(
                inside, 1.0 / (base + along_x * slope), 0.0
            )
    for slot in (0, 1):
        side, rest = filter_terms(
            inverse[slot, pl.ds(0, 8), :],
            inverse[slot, pl.ds(1, 8), :],
            inverse[slot, pl.ds(2, 8), :],
            first,
            last,
        )
        weights[2 * slot] = side
        weights[2 * slot + 1] = rest


def spread_of(filtered, weight, kind, energy):
    physical = filtered * weight
    physical = jnp.where(kind == 1.0, 1.0, jnp.where(kind == 2.0, 0.0, physical))
    return -DERIVATIVE * physical * physical * energy * weight


def around(ref, plane, first, last):
    return filter_terms(
        ref[plane, pl.ds(7, 8), :],
        ref[plane, pl.ds(8, 8), :],
        ref[plane, pl.ds(9, 8), :],
        first,
        last,
    )


def add_volumes(planes, factors, scaled, lower, upper, start, partial):
    def volume_group(g, carry):
        base = pl.multiple_of(8 * GROUP * g, 8 * GROUP)
        scales = [
            jnp.broadcast_to(factors[pl.ds(GROUP * g + k, 1), :], (8, NZ)) for k in range(GROUP)
        ]
        if start is None:
            totals = [jnp.zeros((8, NZ), jnp.float32) for _ in range(GROUP)]
        else:
            totals = [start[pl.ds(base + 8 * k, 8), :] for k in range(GROUP)]
        for place, x in planes:
            values, floor, ceiling = scaled[place], lower[x], upper[x]
            for k in range(GROUP):
                totals[k] += jnp.minimum(jnp.maximum(values * scales[k], floor), ceiling)
        for k in range(GROUP):
            partial[pl.ds(base + 8 * k, 8), :] = totals[k]
        return carry

    lax.fori_loop(0, SLOTS // GROUP, volume_group, 0)


def middle(
    factors,
    density,
    passive,
    own_energy,
    inverse,
    weights,
    y_high,
    y_low,
    sent_a,
    sent_b,
    spread,
    sensitivity,
    scaled,
    lower,
    upper,
    partial,
    dens,
    energy,
):
    def rows(ref, kind):
        return ref[pl.ds(kind * NXL, NXL), :]

    odd = is_odd("gy")

    def sent_low(kind):
        return jnp.where(odd, rows(sent_b, kind), rows(sent_a, kind))

    def sent_high(kind):
        return jnp.where(odd, rows(sent_a, kind), rows(sent_b, kind))

    first, last = lane_ends(NXL)

    def row_nodes(ref, step, at):
        return [rows(ref, at + step * c) for c in range(3)]

    def row_energy(here, above):
        before, after = [], []
        for c in range(3):
            sums = corner_sums(here[c], above[c], last)
            before.extend(sums)
            after.extend(pltpu.roll(f, NXL - 1, 0) for f in sums)
        return element_energy(before, after)

    nodes_8 = row_nodes(y_high, 2, 2)
    energy_low = row_energy(row_nodes(y_low, 1, 2), [sent_low(2 + 2 * c) for c in range(3)])
    energy_7 = row_energy([sent_high(2 + c) for c in range(3)], nodes_8)
    energy_high = row_energy(nodes_8, row_nodes(y_high, 2, 3))

    dens[:, pl.ds(8, NYL), :] = density[...]
    dens[:, 7, :] = rows(y_low, 1)
    dens[:, 16, :] = rows(y_high, 0)
    energy[...] = own_energy[...]
    energy[:, 7, :] = energy_7

    for row, low, mid, high, kind, row_energies in (
        (0, rows(y_low, 0), rows(y_low, 1), sent_low(0), rows(y_low, 5), energy_low),
        (9, sent_high(1), rows(y_high, 0), rows(y_high, 1), rows(y_high, 8), energy_high),
    ):
        side, rest = filter_terms(low, mid, high, first, last)
        filtered = rest + pltpu.roll(side, 1, 0) + pltpu.roll(side, NXL - 1, 0)
        weight = jnp.broadcast_to(inverse[0, pl.ds(row, 1), :], (NXL, NZ))
        spread[:, row + 7, :] = spread_of(filtered, weight, kind, row_energies)

    first, last = lane_ends(NYL)
    weight = inverse[0, pl.ds(1, 8), :]

    def spread_plane(x, carry):
        side_before, side_here, rest_here = carry
        side_after, rest_after = around(dens, x + 1, first, last)
        spread[x, pl.ds(8, 8), :] = spread_of(
            rest_here + side_before + side_after,
            weight,
            passive[x].astype(jnp.float32),
            energy[x],
        )
        return side_here, side_after, rest_after

    side_0, _ = around(dens, 0, first, last)
    carry = (side_0,) + around(dens, 1, first, last)
    for x in range(1, NXL - 1):
        carry = spread_plane(x, carry)

    scale = 1.0 / (weights[1] + 2.0 * weights[0])

    def out_plane(x, carry):
        side_before, side_here, rest_here = carry
        side_after, rest_after = around(spread, x + 1, first, last)
        sens = rest_here + side_before + side_after
        sensitivity[x] = sens
        scaled[x] = density[x] * jnp.sqrt(-sens * scale)
        return side_here, side_after, rest_after

    side_1, _ = around(spread, 1, first, last)
    carry = (side_1,) + around(spread, 2, first, last)
    for x in range(2, NXL - 2):
        carry = out_plane(x, carry)

    here = density[...]
    kind = passive[...]
    fixed = jnp.where(kind == 1, 1.0, 0.0)
    lower[...] = jnp.where(kind == 0, jnp.maximum(here - MOVE_LIMIT, 0.0), fixed)
    upper[...] = jnp.where(kind == 0, jnp.minimum(here + MOVE_LIMIT, 1.0), fixed)
    add_volumes(
        [(x, x) for x in range(2, NXL - 2)], factors, scaled, lower, upper, None, partial
    )


def edges(
    factors,
    density,
    displacement,
    passive,
    y_high,
    y_low,
    received_a,
    received_b,
    inverse,
    weights,
    spread,
    inner_sensitivity,
    lower,
    upper,
    start,
    sensitivity,
    scaled,
    sums_out,
    dens,
    disp,
    kind_of,
    rim,
    partial,
    x_high,
    x_low,
    *,
    copies,
):
    odd = is_odd("gx")
    x_high[...] = jnp.where(odd, received_a[...], received_b[...])
    x_low[...] = jnp.where(odd, received_b[...], received_a[...])
    first, last = lane_ends(NYL)
    at_end = (
        lax.axis_index("gx") == 0,
        lax.axis_index("gx") == lax.axis_size("gx") - 1,
    )
    for side, (own, far, slabs, low_rows, pick) in enumerate(
        ((0, x_low, 48, 66, 1), (NXL - 2, x_high, 72, 90, 0))
    ):
        for k in (0, 1):
            own_at, far_at = (2 + k, k) if side == 0 else (k, 2 + k)
            dens[side, own_at, pl.ds(2, NYL), :] = density[own + k]
            dens[side, far_at, pl.ds(2, NYL), :] = far[pl.ds(8 * k, 8), :]
            for row in (0, 1):
                dens[side, own_at, pl.ds(NYL + 2 + row, 1), :] = y_high[
                    pl.ds(row * NXL + own + k, 1), :
                ]
                dens[side, own_at, pl.ds(row, 1), :] = y_low[pl.ds(row * NXL + own + k, 1), :]
                dens[side, far_at, pl.ds(NYL + 2 + row, 1), :] = far[
                    pl.ds(slabs + 2 * row + k, 1), :
                ]
                dens[side, far_at, pl.ds(row, 1), :] = far[pl.ds(low_rows + 2 * row + k, 1), :]
        for c in range(3):
            mine = ((1, 0), (2, 1)) if side == 0 else ((0, NXL - 1),)
            theirs = ((0, 2 + c, 1),) if side == 0 else ((1, 2 + 2 * c, 0), (2, 3 + 2 * c, 1))
            for at, x in mine:
                disp[side, c, at, pl.ds(1, NYL), :] = displacement[c, x]
                disp[side, c, at, pl.ds(0, 1), :] = y_low[pl.ds((2 + c) * NXL + x, 1), :]
                for row in (0, 1):
                    disp[side, c, at, pl.ds(NYL + 1 + row, 1), :] = y_high[
                        pl.ds((2 + 2 * c + row) * NXL + x, 1), :
                    ]
            for at, slab, k in theirs:
                disp[side, c, at, pl.ds(1, NYL), :] = far[pl.ds(8 * slab, 8), :]
                disp[side, c, at, pl.ds(0, 1), :] = far[pl.ds(low_rows + 2 * (2 + c) + k, 1), :]
                for row in (0, 1):
                    disp[side, c, at, pl.ds(NYL + 1 + row, 1), :] = far[
                        pl.ds(slabs + 2 * (2 + 2 * c + row) + k, 1), :
                    ]
        own_at, far_at, x = (1, 0, 0) if side == 0 else (0, 1, NXL - 1)
        kind_of[side, own_at, pl.ds(1, NYL), :] = passive[x].astype(jnp.float32)
        kind_of[side, own_at, pl.ds(0, 1), :] = y_low[pl.ds(5 * NXL + x, 1), :]
        kind_of[side, own_at, pl.ds(NYL + 1, 1), :] = y_high[pl.ds(8 * NXL + x, 1), :]
        kind_of[side, far_at, pl.ds(1, NYL), :] = far[pl.ds(40 if side == 0 else 64, 8), :]
        kind_of[side, far_at, pl.ds(0, 1), :] = far[pl.ds(low_rows + 10 + pick, 1), :]
        kind_of[side, far_at, pl.ds(NYL + 1, 1), :] = far[pl.ds(slabs + 16 + pick, 1), :]

        for v in (0, 1):
            rows = pl.ds(8 * v, 8)
            terms = [
                filter_terms(
                    dens[side, p, rows, :],
                    dens[side, p, pl.ds(8 * v + 1, 8), :],
                    dens[side, p, pl.ds(8 * v + 2, 8), :],
                    first,
                    last,
                )
                for p in range(4)
            ]
            nodes = []
            for p in range(3):
                sums = []
                for c in range(3):
                    sums.extend(
                        corner_sums(
                            disp[side, c, p, rows, :],
                            disp[side, c, p, pl.ds(8 * v + 1, 8), :],
                            last,
                        )
                    )
                nodes.append(sums)
            inner = inverse[0, rows, :]
            by_place = (
                jnp.where(at_end[side], 0.0, inner),
                jnp.where(at_end[side], inverse[1, rows, :], inner),
            )
            for k in (0, 1):
                weight = by_place[k] if side == 0 else by_place[1 - k]
                rim[side, (k if side == 0 else 2 + k), pl.ds(7 + 8 * v, 8), :] = spread_of(
                    terms[k + 1][1] + terms[k][0] + terms[k + 2][0],
                    weight,
                    kind_of[side, k, rows, :],
                    element_energy(nodes[k], nodes[k + 1]),
                )
        for k in (0, 1):
            rim[side, (2 + k if side == 0 else k), :, :] = spread[1 + k if side == 0 else 13 + k]

    inner_planes = pl.ds(2, NXL - 4)
    sensitivity[inner_planes] = inner_sensitivity[inner_planes]
    side_inner, rest_inner, side_edge, rest_edge = (weights[i] for i in range(4))
    for side in (0, 1):
        outer_side = jnp.where(at_end[side], 0.0, side_inner)
        next_side = jnp.where(at_end[side], side_edge, side_inner)
        outer = jnp.where(at_end[side], rest_edge, rest_inner) + outer_side + side_inner
        inner = rest_inner + next_side + side_inner
        terms = [around(rim.at[side], p, first, last) for p in range(4)]
        for k in (0, 1):
            x = k if side == 0 else NXL - 2 + k
            sens = terms[k + 1][1] + terms[k][0] + terms[k + 2][0]
            weight = outer if k == side else inner
            sensitivity[x] = sens
            scaled[2 * side + k] = density[x] * jnp.sqrt(-sens / weight)

    add_volumes(
        [(0, 0), (1, 1), (2, NXL - 2), (3, NXL - 1)],
        factors,
        scaled,
        lower,
        upper,
        start,
        partial,
    )
    rows_of = [partial[pl.ds(s, SLOTS, stride=8), :] for s in range(8)]
    lines = ((rows_of[0] + rows_of[1]) + (rows_of[2] + rows_of[3])) + (
        (rows_of[4] + rows_of[5]) + (rows_of[6] + rows_of[7])
    )
    volumes = lax.dot_general(
        jnp.ones((8, NZ), jnp.float32),
        lines,
        (((1,), (1,)), ((), ())),
        precision=lax.Precision.HIGHEST,
        preferred_element_type=jnp.float32,
    )
    second = lax.broadcasted_iota(jnp.int32, (8, NZ), 0) > 0
    pair = jnp.where(second, volumes[:, NZ:], volumes[:, :NZ])[0:2]
    for copy in range(copies):
        sums_out[copy] = pair


def add_copies(received, out, *, copies):
    total = jnp.sum(received[...], axis=0)
    for copy in range(copies):
        out[copy] = total


def finish(
    received,
    scaled,
    scaled_edge,
    lower,
    upper,
    sensitivity,
    new_density_far,
    sensitivity_far,
    new_density,
    sems,
    *,
    target,
):
    copies = [
        pltpu.make_async_copy(sensitivity, sensitivity_far, sems.at[0]),
        pltpu.make_async_copy(new_density, new_density_far, sems.at[1]),
    ]
    copies[0].start()
    volumes = jnp.sum(received[...], axis=0)
    slot = lax.broadcasted_iota(jnp.int32, (2, NZ), 0) * NZ + lax.broadcasted_iota(
        jnp.int32, (2, NZ), 1
    )
    above = jnp.sum(jnp.where((volumes > target) & (slot < TRIALS), 1.0, 0.0))
    middle_end = -BRACKET + STEP * above + 0.5 * STEP
    factor = jnp.exp(jnp.full((8, NZ), -0.5, jnp.float32) * middle_end)[None]
    inner = pl.ds(2, NXL - 4)
    for ref, place, planes in (
        (scaled, inner, inner),
        (scaled_edge, pl.ds(0, 2), pl.ds(0, 2)),
        (scaled_edge, pl.ds(2, 2), pl.ds(NXL - 2, 2)),
    ):
        new_density[planes] = jnp.minimum(
            jnp.maximum(ref[place] * factor, lower[planes]), upper[planes]
        )
    copies[1].start()
    for copy in copies:
        copy.wait()


def f32(*shape):
    return jax.ShapeDtypeStruct(shape, jnp.float32)


def near(*shape, dtype=jnp.float32):
    return pltpu.VMEM(shape, dtype)


def far(array):
    return pltpu.with_memory_space_constraint(array, pltpu.HBM)


def held(array):
    return pltpu.with_memory_space_constraint(array, pltpu.VMEM)


def call(kernel, outputs, inputs, scratch=(), specs=None, out_specs=None, cost=0):
    return pl.pallas_call(
        kernel,
        out_shape=outputs,
        in_specs=specs or [VMEM] * len(inputs),
        out_specs=out_specs or jax.tree.map(lambda _: VMEM, outputs),
        scratch_shapes=list(scratch),
        cost_estimate=pl.CostEstimate(
            flops=cost * 4000, bytes_accessed=cost * 1000, transcendentals=0
        ),
        compiler_params=pltpu.CompilerParams(vmem_limit_bytes=16 << 20),
    )(*inputs)


def swapped(block, axis, start):
    pairs = [(i, i + 1) for i in range(start, lax.axis_size(axis) - 1, 2)]
    return lax.ppermute(block, axis, pairs + [(j, i) for i, j in pairs])


def reduction_groups(count_x, count_y):
    chips_x = count_y // SIDE
    across, along = {}, {}
    for gx in range(count_x):
        for gy in range(count_y):
            device = gx * count_y + gy
            x, y = gy // SIDE, gy % SIDE
            across.setdefault((gx // 2, min(x, chips_x - 1 - x)), []).append(device)
            along.setdefault((gx % 2, y, x // 2), []).append(device)
    return list(across.values()), list(along.values())


def per_device(density, displacement, passive):
    count_x, count_y = lax.axis_size("gx"), lax.axis_size("gy")
    assert density.shape == (NXL, NYL, NZ)
    block = (NXL, NYL, NZ)
    density, displacement, passive, sent_a, sent_b = call(
        pack_y,
        (
            near(*block),
            near(3, *block),
            near(*block, dtype=jnp.int32),
            near(9 * NXL, NZ),
            near(9 * NXL, NZ),
        ),
        (far(density), far(displacement), far(passive)),
        [pltpu.SemaphoreType.DMA((3,))],
        specs=[pl.BlockSpec(memory_space=pltpu.HBM)] * 3,
        cost=1000,
    )
    received_a = held(swapped(sent_a, "gy", 1))
    received_b = held(swapped(sent_b, "gy", 0))
    own_energy, inverse, weights, factors = call(
        interior_energy,
        (near(*block), near(2, 16, NZ), near(4, NYL, NZ), near(SLOTS, NZ)),
        (displacement,),
        cost=1000,
    )
    y_high, y_low, to_a, to_b = call(
        pack_x,
        (near(9 * NXL, NZ), near(6 * NXL, NZ), near(104, NZ), near(104, NZ)),
        (density, displacement, passive, received_a, received_b, weights),
        cost=500,
    )
    received_a = held(swapped(to_a, "gx", 1))
    received_b = held(swapped(to_b, "gx", 0))
    spread, sensitivity, scaled, lower, upper, partial = call(
        middle,
        (near(NXL, 24, NZ),) + (near(*block),) * 4 + (near(8 * SLOTS, NZ),),
        (
            factors,
            density,
            passive,
            own_energy,
            inverse,
            weights,
            y_high,
            y_low,
            sent_a,
            sent_b,
        ),
        [pltpu.VMEM((NXL, 24, NZ), jnp.float32), pltpu.VMEM(block, jnp.float32)],
        cost=5000,
    )
    across, along = reduction_groups(count_x, count_y)
    first_group, second_group = len(across[0]), len(along[0])
    sensitivity, scaled_edge, volumes = call(
        functools.partial(edges, copies=first_group),
        (near(*block), near(4, NYL, NZ), near(first_group, 2, NZ)),
        (
            factors,
            density,
            displacement,
            passive,
            y_high,
            y_low,
            received_a,
            received_b,
            inverse,
            weights,
            spread,
            sensitivity,
            lower,
            upper,
            partial,
        ),
        [
            pltpu.VMEM((2, 4, 24, NZ), jnp.float32),
            pltpu.VMEM((2, 3, 3, 24, NZ), jnp.float32),
            pltpu.VMEM((2, 2, 16, NZ), jnp.float32),
            pltpu.VMEM((2, 4, 24, NZ), jnp.float32),
            pltpu.VMEM((8 * SLOTS, NZ), jnp.float32),
            pltpu.VMEM((104, NZ), jnp.float32),
            pltpu.VMEM((104, NZ), jnp.float32),
        ],
        cost=3000,
    )

    volumes = lax.all_to_all(volumes, ("gx", "gy"), 0, 0, axis_index_groups=across)
    volumes = call(
        functools.partial(add_copies, copies=second_group),
        near(second_group, 2, NZ),
        (held(volumes),),
        cost=300,
    )
    volumes = lax.all_to_all(volumes, ("gx", "gy"), 0, 0, axis_index_groups=along)
    target = VOLUME_SHARE * (count_x * NXL) * (count_y * NYL) * NZ
    new_density, sensitivity = call(
        functools.partial(finish, target=target),
        (f32(*block), f32(*block)),
        (held(volumes), scaled, scaled_edge, lower, upper, sensitivity),
        [pltpu.VMEM(block, jnp.float32), pltpu.SemaphoreType.DMA((2,))],
        out_specs=(pl.BlockSpec(memory_space=pltpu.HBM),) * 2,
        cost=500,
    )
    return new_density, sensitivity


def solution(mesh):
    return jax.shard_map(
        per_device,
        mesh=mesh,
        in_specs=(P("gx", "gy", None), P(None, "gx", "gy", None), P("gx", "gy", None)),
        out_specs=(P("gx", "gy", None), P("gx", "gy", None)),
        check_vma=False,
    )
```

```python
import functools
import math

import jax
import jax.numpy as jnp
from jax import lax
from jax.experimental import pallas as pl
from jax.experimental.pallas import tpu as pltpu
from jax.sharding import PartitionSpec as P

BISECT = 8
BRACKET = 8.0
MOVE_LIMIT = 0.2
VOLUME_SHARE = 0.35
DERIVATIVE = 3.0 * (1.0 - 1e-09)
EDGE_WEIGHT = 1.5 - math.sqrt(2.0)
POISSON = 0.3
LAME = POISSON / ((1.0 + POISSON) * (1.0 - 2.0 * POISSON))
SHEAR = 0.5 / (1.0 + POISSON)

NXL = 16
NYL = 8
NZ = 128
TRIALS = 2 ** BISECT - 1
SLOTS = TRIALS + 1
STEP = 2.0 * BRACKET / 2 ** BISECT
GROUP = 16
PAIRS = NXL // 2 - 2
SIDE = 4

VMEM = pl.BlockSpec(memory_space=pltpu.VMEM)


def is_odd(axis):
    return lax.rem(lax.axis_index(axis), 2) == 1


def pack_y(
    density_far, displacement_far, passive_far, density, displacement, passive, send_a, send_b, sems
):
    copies = [
        pltpu.make_async_copy(far, local, sems.at[i])
        for i, (far, local) in enumerate(
            (
                (density_far, density),
                (displacement_far, displacement),
                (passive_far, passive),
            )
        )
    ]
    for copy in copies:
        copy.start()
    for copy in copies:
        copy.wait()

    def fill(to_low, to_high):
        for row in (0, 1):
            to_low[pl.ds(row * NXL, NXL), :] = density[:, row, :]
            to_high[pl.ds(row * NXL, NXL), :] = density[:, NYL - 2 + row, :]
        for c in range(3):
            for row in (0, 1):
                to_low[pl.ds((2 + 2 * c + row) * NXL, NXL), :] = displacement[c, :, row, :]
            to_high[pl.ds((2 + c) * NXL, NXL), :] = displacement[c, :, NYL - 1, :]
        to_low[pl.ds(8 * NXL, NXL), :] = passive[:, 0, :].astype(jnp.float32)
        to_high[pl.ds(5 * NXL, NXL), :] = passive[:, NYL - 1, :].astype(jnp.float32)
        to_high[pl.ds(6 * NXL, 3 * NXL), :] = jnp.zeros((3 * NXL, NZ), jnp.float32)

    odd = is_odd("gy")
    pl.when(odd)(lambda: fill(send_b, send_a))
    pl.when(jnp.logical_not(odd))(lambda: fill(send_a, send_b))


def pack_x(
    density, displacement, passive, received_a, received_b, after, y_high, y_low, send_a, send_b
):
    del after
    odd = is_odd("gy")
    y_high[...] = jnp.where(odd, received_a[...], received_b[...])
    low = pl.ds(0, 6 * NXL)
    y_low[...] = jnp.where(odd, received_b[low, :], received_a[low, :])

    def fill(to_low, to_high):
        for k in (0, 1):
            to_low[pl.ds(8 * k, 8), :] = density[k]
            to_high[pl.ds(8 * k, 8), :] = density[NXL - 2 + k]
        for c in range(3):
            for k in (0, 1):
                to_low[pl.ds(8 * (2 + 2 * c + k), 8), :] = displacement[c, k]
            to_high[pl.ds(8 * (2 + c), 8), :] = displacement[c, NXL - 1]
        to_low[pl.ds(64, 8), :] = passive[0].astype(jnp.float32)
        to_high[pl.ds(40, 8), :] = passive[NXL - 1].astype(jnp.float32)
        for base, first, out in ((72, 0, to_low), (48, NXL - 2, to_high)):
            for kind in range(9):
                out[pl.ds(base + 2 * kind, 2), :] = y_high[pl.ds(NXL * kind + first, 2), :]
            for kind in range(6):
                out[pl.ds(base + 18 + 2 * kind, 2), :] = y_low[pl.ds(NXL * kind + first, 2), :]
            out[pl.ds(base + 30, 2), :] = jnp.zeros((2, NZ), jnp.float32)
        to_high[pl.ds(80, 24), :] = jnp.zeros((24, NZ), jnp.float32)

    odd_x = is_odd("gx")
    pl.when(odd_x)(lambda: fill(send_b, send_a))
    pl.when(jnp.logical_not(odd_x))(lambda: fill(send_a, send_b))


def lane_ends(height):
    lane = lax.broadcasted_iota(jnp.int32, (height, NZ), 1)
    return lane == 0, lane == NZ - 1


def z_sum(f, first, last):
    return jnp.where(first, 0.0, pltpu.roll(f, 1, 1)) + jnp.where(
        last, 0.0, pltpu.roll(f, NZ - 1, 1)
    )


def filter_terms(low, mid, high, first, last):
    across = z_sum(mid, first, last)
    along = low + high
    both = across + along
    side = 0.5 * mid + EDGE_WEIGHT * both
    rest = 1.5 * mid + 0.5 * both + EDGE_WEIGHT * z_sum(along, first, last)
    return side, rest


def corner_sums(here, above, last):
    total = here + above
    slope = above - here
    total_next = jnp.where(last, 0.0, pltpu.roll(total, NZ - 1, 1))
    slope_next = jnp.where(last, 0.0, pltpu.roll(slope, NZ - 1, 1))
    return (total + total_next, total_next - total, slope + slope_next, slope_next - slope)


def element_energy(before, after):
    modes = []
    for c in range(3):
        for k in range(4):
            low, high = before[4 * c + k], after[4 * c + k]
            modes.append((low + high, high - low))
    u, v, w = (
        {(a, k // 2, k % 2): modes[4 * c + k][a] for a in (0, 1) for k in range(4)}
        for c in range(3)
    )

    def sq(x):
        return x * x

    trace = sq(u[1, 0, 0] + v[0, 1, 0] + w[0, 0, 1]) + (1.0 / 3.0) * (
        sq(v[1, 1, 0] + w[1, 0, 1]) + sq(u[1, 1, 0] + w[0, 1, 1]) + sq(u[1, 0, 1] + v[0, 1, 1])
    )
    normal = sq(u[1, 0, 0]) + sq(v[0, 1, 0]) + sq(w[0, 0, 1])
    linear = (
        sq(v[1, 1, 0])
        + sq(w[1, 0, 1])
        + sq(u[1, 1, 0])
        + sq(w[0, 1, 1])
        + sq(u[1, 0, 1])
        + sq(v[0, 1, 1])
    )
    bilinear = sq(u[1, 1, 1]) + sq(v[1, 1, 1]) + sq(w[1, 1, 1])
    shear = (
        sq(u[0, 1, 0] + v[1, 0, 0]) + sq(u[0, 0, 1] + w[1, 0, 0]) + sq(v[0, 0, 1] + w[0, 1, 0])
    )
    twist = (
        sq(u[0, 1, 1] + v[1, 0, 1]) + sq(u[0, 1, 1] + w[1, 1, 0]) + sq(v[1, 0, 1] + w[1, 1, 0])
    )
    return (
        (LAME / 16.0) * trace
        + (SHEAR / 8.0) * normal
        + (SHEAR / 16.0) * (linear + shear)
        + ((LAME + 4.0 * SHEAR) / 144.0) * bilinear
        + (SHEAR / 48.0) * twist
    )


def interior(
    density,
    displacement,
    passive,
    energy,
    inverse,
    weights,
    factors,
    lower,
    upper,
    lower_outer,
    upper_outer,
    partial,
    own_spread,
    inner,
):
    start_y = lax.axis_index("gy") * NYL
    total_y = lax.axis_size("gy") * NYL
    first, last = lane_ends(NYL)

    def nodes(plane):
        here = []
        for c in range(3):
            f = displacement[c, plane]
            here.extend(corner_sums(f, pltpu.roll(f, NYL - 1, 0), last))
        return tuple(here)

    def plane_energy(x, before):
        after = nodes(x + 1)
        energy[x] = element_energy(before, after)
        return after

    before = nodes(0)
    for x in range(NXL - 1):
        before = plane_energy(x, before)
    energy[NXL - 1] = jnp.zeros((NYL, NZ), jnp.float32)
    trial = lax.broadcasted_iota(jnp.int32, (SLOTS, NZ), 0).astype(jnp.float32)
    factors[...] = jnp.exp(-0.5 * (-BRACKET + STEP * (trial + 1.0)))

    along_z = jnp.where(first | last, 1.0, 2.0)
    for v in (0, 1):
        index_y = start_y - 1 + 8 * v + lax.broadcasted_iota(jnp.int32, (8, NZ), 0)
        inside = (index_y >= 0) & (index_y < total_y)
        along_y = jnp.where((index_y == 0) | (index_y == total_y - 1), 1.0, 2.0)
        base = 1.5 + 0.5 * (along_y + along_z) + EDGE_WEIGHT * along_y * along_z
        slope = 0.5 + EDGE_WEIGHT * (along_y + along_z)
        for slot, along_x in ((0, 2.0), (1, 1.0)):
            inverse[slot, pl.ds(8 * v, 8), :] = jnp.where(
                inside, 1.0 / (base + along_x * slope), 0.0
            )
    for slot in (0, 1):
        side, rest = filter_terms(
            inverse[slot, pl.ds(0, 8), :],
            inverse[slot, pl.ds(1, 8), :],
            inverse[slot, pl.ds(2, 8), :],
            first,
            last,
        )
        weights[2 * slot] = side
        weights[2 * slot + 1] = rest

    here = density[...]
    kind = passive[...]
    fixed = jnp.where(kind == 1, 1.0, 0.0)
    lower[...] = jnp.where(kind == 0, jnp.maximum(here - MOVE_LIMIT, 0.0), fixed)
    upper[...] = jnp.where(kind == 0, jnp.minimum(here + MOVE_LIMIT, 1.0), fixed)

    def rolled_terms(f):
        return filter_terms(pltpu.roll(f, 1, 0), f, pltpu.roll(f, NYL - 1, 0), first, last)

    weight = inverse[0, pl.ds(1, 8), :]
    before, here = rolled_terms(density[0]), rolled_terms(density[1])
    for x in range(1, NXL - 1):
        after = rolled_terms(density[x + 1])
        own_spread[x] = spread_of(
            here[1] + before[0] + after[0], weight, passive[x].astype(jnp.float32), energy[x]
        )
        before, here = here, after
    scale = 1.0 / (weights[1] + 2.0 * weights[0])
    before, here = rolled_terms(own_spread[1]), rolled_terms(own_spread[2])
    values = []
    for x in range(2, NXL - 2):
        after = rolled_terms(own_spread[x + 1])
        sens = here[1] + before[0] + after[0]
        values.append(density[x] * jnp.sqrt(-sens * scale))
        before, here = here, after
    for p in range(PAIRS):
        x = 2 + 2 * p
        inner[0, p] = row_pack(values[2 * p], values[2 * p + 1], True)
        for i, (limit, outer) in enumerate(((lower, lower_outer), (upper, upper_outer))):
            inner[1 + i, p] = row_pack(limit[x], limit[x + 1], True)
            outer[p] = row_pack(limit[x], limit[x + 1], False)
    add_volumes(
        [(p, p) for p in range(PAIRS)],
        factors,
        inner.at[0],
        inner.at[1],
        inner.at[2],
        None,
        partial,
    )


def spread_of(filtered, weight, kind, energy):
    physical = filtered * weight
    physical = jnp.where(kind == 1.0, 1.0, jnp.where(kind == 2.0, 0.0, physical))
    return -DERIVATIVE * physical * physical * energy * weight


def row_pack(one, two, inner):
    row = lax.broadcasted_iota(jnp.int32, (NYL, NZ), 0)
    mid = (row >= 2) & (row < 6)
    turned = pltpu.roll(two, 4, 0)
    return jnp.where(mid, one, turned) if inner else jnp.where(mid, turned, one)


def around(ref, plane, first, last):
    return filter_terms(
        ref[plane, pl.ds(7, 8), :],
        ref[plane, pl.ds(8, 8), :],
        ref[plane, pl.ds(9, 8), :],
        first,
        last,
    )


def add_volumes(planes, factors, scaled, lower, upper, start, partial):
    def volume_group(g, carry):
        base = pl.multiple_of(8 * GROUP * g, 8 * GROUP)
        scales = [
            jnp.broadcast_to(factors[pl.ds(GROUP * g + k, 1), :], (8, NZ)) for k in range(GROUP)
        ]
        if start is None:
            totals = [jnp.zeros((8, NZ), jnp.float32) for _ in range(GROUP)]
        else:
            totals = [start[pl.ds(base + 8 * k, 8), :] for k in range(GROUP)]
        for place, x in planes:
            values, floor, ceiling = scaled[place], lower[x], upper[x]
            for k in range(GROUP):
                totals[k] += jnp.minimum(jnp.maximum(values * scales[k], floor), ceiling)
        for k in range(GROUP):
            partial[pl.ds(base + 8 * k, 8), :] = totals[k]
        return carry

    lax.fori_loop(0, SLOTS // GROUP, volume_group, 0)


def middle(
    factors,
    density,
    passive,
    own_energy,
    inverse,
    weights,
    y_high,
    y_low,
    sent_a,
    sent_b,
    lower_outer,
    upper_outer,
    start,
    spread,
    sensitivity,
    scaled,
    partial,
    dens,
    energy,
    outer,
):
    def rows(ref, kind):
        return ref[pl.ds(kind * NXL, NXL), :]

    odd = is_odd("gy")

    def sent_low(kind):
        return jnp.where(odd, rows(sent_b, kind), rows(sent_a, kind))

    def sent_high(kind):
        return jnp.where(odd, rows(sent_a, kind), rows(sent_b, kind))

    first, last = lane_ends(NXL)

    def row_nodes(ref, step, at):
        return [rows(ref, at + step * c) for c in range(3)]

    def row_energy(here, above):
        before, after = [], []
        for c in range(3):
            sums = corner_sums(here[c], above[c], last)
            before.extend(sums)
            after.extend(pltpu.roll(f, NXL - 1, 0) for f in sums)
        return element_energy(before, after)

    nodes_8 = row_nodes(y_high, 2, 2)
    energy_low = row_energy(row_nodes(y_low, 1, 2), [sent_low(2 + 2 * c) for c in range(3)])
    energy_7 = row_energy([sent_high(2 + c) for c in range(3)], nodes_8)
    energy_high = row_energy(nodes_8, row_nodes(y_high, 2, 3))

    dens[:, pl.ds(8, NYL), :] = density[...]
    dens[:, 7, :] = rows(y_low, 1)
    dens[:, 16, :] = rows(y_high, 0)
    energy[...] = own_energy[...]
    energy[:, 7, :] = energy_7

    for row, low, mid, high, kind, row_energies in (
        (0, rows(y_low, 0), rows(y_low, 1), sent_low(0), rows(y_low, 5), energy_low),
        (9, sent_high(1), rows(y_high, 0), rows(y_high, 1), rows(y_high, 8), energy_high),
    ):
        side, rest = filter_terms(low, mid, high, first, last)
        filtered = rest + pltpu.roll(side, 1, 0) + pltpu.roll(side, NXL - 1, 0)
        weight = jnp.broadcast_to(inverse[0, pl.ds(row, 1), :], (NXL, NZ))
        spread[:, row + 7, :] = spread_of(filtered, weight, kind, row_energies)

    first, last = lane_ends(NYL)
    weight = inverse[0, pl.ds(1, 8), :]

    def spread_plane(x, carry):
        side_before, side_here, rest_here = carry
        side_after, rest_after = around(dens, x + 1, first, last)
        spread[x, pl.ds(8, 8), :] = spread_of(
            rest_here + side_before + side_after,
            weight,
            passive[x].astype(jnp.float32),
            energy[x],
        )
        return side_here, side_after, rest_after

    side_0, _ = around(dens, 0, first, last)
    carry = (side_0,) + around(dens, 1, first, last)
    for x in range(1, NXL - 1):
        carry = spread_plane(x, carry)

    scale = 1.0 / (weights[1] + 2.0 * weights[0])

    def out_plane(x, carry):
        side_before, side_here, rest_here = carry
        side_after, rest_after = around(spread, x + 1, first, last)
        sens = rest_here + side_before + side_after
        sensitivity[x] = sens
        scaled[x] = density[x] * jnp.sqrt(-sens * scale)
        return side_here, side_after, rest_after

    side_1, _ = around(spread, 1, first, last)
    carry = (side_1,) + around(spread, 2, first, last)
    for x in range(2, NXL - 2):
        carry = out_plane(x, carry)

    for p in range(PAIRS):
        outer[p] = row_pack(scaled[2 + 2 * p], scaled[3 + 2 * p], False)
    add_volumes(
        [(p, p) for p in range(PAIRS)],
        factors,
        outer,
        lower_outer,
        upper_outer,
        start,
        partial,
    )


def edges(
    factors,
    density,
    displacement,
    passive,
    y_high,
    y_low,
    received_a,
    received_b,
    inverse,
    weights,
    spread,
    inner_sensitivity,
    lower,
    upper,
    start,
    sensitivity,
    scaled,
    sums_out,
    dens,
    disp,
    kind_of,
    rim,
    partial,
    x_high,
    x_low,
    *,
    copies,
):
    odd = is_odd("gx")
    x_high[...] = jnp.where(odd, received_a[...], received_b[...])
    x_low[...] = jnp.where(odd, received_b[...], received_a[...])
    first, last = lane_ends(NYL)
    at_end = (
        lax.axis_index("gx") == 0,
        lax.axis_index("gx") == lax.axis_size("gx") - 1,
    )
    for side, (own, far, slabs, low_rows, pick) in enumerate(
        ((0, x_low, 48, 66, 1), (NXL - 2, x_high, 72, 90, 0))
    ):
        for k in (0, 1):
            own_at, far_at = (2 + k, k) if side == 0 else (k, 2 + k)
            dens[side, own_at, pl.ds(2, NYL), :] = density[own + k]
            dens[side, far_at, pl.ds(2, NYL), :] = far[pl.ds(8 * k, 8), :]
            for row in (0, 1):
                dens[side, own_at, pl.ds(NYL + 2 + row, 1), :] = y_high[
                    pl.ds(row * NXL + own + k, 1), :
                ]
                dens[side, own_at, pl.ds(row, 1), :] = y_low[pl.ds(row * NXL + own + k, 1), :]
                dens[side, far_at, pl.ds(NYL + 2 + row, 1), :] = far[
                    pl.ds(slabs + 2 * row + k, 1), :
                ]
                dens[side, far_at, pl.ds(row, 1), :] = far[pl.ds(low_rows + 2 * row + k, 1), :]
        for c in range(3):
            mine = ((1, 0), (2, 1)) if side == 0 else ((0, NXL - 1),)
            theirs = ((0, 2 + c, 1),) if side == 0 else ((1, 2 + 2 * c, 0), (2, 3 + 2 * c, 1))
            for at, x in mine:
                disp[side, c, at, pl.ds(1, NYL), :] = displacement[c, x]
                disp[side, c, at, pl.ds(0, 1), :] = y_low[pl.ds((2 + c) * NXL + x, 1), :]
                for row in (0, 1):
                    disp[side, c, at, pl.ds(NYL + 1 + row, 1), :] = y_high[
                        pl.ds((2 + 2 * c + row) * NXL + x, 1), :
                    ]
            for at, slab, k in theirs:
                disp[side, c, at, pl.ds(1, NYL), :] = far[pl.ds(8 * slab, 8), :]
                disp[side, c, at, pl.ds(0, 1), :] = far[pl.ds(low_rows + 2 * (2 + c) + k, 1), :]
                for row in (0, 1):
                    disp[side, c, at, pl.ds(NYL + 1 + row, 1), :] = far[
                        pl.ds(slabs + 2 * (2 + 2 * c + row) + k, 1), :
                    ]
        own_at, far_at, x = (1, 0, 0) if side == 0 else (0, 1, NXL - 1)
        kind_of[side, own_at, pl.ds(1, NYL), :] = passive[x].astype(jnp.float32)
        kind_of[side, own_at, pl.ds(0, 1), :] = y_low[pl.ds(5 * NXL + x, 1), :]
        kind_of[side, own_at, pl.ds(NYL + 1, 1), :] = y_high[pl.ds(8 * NXL + x, 1), :]
        kind_of[side, far_at, pl.ds(1, NYL), :] = far[pl.ds(40 if side == 0 else 64, 8), :]
        kind_of[side, far_at, pl.ds(0, 1), :] = far[pl.ds(low_rows + 10 + pick, 1), :]
        kind_of[side, far_at, pl.ds(NYL + 1, 1), :] = far[pl.ds(slabs + 16 + pick, 1), :]

        for v in (0, 1):
            rows = pl.ds(8 * v, 8)
            terms = [
                filter_terms(
                    dens[side, p, rows, :],
                    dens[side, p, pl.ds(8 * v + 1, 8), :],
                    dens[side, p, pl.ds(8 * v + 2, 8), :],
                    first,
                    last,
                )
                for p in range(4)
            ]
            nodes = []
            for p in range(3):
                sums = []
                for c in range(3):
                    sums.extend(
                        corner_sums(
                            disp[side, c, p, rows, :],
                            disp[side, c, p, pl.ds(8 * v + 1, 8), :],
                            last,
                        )
                    )
                nodes.append(sums)
            inner = inverse[0, rows, :]
            by_place = (
                jnp.where(at_end[side], 0.0, inner),
                jnp.where(at_end[side], inverse[1, rows, :], inner),
            )
            for k in (0, 1):
                weight = by_place[k] if side == 0 else by_place[1 - k]
                rim[side, (k if side == 0 else 2 + k), pl.ds(7 + 8 * v, 8), :] = spread_of(
                    terms[k + 1][1] + terms[k][0] + terms[k + 2][0],
                    weight,
                    kind_of[side, k, rows, :],
                    element_energy(nodes[k], nodes[k + 1]),
                )
        for k in (0, 1):
            rim[side, (2 + k if side == 0 else k), :, :] = spread[1 + k if side == 0 else 13 + k]

    inner_planes = pl.ds(2, NXL - 4)
    sensitivity[inner_planes] = inner_sensitivity[inner_planes]
    side_inner, rest_inner, side_edge, rest_edge = (weights[i] for i in range(4))
    for side in (0, 1):
        outer_side = jnp.where(at_end[side], 0.0, side_inner)
        next_side = jnp.where(at_end[side], side_edge, side_inner)
        outer = jnp.where(at_end[side], rest_edge, rest_inner) + outer_side + side_inner
        inner = rest_inner + next_side + side_inner
        terms = [around(rim.at[side], p, first, last) for p in range(4)]
        for k in (0, 1):
            x = k if side == 0 else NXL - 2 + k
            sens = terms[k + 1][1] + terms[k][0] + terms[k + 2][0]
            weight = outer if k == side else inner
            sensitivity[x] = sens
            scaled[2 * side + k] = density[x] * jnp.sqrt(-sens / weight)

    add_volumes(
        [(0, 0), (1, 1), (2, NXL - 2), (3, NXL - 1)],
        factors,
        scaled,
        lower,
        upper,
        start,
        partial,
    )
    rows_of = [partial[pl.ds(s, SLOTS, stride=8), :] for s in range(8)]
    lines = ((rows_of[0] + rows_of[1]) + (rows_of[2] + rows_of[3])) + (
        (rows_of[4] + rows_of[5]) + (rows_of[6] + rows_of[7])
    )
    volumes = lax.dot_general(
        jnp.ones((8, NZ), jnp.float32),
        lines,
        (((1,), (1,)), ((), ())),
        precision=lax.Precision.HIGHEST,
        preferred_element_type=jnp.float32,
    )
    second = lax.broadcasted_iota(jnp.int32, (8, NZ), 0) > 0
    pair = jnp.where(second, volumes[:, NZ:], volumes[:, :NZ])[0:2]
    for copy in range(copies):
        sums_out[copy] = pair


def add_copies(received, out, *, copies):
    total = jnp.sum(received[...], axis=0)
    for copy in range(copies):
        out[copy] = total


def finish(
    received,
    scaled,
    scaled_edge,
    lower,
    upper,
    sensitivity,
    new_density_far,
    sensitivity_far,
    new_density,
    sems,
    *,
    target,
):
    copies = [
        pltpu.make_async_copy(sensitivity, sensitivity_far, sems.at[0]),
        pltpu.make_async_copy(new_density, new_density_far, sems.at[1]),
    ]
    copies[0].start()
    volumes = jnp.sum(received[...], axis=0)
    slot = lax.broadcasted_iota(jnp.int32, (2, NZ), 0) * NZ + lax.broadcasted_iota(
        jnp.int32, (2, NZ), 1
    )
    above = jnp.sum(jnp.where((volumes > target) & (slot < TRIALS), 1.0, 0.0))
    middle_end = -BRACKET + STEP * above + 0.5 * STEP
    factor = jnp.exp(jnp.full((8, NZ), -0.5, jnp.float32) * middle_end)[None]
    inner = pl.ds(2, NXL - 4)
    for ref, place, planes in (
        (scaled, inner, inner),
        (scaled_edge, pl.ds(0, 2), pl.ds(0, 2)),
        (scaled_edge, pl.ds(2, 2), pl.ds(NXL - 2, 2)),
    ):
        new_density[planes] = jnp.minimum(
            jnp.maximum(ref[place] * factor, lower[planes]), upper[planes]
        )
    copies[1].start()
    for copy in copies:
        copy.wait()


def f32(*shape):
    return jax.ShapeDtypeStruct(shape, jnp.float32)


def near(*shape, dtype=jnp.float32):
    return pltpu.VMEM(shape, dtype)


def far(array):
    return pltpu.with_memory_space_constraint(array, pltpu.HBM)


def held(array):
    return pltpu.with_memory_space_constraint(array, pltpu.VMEM)


def call(kernel, outputs, inputs, scratch=(), specs=None, out_specs=None, cost=0):
    return pl.pallas_call(
        kernel,
        out_shape=outputs,
        in_specs=specs or [VMEM] * len(inputs),
        out_specs=out_specs or jax.tree.map(lambda _: VMEM, outputs),
        scratch_shapes=list(scratch),
        cost_estimate=pl.CostEstimate(
            flops=cost * 4000, bytes_accessed=cost * 1000, transcendentals=0
        ),
        compiler_params=pltpu.CompilerParams(vmem_limit_bytes=16 << 20),
    )(*inputs)


def swapped(block, axis, start):
    pairs = [(i, i + 1) for i in range(start, lax.axis_size(axis) - 1, 2)]
    return lax.ppermute(block, axis, pairs + [(j, i) for i, j in pairs])


def reduction_groups(count_x, count_y):
    chips_x = count_y // SIDE
    across, along = {}, {}
    for gx in range(count_x):
        for gy in range(count_y):
            device = gx * count_y + gy
            x, y = gy // SIDE, gy % SIDE
            across.setdefault((gx // 2, min(x, chips_x - 1 - x)), []).append(device)
            along.setdefault((gx % 2, y, x // 2), []).append(device)
    return list(across.values()), list(along.values())


def per_device(density, displacement, passive):
    count_x, count_y = lax.axis_size("gx"), lax.axis_size("gy")
    assert density.shape == (NXL, NYL, NZ)
    block = (NXL, NYL, NZ)
    density, displacement, passive, sent_a, sent_b = call(
        pack_y,
        (
            near(*block),
            near(3, *block),
            near(*block, dtype=jnp.int32),
            near(9 * NXL, NZ),
            near(9 * NXL, NZ),
        ),
        (far(density), far(displacement), far(passive)),
        [pltpu.SemaphoreType.DMA((3,))],
        specs=[pl.BlockSpec(memory_space=pltpu.HBM)] * 3,
        cost=1000,
    )
    received_a = held(swapped(sent_a, "gy", 1))
    received_b = held(swapped(sent_b, "gy", 0))
    (
        own_energy,
        inverse,
        weights,
        factors,
        lower,
        upper,
        lower_outer,
        upper_outer,
        start,
    ) = call(
        interior,
        (near(*block), near(2, 16, NZ), near(4, NYL, NZ), near(SLOTS, NZ))
        + (near(*block),) * 2
        + (near(PAIRS, NYL, NZ),) * 2
        + (near(8 * SLOTS, NZ),),
        (density, displacement, passive),
        [
            pltpu.VMEM(block, jnp.float32),
            pltpu.VMEM((3, PAIRS, NYL, NZ), jnp.float32),
        ],
        cost=1000,
    )
    y_high, y_low, to_a, to_b = call(
        pack_x,
        (near(9 * NXL, NZ), near(6 * NXL, NZ), near(104, NZ), near(104, NZ)),
        (density, displacement, passive, received_a, received_b, weights),
        cost=500,
    )
    received_a = held(swapped(to_a, "gx", 1))
    received_b = held(swapped(to_b, "gx", 0))
    spread, sensitivity, scaled, partial = call(
        middle,
        (near(NXL, 24, NZ),) + (near(*block),) * 2 + (near(8 * SLOTS, NZ),),
        (
            factors,
            density,
            passive,
            own_energy,
            inverse,
            weights,
            y_high,
            y_low,
            sent_a,
            sent_b,
            lower_outer,
            upper_outer,
            start,
        ),
        [
            pltpu.VMEM((NXL, 24, NZ), jnp.float32),
            pltpu.VMEM(block, jnp.float32),
            pltpu.VMEM((PAIRS, NYL, NZ), jnp.float32),
        ],
        cost=5000,
    )
    across, along = reduction_groups(count_x, count_y)
    first_group, second_group = len(across[0]), len(along[0])
    sensitivity, scaled_edge, volumes = call(
        functools.partial(edges, copies=first_group),
        (near(*block), near(4, NYL, NZ), near(first_group, 2, NZ)),
        (
            factors,
            density,
            displacement,
            passive,
            y_high,
            y_low,
            received_a,
            received_b,
            inverse,
            weights,
            spread,
            sensitivity,
            lower,
            upper,
            partial,
        ),
        [
            pltpu.VMEM((2, 4, 24, NZ), jnp.float32),
            pltpu.VMEM((2, 3, 3, 24, NZ), jnp.float32),
            pltpu.VMEM((2, 2, 16, NZ), jnp.float32),
            pltpu.VMEM((2, 4, 24, NZ), jnp.float32),
            pltpu.VMEM((8 * SLOTS, NZ), jnp.float32),
            pltpu.VMEM((104, NZ), jnp.float32),
            pltpu.VMEM((104, NZ), jnp.float32),
        ],
        cost=3000,
    )

    volumes = lax.all_to_all(volumes, ("gx", "gy"), 0, 0, axis_index_groups=across)
    volumes = call(
        functools.partial(add_copies, copies=second_group),
        near(second_group, 2, NZ),
        (held(volumes),),
        cost=300,
    )
    volumes = lax.all_to_all(volumes, ("gx", "gy"), 0, 0, axis_index_groups=along)
    target = VOLUME_SHARE * (count_x * NXL) * (count_y * NYL) * NZ
    new_density, sensitivity = call(
        functools.partial(finish, target=target),
        (f32(*block), f32(*block)),
        (held(volumes), scaled, scaled_edge, lower, upper, sensitivity),
        [pltpu.VMEM(block, jnp.float32), pltpu.SemaphoreType.DMA((2,))],
        out_specs=(pl.BlockSpec(memory_space=pltpu.HBM),) * 2,
        cost=500,
    )
    return new_density, sensitivity


def solution(mesh):
    return jax.shard_map(
        per_device,
        mesh=mesh,
        in_specs=(P("gx", "gy", None), P(None, "gx", "gy", None), P("gx", "gy", None)),
        out_specs=(P("gx", "gy", None), P("gx", "gy", None)),
        check_vma=False,
    )
```

```python
import functools
import math

import jax
import jax.numpy as jnp
from jax import lax
from jax.experimental import pallas as pl
from jax.experimental.pallas import tpu as pltpu
from jax.sharding import PartitionSpec as P

BISECT = 8
BRACKET = 8.0
MOVE_LIMIT = 0.2
VOLUME_SHARE = 0.35
DERIVATIVE = 3.0 * (1.0 - 1e-09)
EDGE_WEIGHT = 1.5 - math.sqrt(2.0)
POISSON = 0.3
LAME = POISSON / ((1.0 + POISSON) * (1.0 - 2.0 * POISSON))
SHEAR = 0.5 / (1.0 + POISSON)

NXL = 16
NYL = 8
NZ = 128
TRIALS = 2 ** BISECT - 1
SLOTS = TRIALS + 1
STEP = 2.0 * BRACKET / 2 ** BISECT
GROUP = 16
PAIRS = NXL // 2 - 2
SIDE = 4

VMEM = pl.BlockSpec(memory_space=pltpu.VMEM)


def is_odd(axis):
    return lax.rem(lax.axis_index(axis), 2) == 1


def pack_y(
    density_far, displacement_far, passive_far, density, displacement, passive, send_a, send_b, sems
):
    copies = [
        pltpu.make_async_copy(far, local, sems.at[i])
        for i, (far, local) in enumerate(
            (
                (density_far, density),
                (displacement_far, displacement),
                (passive_far, passive),
            )
        )
    ]
    for copy in copies:
        copy.start()
    for copy in copies:
        copy.wait()

    def fill(to_low, to_high):
        for row in (0, 1):
            to_low[pl.ds(row * NXL, NXL), :] = density[:, row, :]
            to_high[pl.ds(row * NXL, NXL), :] = density[:, NYL - 2 + row, :]
        for c in range(3):
            for row in (0, 1):
                to_low[pl.ds((2 + 2 * c + row) * NXL, NXL), :] = displacement[c, :, row, :]
            to_high[pl.ds((2 + c) * NXL, NXL), :] = displacement[c, :, NYL - 1, :]
        to_low[pl.ds(8 * NXL, NXL), :] = passive[:, 0, :].astype(jnp.float32)
        to_high[pl.ds(5 * NXL, NXL), :] = passive[:, NYL - 1, :].astype(jnp.float32)
        to_high[pl.ds(6 * NXL, 3 * NXL), :] = jnp.zeros((3 * NXL, NZ), jnp.float32)

    odd = is_odd("gy")
    pl.when(odd)(lambda: fill(send_b, send_a))
    pl.when(jnp.logical_not(odd))(lambda: fill(send_a, send_b))


def pack_x(
    density, displacement, passive, received_a, received_b, after, y_high, y_low, send_a, send_b
):
    del after
    odd = is_odd("gy")
    y_high[...] = jnp.where(odd, received_a[...], received_b[...])
    low = pl.ds(0, 6 * NXL)
    y_low[...] = jnp.where(odd, received_b[low, :], received_a[low, :])

    def fill(to_low, to_high):
        for k in (0, 1):
            to_low[pl.ds(8 * k, 8), :] = density[k]
            to_high[pl.ds(8 * k, 8), :] = density[NXL - 2 + k]
        for c in range(3):
            for k in (0, 1):
                to_low[pl.ds(8 * (2 + 2 * c + k), 8), :] = displacement[c, k]
            to_high[pl.ds(8 * (2 + c), 8), :] = displacement[c, NXL - 1]
        to_low[pl.ds(64, 8), :] = passive[0].astype(jnp.float32)
        to_high[pl.ds(40, 8), :] = passive[NXL - 1].astype(jnp.float32)
        for base, first, out in ((72, 0, to_low), (48, NXL - 2, to_high)):
            for kind in range(9):
                out[pl.ds(base + 2 * kind, 2), :] = y_high[pl.ds(NXL * kind + first, 2), :]
            for kind in range(6):
                out[pl.ds(base + 18 + 2 * kind, 2), :] = y_low[pl.ds(NXL * kind + first, 2), :]
            out[pl.ds(base + 30, 2), :] = jnp.zeros((2, NZ), jnp.float32)
        to_high[pl.ds(80, 24), :] = jnp.zeros((24, NZ), jnp.float32)

    odd_x = is_odd("gx")
    pl.when(odd_x)(lambda: fill(send_b, send_a))
    pl.when(jnp.logical_not(odd_x))(lambda: fill(send_a, send_b))


def lane_ends(height):
    lane = lax.broadcasted_iota(jnp.int32, (height, NZ), 1)
    return lane == 0, lane == NZ - 1


def z_sum(f, first, last):
    return jnp.where(first, 0.0, pltpu.roll(f, 1, 1)) + jnp.where(
        last, 0.0, pltpu.roll(f, NZ - 1, 1)
    )


def filter_terms(low, mid, high, first, last):
    across = z_sum(mid, first, last)
    along = low + high
    both = across + along
    side = 0.5 * mid + EDGE_WEIGHT * both
    rest = 1.5 * mid + 0.5 * both + EDGE_WEIGHT * z_sum(along, first, last)
    return side, rest


def corner_sums(here, above, last):
    total = here + above
    slope = above - here
    total_next = jnp.where(last, 0.0, pltpu.roll(total, NZ - 1, 1))
    slope_next = jnp.where(last, 0.0, pltpu.roll(slope, NZ - 1, 1))
    return (total + total_next, total_next - total, slope + slope_next, slope_next - slope)


def element_energy(before, after):
    modes = []
    for c in range(3):
        for k in range(4):
            low, high = before[4 * c + k], after[4 * c + k]
            modes.append((low + high, high - low))
    u, v, w = (
        {(a, k // 2, k % 2): modes[4 * c + k][a] for a in (0, 1) for k in range(4)}
        for c in range(3)
    )

    def sq(x):
        return x * x

    trace = sq(u[1, 0, 0] + v[0, 1, 0] + w[0, 0, 1]) + (1.0 / 3.0) * (
        sq(v[1, 1, 0] + w[1, 0, 1]) + sq(u[1, 1, 0] + w[0, 1, 1]) + sq(u[1, 0, 1] + v[0, 1, 1])
    )
    normal = sq(u[1, 0, 0]) + sq(v[0, 1, 0]) + sq(w[0, 0, 1])
    linear = (
        sq(v[1, 1, 0])
        + sq(w[1, 0, 1])
        + sq(u[1, 1, 0])
        + sq(w[0, 1, 1])
        + sq(u[1, 0, 1])
        + sq(v[0, 1, 1])
    )
    bilinear = sq(u[1, 1, 1]) + sq(v[1, 1, 1]) + sq(w[1, 1, 1])
    shear = (
        sq(u[0, 1, 0] + v[1, 0, 0]) + sq(u[0, 0, 1] + w[1, 0, 0]) + sq(v[0, 0, 1] + w[0, 1, 0])
    )
    twist = (
        sq(u[0, 1, 1] + v[1, 0, 1]) + sq(u[0, 1, 1] + w[1, 1, 0]) + sq(v[1, 0, 1] + w[1, 1, 0])
    )
    return (
        (LAME / 16.0) * trace
        + (SHEAR / 8.0) * normal
        + (SHEAR / 16.0) * (linear + shear)
        + ((LAME + 4.0 * SHEAR) / 144.0) * bilinear
        + (SHEAR / 48.0) * twist
    )


def interior(
    density,
    displacement,
    passive,
    energy,
    inverse,
    weights,
    factors,
    lower,
    upper,
    lower_outer,
    upper_outer,
    partial,
    own_spread,
    inner,
):
    start_y = lax.axis_index("gy") * NYL
    total_y = lax.axis_size("gy") * NYL
    first, last = lane_ends(NYL)

    def nodes(plane):
        here = []
        for c in range(3):
            f = displacement[c, plane]
            here.extend(corner_sums(f, pltpu.roll(f, NYL - 1, 0), last))
        return tuple(here)

    def plane_energy(x, before):
        after = nodes(x + 1)
        energy[x] = element_energy(before, after)
        return after

    before = nodes(0)
    for x in range(NXL - 1):
        before = plane_energy(x, before)
    energy[NXL - 1] = jnp.zeros((NYL, NZ), jnp.float32)
    trial = lax.broadcasted_iota(jnp.int32, (SLOTS, NZ), 0).astype(jnp.float32)
    factors[...] = jnp.exp(-0.5 * (-BRACKET + STEP * (trial + 1.0)))

    along_z = jnp.where(first | last, 1.0, 2.0)
    for v in (0, 1):
        index_y = start_y - 1 + 8 * v + lax.broadcasted_iota(jnp.int32, (8, NZ), 0)
        inside = (index_y >= 0) & (index_y < total_y)
        along_y = jnp.where((index_y == 0) | (index_y == total_y - 1), 1.0, 2.0)
        base = 1.5 + 0.5 * (along_y + along_z) + EDGE_WEIGHT * along_y * along_z
        slope = 0.5 + EDGE_WEIGHT * (along_y + along_z)
        for slot, along_x in ((0, 2.0), (1, 1.0)):
            inverse[slot, pl.ds(8 * v, 8), :] = jnp.where(
                inside, 1.0 / (base + along_x * slope), 0.0
            )
    for slot in (0, 1):
        side, rest = filter_terms(
            inverse[slot, pl.ds(0, 8), :],
            inverse[slot, pl.ds(1, 8), :],
            inverse[slot, pl.ds(2, 8), :],
            first,
            last,
        )
        weights[2 * slot] = side
        weights[2 * slot + 1] = rest

    here = density[...]
    kind = passive[...]
    fixed = jnp.where(kind == 1, 1.0, 0.0)
    lower[...] = jnp.where(kind == 0, jnp.maximum(here - MOVE_LIMIT, 0.0), fixed)
    upper[...] = jnp.where(kind == 0, jnp.minimum(here + MOVE_LIMIT, 1.0), fixed)

    def rolled_terms(f):
        return filter_terms(pltpu.roll(f, 1, 0), f, pltpu.roll(f, NYL - 1, 0), first, last)

    weight = inverse[0, pl.ds(1, 8), :]
    before, here = rolled_terms(density[0]), rolled_terms(density[1])
    for x in range(1, NXL - 1):
        after = rolled_terms(density[x + 1])
        own_spread[x] = spread_of(
            here[1] + before[0] + after[0], weight, passive[x].astype(jnp.float32), energy[x]
        )
        before, here = here, after
    scale = 1.0 / (weights[1] + 2.0 * weights[0])
    before, here = rolled_terms(own_spread[1]), rolled_terms(own_spread[2])
    values = []
    for x in range(2, NXL - 2):
        after = rolled_terms(own_spread[x + 1])
        sens = here[1] + before[0] + after[0]
        values.append(density[x] * jnp.sqrt(-sens * scale))
        before, here = here, after
    for p in range(PAIRS):
        x = 2 + 2 * p
        inner[0, p] = row_pack(values[2 * p], values[2 * p + 1], True)
        for i, (limit, outer) in enumerate(((lower, lower_outer), (upper, upper_outer))):
            inner[1 + i, p] = row_pack(limit[x], limit[x + 1], True)
            outer[p] = row_pack(limit[x], limit[x + 1], False)
    add_volumes(
        [(p, p) for p in range(PAIRS)],
        factors,
        inner.at[0],
        inner.at[1],
        inner.at[2],
        None,
        partial,
    )


def spread_of(filtered, weight, kind, energy):
    physical = filtered * weight
    physical = jnp.where(kind == 1.0, 1.0, jnp.where(kind == 2.0, 0.0, physical))
    return -DERIVATIVE * physical * physical * energy * weight


def row_pack(one, two, inner):
    row = lax.broadcasted_iota(jnp.int32, (NYL, NZ), 0)
    mid = (row >= 2) & (row < 6)
    turned = pltpu.roll(two, 4, 0)
    return jnp.where(mid, one, turned) if inner else jnp.where(mid, turned, one)


def around(ref, plane, first, last):
    return filter_terms(
        ref[plane, pl.ds(7, 8), :],
        ref[plane, pl.ds(8, 8), :],
        ref[plane, pl.ds(9, 8), :],
        first,
        last,
    )


def add_volumes(planes, factors, scaled, lower, upper, start, partial):
    def volume_group(g, carry):
        base = pl.multiple_of(8 * GROUP * g, 8 * GROUP)
        scales = [
            jnp.broadcast_to(factors[pl.ds(GROUP * g + k, 1), :], (8, NZ)) for k in range(GROUP)
        ]
        if start is None:
            totals = [jnp.zeros((8, NZ), jnp.float32) for _ in range(GROUP)]
        else:
            totals = [start[pl.ds(base + 8 * k, 8), :] for k in range(GROUP)]
        for place, x in planes:
            values, floor, ceiling = scaled[place], lower[x], upper[x]
            for k in range(GROUP):
                totals[k] += jnp.minimum(jnp.maximum(values * scales[k], floor), ceiling)
        for k in range(GROUP):
            partial[pl.ds(base + 8 * k, 8), :] = totals[k]
        return carry

    lax.fori_loop(0, SLOTS // GROUP, volume_group, 0, unroll=4)


def middle(
    factors,
    density,
    passive,
    own_energy,
    inverse,
    weights,
    y_high,
    y_low,
    sent_a,
    sent_b,
    lower_outer,
    upper_outer,
    start,
    spread,
    sensitivity,
    scaled,
    partial,
    dens,
    energy,
    outer,
):
    def rows(ref, kind):
        return ref[pl.ds(kind * NXL, NXL), :]

    odd = is_odd("gy")

    def sent_low(kind):
        return jnp.where(odd, rows(sent_b, kind), rows(sent_a, kind))

    def sent_high(kind):
        return jnp.where(odd, rows(sent_a, kind), rows(sent_b, kind))

    first, last = lane_ends(NXL)

    def row_nodes(ref, step, at):
        return [rows(ref, at + step * c) for c in range(3)]

    def row_energy(here, above):
        before, after = [], []
        for c in range(3):
            sums = corner_sums(here[c], above[c], last)
            before.extend(sums)
            after.extend(pltpu.roll(f, NXL - 1, 0) for f in sums)
        return element_energy(before, after)

    nodes_8 = row_nodes(y_high, 2, 2)
    energy_low = row_energy(row_nodes(y_low, 1, 2), [sent_low(2 + 2 * c) for c in range(3)])
    energy_7 = row_energy([sent_high(2 + c) for c in range(3)], nodes_8)
    energy_high = row_energy(nodes_8, row_nodes(y_high, 2, 3))

    dens[:, pl.ds(8, NYL), :] = density[...]
    dens[:, 7, :] = rows(y_low, 1)
    dens[:, 16, :] = rows(y_high, 0)
    energy[...] = own_energy[...]
    energy[:, 7, :] = energy_7

    for row, low, mid, high, kind, row_energies in (
        (0, rows(y_low, 0), rows(y_low, 1), sent_low(0), rows(y_low, 5), energy_low),
        (9, sent_high(1), rows(y_high, 0), rows(y_high, 1), rows(y_high, 8), energy_high),
    ):
        side, rest = filter_terms(low, mid, high, first, last)
        filtered = rest + pltpu.roll(side, 1, 0) + pltpu.roll(side, NXL - 1, 0)
        weight = jnp.broadcast_to(inverse[0, pl.ds(row, 1), :], (NXL, NZ))
        spread[:, row + 7, :] = spread_of(filtered, weight, kind, row_energies)

    first, last = lane_ends(NYL)
    weight = inverse[0, pl.ds(1, 8), :]

    def spread_plane(x, carry):
        side_before, side_here, rest_here = carry
        side_after, rest_after = around(dens, x + 1, first, last)
        spread[x, pl.ds(8, 8), :] = spread_of(
            rest_here + side_before + side_after,
            weight,
            passive[x].astype(jnp.float32),
            energy[x],
        )
        return side_here, side_after, rest_after

    side_0, _ = around(dens, 0, first, last)
    carry = (side_0,) + around(dens, 1, first, last)
    for x in range(1, NXL - 1):
        carry = spread_plane(x, carry)

    scale = 1.0 / (weights[1] + 2.0 * weights[0])

    def out_plane(x, carry):
        side_before, side_here, rest_here = carry
        side_after, rest_after = around(spread, x + 1, first, last)
        sens = rest_here + side_before + side_after
        sensitivity[x] = sens
        scaled[x] = density[x] * jnp.sqrt(-sens * scale)
        return side_here, side_after, rest_after

    side_1, _ = around(spread, 1, first, last)
    carry = (side_1,) + around(spread, 2, first, last)
    for x in range(2, NXL - 2):
        carry = out_plane(x, carry)

    for p in range(PAIRS):
        outer[p] = row_pack(scaled[2 + 2 * p], scaled[3 + 2 * p], False)
    add_volumes(
        [(p, p) for p in range(PAIRS)],
        factors,
        outer,
        lower_outer,
        upper_outer,
        start,
        partial,
    )


def edges(
    factors,
    density,
    displacement,
    passive,
    y_high,
    y_low,
    received_a,
    received_b,
    inverse,
    weights,
    spread,
    inner_sensitivity,
    lower,
    upper,
    start,
    sensitivity,
    scaled,
    sums_out,
    dens,
    disp,
    kind_of,
    rim,
    partial,
    x_high,
    x_low,
    *,
    copies,
):
    odd = is_odd("gx")
    x_high[...] = jnp.where(odd, received_a[...], received_b[...])
    x_low[...] = jnp.where(odd, received_b[...], received_a[...])
    first, last = lane_ends(NYL)
    at_end = (
        lax.axis_index("gx") == 0,
        lax.axis_index("gx") == lax.axis_size("gx") - 1,
    )
    for side, (own, far, slabs, low_rows, pick) in enumerate(
        ((0, x_low, 48, 66, 1), (NXL - 2, x_high, 72, 90, 0))
    ):
        for k in (0, 1):
            own_at, far_at = (2 + k, k) if side == 0 else (k, 2 + k)
            dens[side, own_at, pl.ds(2, NYL), :] = density[own + k]
            dens[side, far_at, pl.ds(2, NYL), :] = far[pl.ds(8 * k, 8), :]
            for row in (0, 1):
                dens[side, own_at, pl.ds(NYL + 2 + row, 1), :] = y_high[
                    pl.ds(row * NXL + own + k, 1), :
                ]
                dens[side, own_at, pl.ds(row, 1), :] = y_low[pl.ds(row * NXL + own + k, 1), :]
                dens[side, far_at, pl.ds(NYL + 2 + row, 1), :] = far[
                    pl.ds(slabs + 2 * row + k, 1), :
                ]
                dens[side, far_at, pl.ds(row, 1), :] = far[pl.ds(low_rows + 2 * row + k, 1), :]
        for c in range(3):
            mine = ((1, 0), (2, 1)) if side == 0 else ((0, NXL - 1),)
            theirs = ((0, 2 + c, 1),) if side == 0 else ((1, 2 + 2 * c, 0), (2, 3 + 2 * c, 1))
            for at, x in mine:
                disp[side, c, at, pl.ds(1, NYL), :] = displacement[c, x]
                disp[side, c, at, pl.ds(0, 1), :] = y_low[pl.ds((2 + c) * NXL + x, 1), :]
                for row in (0, 1):
                    disp[side, c, at, pl.ds(NYL + 1 + row, 1), :] = y_high[
                        pl.ds((2 + 2 * c + row) * NXL + x, 1), :
                    ]
            for at, slab, k in theirs:
                disp[side, c, at, pl.ds(1, NYL), :] = far[pl.ds(8 * slab, 8), :]
                disp[side, c, at, pl.ds(0, 1), :] = far[pl.ds(low_rows + 2 * (2 + c) + k, 1), :]
                for row in (0, 1):
                    disp[side, c, at, pl.ds(NYL + 1 + row, 1), :] = far[
                        pl.ds(slabs + 2 * (2 + 2 * c + row) + k, 1), :
                    ]
        own_at, far_at, x = (1, 0, 0) if side == 0 else (0, 1, NXL - 1)
        kind_of[side, own_at, pl.ds(1, NYL), :] = passive[x].astype(jnp.float32)
        kind_of[side, own_at, pl.ds(0, 1), :] = y_low[pl.ds(5 * NXL + x, 1), :]
        kind_of[side, own_at, pl.ds(NYL + 1, 1), :] = y_high[pl.ds(8 * NXL + x, 1), :]
        kind_of[side, far_at, pl.ds(1, NYL), :] = far[pl.ds(40 if side == 0 else 64, 8), :]
        kind_of[side, far_at, pl.ds(0, 1), :] = far[pl.ds(low_rows + 10 + pick, 1), :]
        kind_of[side, far_at, pl.ds(NYL + 1, 1), :] = far[pl.ds(slabs + 16 + pick, 1), :]

        for v in (0, 1):
            rows = pl.ds(8 * v, 8)
            terms = [
                filter_terms(
                    dens[side, p, rows, :],
                    dens[side, p, pl.ds(8 * v + 1, 8), :],
                    dens[side, p, pl.ds(8 * v + 2, 8), :],
                    first,
                    last,
                )
                for p in range(4)
            ]
            nodes = []
            for p in range(3):
                sums = []
                for c in range(3):
                    sums.extend(
                        corner_sums(
                            disp[side, c, p, rows, :],
                            disp[side, c, p, pl.ds(8 * v + 1, 8), :],
                            last,
                        )
                    )
                nodes.append(sums)
            inner = inverse[0, rows, :]
            by_place = (
                jnp.where(at_end[side], 0.0, inner),
                jnp.where(at_end[side], inverse[1, rows, :], inner),
            )
            for k in (0, 1):
                weight = by_place[k] if side == 0 else by_place[1 - k]
                rim[side, (k if side == 0 else 2 + k), pl.ds(7 + 8 * v, 8), :] = spread_of(
                    terms[k + 1][1] + terms[k][0] + terms[k + 2][0],
                    weight,
                    kind_of[side, k, rows, :],
                    element_energy(nodes[k], nodes[k + 1]),
                )
        for k in (0, 1):
            rim[side, (2 + k if side == 0 else k), :, :] = spread[1 + k if side == 0 else 13 + k]

    inner_planes = pl.ds(2, NXL - 4)
    sensitivity[inner_planes] = inner_sensitivity[inner_planes]
    side_inner, rest_inner, side_edge, rest_edge = (weights[i] for i in range(4))
    for side in (0, 1):
        outer_side = jnp.where(at_end[side], 0.0, side_inner)
        next_side = jnp.where(at_end[side], side_edge, side_inner)
        outer = jnp.where(at_end[side], rest_edge, rest_inner) + outer_side + side_inner
        inner = rest_inner + next_side + side_inner
        terms = [around(rim.at[side], p, first, last) for p in range(4)]
        for k in (0, 1):
            x = k if side == 0 else NXL - 2 + k
            sens = terms[k + 1][1] + terms[k][0] + terms[k + 2][0]
            weight = outer if k == side else inner
            sensitivity[x] = sens
            scaled[2 * side + k] = density[x] * jnp.sqrt(-sens / weight)

    add_volumes(
        [(0, 0), (1, 1), (2, NXL - 2), (3, NXL - 1)],
        factors,
        scaled,
        lower,
        upper,
        start,
        partial,
    )
    rows_of = [partial[pl.ds(s, SLOTS, stride=8), :] for s in range(8)]
    lines = ((rows_of[0] + rows_of[1]) + (rows_of[2] + rows_of[3])) + (
        (rows_of[4] + rows_of[5]) + (rows_of[6] + rows_of[7])
    )
    volumes = lax.dot_general(
        jnp.ones((8, NZ), jnp.float32),
        lines,
        (((1,), (1,)), ((), ())),
        precision=lax.Precision.HIGHEST,
        preferred_element_type=jnp.float32,
    )
    second = lax.broadcasted_iota(jnp.int32, (8, NZ), 0) > 0
    pair = jnp.where(second, volumes[:, NZ:], volumes[:, :NZ])[0:2]
    for copy in range(copies):
        sums_out[copy] = pair


def add_copies(received, out, *, copies):
    total = jnp.sum(received[...], axis=0)
    for copy in range(copies):
        out[copy] = total


def finish(
    received,
    scaled,
    scaled_edge,
    lower,
    upper,
    sensitivity,
    new_density_far,
    sensitivity_far,
    new_density,
    sems,
    *,
    target,
):
    copies = [
        pltpu.make_async_copy(sensitivity, sensitivity_far, sems.at[0]),
        pltpu.make_async_copy(new_density, new_density_far, sems.at[1]),
    ]
    copies[0].start()
    volumes = jnp.sum(received[...], axis=0)
    slot = lax.broadcasted_iota(jnp.int32, (2, NZ), 0) * NZ + lax.broadcasted_iota(
        jnp.int32, (2, NZ), 1
    )
    above = jnp.sum(jnp.where((volumes > target) & (slot < TRIALS), 1.0, 0.0))
    middle_end = -BRACKET + STEP * above + 0.5 * STEP
    factor = jnp.exp(jnp.full((8, NZ), -0.5, jnp.float32) * middle_end)[None]
    inner = pl.ds(2, NXL - 4)
    for ref, place, planes in (
        (scaled, inner, inner),
        (scaled_edge, pl.ds(0, 2), pl.ds(0, 2)),
        (scaled_edge, pl.ds(2, 2), pl.ds(NXL - 2, 2)),
    ):
        new_density[planes] = jnp.minimum(
            jnp.maximum(ref[place] * factor, lower[planes]), upper[planes]
        )
    copies[1].start()
    for copy in copies:
        copy.wait()


def f32(*shape):
    return jax.ShapeDtypeStruct(shape, jnp.float32)


def near(*shape, dtype=jnp.float32):
    return pltpu.VMEM(shape, dtype)


def far(array):
    return pltpu.with_memory_space_constraint(array, pltpu.HBM)


def held(array):
    return pltpu.with_memory_space_constraint(array, pltpu.VMEM)


def call(kernel, outputs, inputs, scratch=(), specs=None, out_specs=None, cost=0):
    return pl.pallas_call(
        kernel,
        out_shape=outputs,
        in_specs=specs or [VMEM] * len(inputs),
        out_specs=out_specs or jax.tree.map(lambda _: VMEM, outputs),
        scratch_shapes=list(scratch),
        cost_estimate=pl.CostEstimate(
            flops=cost * 4000, bytes_accessed=cost * 1000, transcendentals=0
        ),
        compiler_params=pltpu.CompilerParams(vmem_limit_bytes=16 << 20),
    )(*inputs)


def swapped(block, axis, start):
    pairs = [(i, i + 1) for i in range(start, lax.axis_size(axis) - 1, 2)]
    return lax.ppermute(block, axis, pairs + [(j, i) for i, j in pairs])


def reduction_groups(count_x, count_y):
    chips_x = count_y // SIDE
    across, along = {}, {}
    for gx in range(count_x):
        for gy in range(count_y):
            device = gx * count_y + gy
            x, y = gy // SIDE, gy % SIDE
            across.setdefault((gx // 2, min(x, chips_x - 1 - x)), []).append(device)
            along.setdefault((gx % 2, y, x // 2), []).append(device)
    return list(across.values()), list(along.values())


def per_device(density, displacement, passive):
    count_x, count_y = lax.axis_size("gx"), lax.axis_size("gy")
    assert density.shape == (NXL, NYL, NZ)
    block = (NXL, NYL, NZ)
    density, displacement, passive, sent_a, sent_b = call(
        pack_y,
        (
            near(*block),
            near(3, *block),
            near(*block, dtype=jnp.int32),
            near(9 * NXL, NZ),
            near(9 * NXL, NZ),
        ),
        (far(density), far(displacement), far(passive)),
        [pltpu.SemaphoreType.DMA((3,))],
        specs=[pl.BlockSpec(memory_space=pltpu.HBM)] * 3,
        cost=1000,
    )
    received_a = held(swapped(sent_a, "gy", 1))
    received_b = held(swapped(sent_b, "gy", 0))
    (
        own_energy,
        inverse,
        weights,
        factors,
        lower,
        upper,
        lower_outer,
        upper_outer,
        start,
    ) = call(
        interior,
        (near(*block), near(2, 16, NZ), near(4, NYL, NZ), near(SLOTS, NZ))
        + (near(*block),) * 2
        + (near(PAIRS, NYL, NZ),) * 2
        + (near(8 * SLOTS, NZ),),
        (density, displacement, passive),
        [
            pltpu.VMEM(block, jnp.float32),
            pltpu.VMEM((3, PAIRS, NYL, NZ), jnp.float32),
        ],
        cost=1000,
    )
    y_high, y_low, to_a, to_b = call(
        pack_x,
        (near(9 * NXL, NZ), near(6 * NXL, NZ), near(104, NZ), near(104, NZ)),
        (density, displacement, passive, received_a, received_b, weights),
        cost=500,
    )
    received_a = held(swapped(to_a, "gx", 1))
    received_b = held(swapped(to_b, "gx", 0))
    spread, sensitivity, scaled, partial = call(
        middle,
        (near(NXL, 24, NZ),) + (near(*block),) * 2 + (near(8 * SLOTS, NZ),),
        (
            factors,
            density,
            passive,
            own_energy,
            inverse,
            weights,
            y_high,
            y_low,
            sent_a,
            sent_b,
            lower_outer,
            upper_outer,
            start,
        ),
        [
            pltpu.VMEM((NXL, 24, NZ), jnp.float32),
            pltpu.VMEM(block, jnp.float32),
            pltpu.VMEM((PAIRS, NYL, NZ), jnp.float32),
        ],
        cost=5000,
    )
    across, along = reduction_groups(count_x, count_y)
    first_group, second_group = len(across[0]), len(along[0])
    sensitivity, scaled_edge, volumes = call(
        functools.partial(edges, copies=first_group),
        (near(*block), near(4, NYL, NZ), near(first_group, 2, NZ)),
        (
            factors,
            density,
            displacement,
            passive,
            y_high,
            y_low,
            received_a,
            received_b,
            inverse,
            weights,
            spread,
            sensitivity,
            lower,
            upper,
            partial,
        ),
        [
            pltpu.VMEM((2, 4, 24, NZ), jnp.float32),
            pltpu.VMEM((2, 3, 3, 24, NZ), jnp.float32),
            pltpu.VMEM((2, 2, 16, NZ), jnp.float32),
            pltpu.VMEM((2, 4, 24, NZ), jnp.float32),
            pltpu.VMEM((8 * SLOTS, NZ), jnp.float32),
            pltpu.VMEM((104, NZ), jnp.float32),
            pltpu.VMEM((104, NZ), jnp.float32),
        ],
        cost=3000,
    )

    volumes = lax.all_to_all(volumes, ("gx", "gy"), 0, 0, axis_index_groups=across)
    volumes = call(
        functools.partial(add_copies, copies=second_group),
        near(second_group, 2, NZ),
        (held(volumes),),
        cost=300,
    )
    volumes = lax.all_to_all(volumes, ("gx", "gy"), 0, 0, axis_index_groups=along)
    target = VOLUME_SHARE * (count_x * NXL) * (count_y * NYL) * NZ
    new_density, sensitivity = call(
        functools.partial(finish, target=target),
        (f32(*block), f32(*block)),
        (held(volumes), scaled, scaled_edge, lower, upper, sensitivity),
        [pltpu.VMEM(block, jnp.float32), pltpu.SemaphoreType.DMA((2,))],
        out_specs=(pl.BlockSpec(memory_space=pltpu.HBM),) * 2,
        cost=500,
    )
    return new_density, sensitivity


def solution(mesh):
    return jax.shard_map(
        per_device,
        mesh=mesh,
        in_specs=(P("gx", "gy", None), P(None, "gx", "gy", None), P("gx", "gy", None)),
        out_specs=(P("gx", "gy", None), P("gx", "gy", None)),
        check_vma=False,
    )
```
